256 devices in a mesh: il: 4 (over x), xl: 16 (over z_lo, y, core), ta: 4 (over z_hi).
Axes of the slice: x: 4, y: 4, z: 8 (z_hi: 4, z_lo: 2; z = z_hi * 2 + z_lo), core: 2. Of those that a mesh axis runs over, the one named last changes fastest.
Arguments:
- traces: float32 [128, 512, 512], P('il', 'xl', 'ta'), may hold values from -6 to 6
- live: int32 [128, 512], P('il', 'xl'), may hold values 0 or 1
- counts: int32 [4, 16, 8], P('il', None, 'ta'), may hold values from 2 to 4, as said below
- levels: int32 [4], replicated, may hold values from 100 to 1500, as said below
Outputs:
- reconstructed: float32 [128, 512, 512], P('il', 'xl', 'ta')
The draws below stay inside these ranges and needn't reach their ends.
Inputs may be any that keep to these rules, and one draw needn't show every extreme that they name: counts[i, x, 2 t + w] is the iteration count of window w of the block of tile (i, x, t); a value of 4 occurs in every draw. `levels`: non-increasing over the iterations.
All inputs are finite; a program needn't handle non-finite values. No bound on the sum of `live` on one device may be relied on, other than what follows from the above.
Results may differ from the reference program's by a relative error of at most 0.0003.
Values may be sent and summed in bfloat16 or wider, within the bound.
No kernel may reach another device: no remote copies, remote signals or barrier semaphores. Data moves between devices by JAX's collectives and lax.ppermute only.
A program may use at most 64 MiB of HBM per device.

```python
import jax
import jax.numpy as jnp
from jax import lax

WIN = 64
WIN_T = 128
WPD = 2
MAXIT = 4
HALO = 16
HALO_T = 32
CORE = 32
CORE_T = 64
NI = 128
NX = 512
NT = 512
N_IL = 4
N_XL = 16
N_TA = 4


def window_plan(key):
    base_key = jax.random.fold_in(key, 11)
    key_pair, key_side, key_heavy = jax.random.split(base_key, 3)
    pair_count = N_XL // 2
    busy_pair = jax.random.randint(key_pair, (N_IL, pair_count, N_TA), 0, 2)
    first_line = (jnp.arange(N_IL)[:, None, None] == 0) & (jnp.arange(pair_count)[None, :, None] == 0) & (jnp.arange(N_TA)[None, None, :] == 0)
    busy_pair = jnp.where(first_line, 1, busy_pair)
    busy_side = jax.random.randint(key_side, (N_IL, pair_count, N_TA), 0, 2)
    parity = jnp.arange(N_XL) % 2
    busy_device = jnp.repeat(busy_pair, 2, axis=1) * (jnp.repeat(busy_side, 2, axis=1) == parity[None, :, None])
    heavy_counts = jax.random.randint(key_heavy, (N_IL, N_XL, N_TA, WPD), MAXIT - 1, MAXIT + 1)
    heavy_counts = jnp.where(jnp.arange(WPD)[None, None, None, :] == 0, MAXIT, heavy_counts)
    light_counts = jnp.full((N_IL, N_XL, N_TA, WPD), 2, jnp.int32)
    chosen = jnp.where(busy_device[:, :, :, None] == 1, heavy_counts, light_counts)
    return chosen.reshape(N_IL, N_XL, N_TA * WPD).astype(jnp.int32)


def draw_counts(key, part):
    return window_plan(key)


def draw_levels(key, part):
    values = jax.random.randint(jax.random.fold_in(key, 5), (MAXIT,), 100, 1501)
    ordered = -jnp.sort(-values)
    steps = jnp.arange(MAXIT)
    ordered = jnp.where(steps == 0, 1500, ordered)
    ordered = jnp.where(steps == MAXIT - 1, 100, ordered)
    return ordered.astype(jnp.int32)


def place_ends(array, stream_key, smallest, high):
    longest = array.shape.index(max(array.shape))
    spots = []
    for shift in (0, 1):
        where = [jax.random.randint(jax.random.fold_in(stream_key, axis), (), 0, length) for axis, length in enumerate(array.shape)]
        where[longest] = (where[longest] + shift) % array.shape[longest]
        spots.append(tuple(where))
    return array.at[spots[0]].set(smallest).at[spots[1]].set(high)


def block_scale(stream_key, dims, cuts, low, top_value):
    loudness = 1.0
    for dim, parts in cuts:
        steps = jax.random.uniform(jax.random.fold_in(jax.random.fold_in(stream_key, 6), dim), (parts,), jnp.float32, low / len(cuts), top_value / len(cuts))
        loudness = loudness * jnp.repeat(jnp.exp(steps), dims[dim] // parts).reshape((-1,) + (1,) * (len(dims) - 1 - dim))
    return loudness


def normal_values(stream_key, dims, deviation, reach, cuts=(), held_as=jnp.bfloat16):
    level = block_scale(stream_key, dims, cuts, -0.22, 0.18) if cuts else 1.0
    drawn = jax.random.normal(stream_key, dims, jnp.float32) * deviation * level
    return jnp.minimum(jnp.maximum(drawn, -reach), reach).astype(held_as)


def setup_inputs(seed: int = 0) -> dict:
    splits = jax.random.split(jax.random.key(seed), 5)
    traces = normal_values(splits[0], (NI, NX, NT), 1.0, 6.0, ((0, 4), (1, 16), (2, 4)), jnp.float32)
    live = place_ends((jax.random.randint(splits[1], (NI, NX), 0, 2) < 1).astype(jnp.int32), jax.random.fold_in(splits[1], 1), 0, 1)
    counts = draw_counts(jax.random.fold_in(splits[4], 71), 0)
    levels = draw_levels(jax.random.fold_in(splits[4], 71), 0)
    return {"traces": traces, "live": live, "counts": counts, "levels": levels}


highest = lax.Precision.HIGHEST

def cosine_table(order):
    rows = jnp.arange(order, dtype=jnp.float32)[:, None]
    columns = jnp.arange(order, dtype=jnp.float32)[None, :]
    table = jnp.sqrt(2.0 / order) * jnp.cos(jnp.pi * (2.0 * columns + 1.0) * rows / (2.0 * order))
    scaling = jnp.where(rows == 0, jnp.sqrt(0.5), 1.0)
    return (table * scaling).astype(jnp.float32)

def taper_table(order):
    centres = jnp.arange(order, dtype=jnp.float32) + 0.5
    return jnp.sin(jnp.pi * centres / order) ** 2

def forward(volume, space_table, time_table):
    result = jnp.einsum('ak,ijk->ija', time_table, volume, precision=highest)
    result = jnp.einsum('bj,ija->iba', space_table, result, precision=highest)
    return jnp.einsum('ci,iba->cba', space_table, result, precision=highest)

def inverse(volume, space_table, time_table):
    result = jnp.einsum('ci,cba->iba', space_table, volume, precision=highest)
    result = jnp.einsum('bj,iba->ija', space_table, result, precision=highest)
    return jnp.einsum('ak,ija->ijk', time_table, result, precision=highest)

def reconstruct(window, window_mask, iterations, thresholds, space_table, time_table, taper):
    keep_part = (1.0 - window_mask)[:, :, None]

    def iterate(step_index, estimate):
        coefficients = forward(estimate, space_table, time_table)
        threshold = thresholds[step_index]
        shrunk = coefficients - jnp.clip(coefficients, -threshold, threshold)
        return window + keep_part * inverse(shrunk, space_table, time_table)
    estimate = lax.fori_loop(0, iterations, iterate, window)
    return estimate * taper

def reference(traces, live, counts, levels):
    live_mask = live.astype(jnp.float32)
    observed = jnp.pad(traces * live_mask[:, :, None], ((HALO, HALO), (HALO, HALO), (HALO_T, HALO_T)))
    live_pad = jnp.pad(live_mask, HALO)
    thresholds = levels.astype(jnp.float32) * 0.001
    space_table = cosine_table(WIN)
    time_table = cosine_table(WIN_T)
    space_taper = taper_table(WIN)
    taper = space_taper[:, None, None] * space_taper[None, :, None] * taper_table(WIN_T)[None, None, :]
    windows_time = WPD * N_TA
    flat_counts = counts.reshape(-1)

    def add_window(totals, window_index):
        first = window_index // (N_XL * windows_time)
        second = window_index // windows_time % N_XL
        third = window_index % windows_time
        start_i = (first * CORE).astype(jnp.int32)
        start_x = (second * CORE).astype(jnp.int32)
        start_t = (third * CORE_T).astype(jnp.int32)
        window = lax.dynamic_slice(observed, (start_i, start_x, start_t), (WIN, WIN, WIN_T))
        window_mask = lax.dynamic_slice(live_pad, (start_i, start_x), (WIN, WIN))
        result = reconstruct(window, window_mask, flat_counts[window_index], thresholds, space_table, time_table, taper)
        current = lax.dynamic_slice(totals, (start_i, start_x, start_t), (WIN, WIN, WIN_T))
        return (lax.dynamic_update_slice(totals, current + result, (start_i, start_x, start_t)), None)
    totals, _ = lax.scan(add_window, jnp.zeros(observed.shape, jnp.float32), jnp.arange(N_IL * N_XL * windows_time, dtype=jnp.int32))
    return totals[HALO:HALO + NI, HALO:HALO + NX, HALO_T:HALO_T + NT]
```

```python
import functools

import jax
import jax.numpy as jnp
import numpy as np
from jax import lax
from jax.experimental import pallas as pl
from jax.experimental.pallas import tpu as pltpu
from jax.sharding import PartitionSpec as P

WIN = 64
WIN_T = 128
WPD = 2
HALO = 16
HALO_T = 32
CORE_T = 64


def padded(block, sides, width):
    for axis, dim in sides:
        count = lax.axis_size(axis)
        forward = [(i, i + 1) for i in range(count - 1)]
        backward = [(target, source) for source, target in forward]
        low = lax.ppermute(
            lax.slice_in_dim(block, block.shape[dim] - width, None, axis=dim), axis, forward
        )
        high = lax.ppermute(lax.slice_in_dim(block, 0, width, axis=dim), axis, backward)
        block = jnp.concatenate([low, block, high], axis=dim)
    return block


f32=jnp.float32; bf16=jnp.bfloat16
DEAD=1e30
def dct(n):
    k=np.arange(n)[:,None]; j=np.arange(n)[None,:]
    c=np.sqrt(2.0/n)*np.cos(np.pi*(2*j+1)*k/(2*n)); c[0]*=np.sqrt(0.5); return c
def two(c):
    hi=np.asarray(c,np.float32).astype(jnp.bfloat16); lo=(c-hi.astype(np.float64)).astype(np.float32).astype(jnp.bfloat16)
    return hi,lo
def time_w(c):
    hi,lo=two(c)
    return np.concatenate([np.concatenate([hi,hi],0),np.concatenate([lo,np.zeros_like(lo)],0)],1)
def space_w(c):
    hi,lo=two(c)
    return np.concatenate([np.concatenate([hi,hi],1),np.concatenate([lo,np.zeros_like(lo)],1)],0)
def tables():
    ct=dct(128); cs=dct(64)
    tw=np.stack([time_w(ct.T),time_w(ct)])
    sw=np.stack([space_w(cs),space_w(cs.T)])
    return tw,sw
def split(x):
    hi=x.astype(bf16); return hi,(x-hi.astype(f32)).astype(bf16)
def tmul(x,w):
    hi,lo=split(x)
    y=jnp.dot(jnp.concatenate([hi,lo],1),w,preferred_element_type=f32)
    return y[:,:128]+y[:,128:]
def smul(x,w):
    hi,lo=split(x)
    y=jnp.dot(w,jnp.concatenate([hi,lo],0),preferred_element_type=f32)
    return y[:64]+y[64:]
def to_lanes(x,n):
    return jnp.concatenate([x[64*q:64*q+64] for q in range(n)],1)
def to_rows(x,n):
    return jnp.concatenate([x[:,128*q:128*q+128] for q in range(n)],0)
def swap(x,n):
    y=jnp.stack([x[:,128*q:128*q+128] for q in range(n)],0)
    return jnp.swapaxes(y,0,1)
C=8
def iterate(k,E,Z,Y,W,th,tw,sw,un):
    def p1(n,c):
        r=pl.ds(pl.multiple_of(n*(C*64),C*64),C*64)
        t=tmul(E[r,:],tw[0])
        u=smul(to_lanes(t,C),sw[0])
        Z[:,pl.ds(pl.multiple_of(n*C,C),C),:]=swap(u,C)
        return c
    lax.fori_loop(0,64//C,p1,0,unroll=un)
    def p2(n,c):
        x=Z[pl.ds(pl.multiple_of(n*C,C),C)].reshape(C*64,128)
        u=smul(to_lanes(x,C),sw[0])
        u=u-jnp.clip(u,-th,th)
        v=smul(u,sw[1])
        Y[:,pl.ds(pl.multiple_of(n*C,C),C),:]=swap(v,C)
        return c
    lax.fori_loop(0,64//C,p2,0,unroll=un)
    def p3(n,c):
        x=Y[pl.ds(pl.multiple_of(n*C,C),C)].reshape(C*64,128)
        u=smul(to_lanes(x,C),sw[1])
        g=tmul(to_rows(u,C),tw[1])
        r=pl.ds(pl.multiple_of(n*(C*64),C*64),C*64)
        w=W[r,:]
        E[r,:]=jnp.where(w>1e29,g,w)
        return c
    lax.fori_loop(0,64//C,p3,0,unroll=un)


def taper_table(order):
    centres = jnp.arange(order, dtype=jnp.float32) + 0.5
    return jnp.sin(jnp.pi * centres / order) ** 2


def main_kernel(cnt, th, w_ref, tw, sw, o_ref, E, Z, Y):
    def slot(s, c):
        W = w_ref.at[s]

        def init(n, c):
            r = pl.ds(pl.multiple_of(n * 512, 512), 512)
            w = W[r, :]
            E[r, :] = jnp.where(w > 1e29, 0.0, w)
            return c

        lax.fori_loop(0, 8, init, 0)

        def step(q, c):
            iterate(q, E, Z, Y, W, th[q], tw, sw, 8)
            return c

        lax.fori_loop(0, cnt[s], step, 0)

        def fin(n, c):
            r = pl.ds(pl.multiple_of(n * 512, 512), 512)
            o_ref[s, r, :] = E[r, :]
            return c

        lax.fori_loop(0, 8, fin, 0)
        return c

    lax.fori_loop(0, 2, slot, 0)


def run_windows(counts, thresholds, windows):
    tw, sw = tables()
    V = pl.BlockSpec(memory_space=pltpu.VMEM)
    S = pl.BlockSpec(memory_space=pltpu.SMEM)
    return pl.pallas_call(
        main_kernel,
        out_shape=jax.ShapeDtypeStruct((2, 4096, 128), f32),
        in_specs=[S, S, V, V, V],
        out_specs=V,
        scratch_shapes=[
            pltpu.VMEM((4096, 128), f32),
            pltpu.VMEM((64, 64, 128), f32),
            pltpu.VMEM((64, 64, 128), f32),
        ],
        compiler_params=pltpu.CompilerParams(vmem_limit_bytes=60000 * 1024),
        name="windows",
    )(counts, thresholds, windows, jnp.asarray(tw), jnp.asarray(sw))


def fold_margins(block, dim, width):
    extent = block.shape[dim]
    inner = extent - 4 * width
    middle = lax.slice_in_dim(block, 2 * width, 2 * width + inner, axis=dim)
    lower_rim = lax.slice_in_dim(block, 0, width, axis=dim)
    upper_rim = lax.slice_in_dim(block, extent - width, extent, axis=dim)
    lower_pad = [(0, inner - width) if axis_number == dim else (0, 0) for axis_number in range(3)]
    upper_pad = [(inner - width, 0) if axis_number == dim else (0, 0) for axis_number in range(3)]
    return middle + jnp.pad(lower_rim, lower_pad) + jnp.pad(upper_rim, upper_pad)


def shards(traces, live, counts, levels):
    live_mask = live.astype(jnp.float32)
    timed = padded(traces * live_mask[:, :, None], (("ta", 2),), HALO_T)
    observed = padded(timed, (("il", 0), ("xl", 1)), HALO)
    live_pad = padded(live.astype(jnp.bfloat16), (("il", 0), ("xl", 1)), HALO).astype(jnp.float32)
    thresholds = levels.astype(jnp.float32) * 0.001
    space_taper = taper_table(WIN)
    taper = (
        space_taper[:, None, None] * space_taper[None, :, None] * taper_table(WIN_T)[None, None, :]
    )
    position = lax.axis_index("xl")
    line_counts = counts[0]
    own_counts = lax.dynamic_index_in_dim(line_counts, position, 0, keepdims=False)
    flagged = jnp.where(live_pad[:, :, None] > 0.5, observed, DEAD)
    windows = jnp.stack([flagged[:, :, 0:128], flagged[:, :, 64:192]]).reshape(2, 4096, 128)
    done = run_windows(own_counts, thresholds, windows).reshape(2, 64, 64, 128) * taper
    results = [done[0], done[1]]
    accumulated = jnp.pad(results[0], ((0, 0), (0, 0), (0, (WPD - 1) * CORE_T)))
    slot = 1
    accumulated = accumulated + jnp.pad(
        results[slot], ((0, 0), (0, 0), (slot * CORE_T, (WPD - 1 - slot) * CORE_T))
    )
    spread = padded(accumulated, (("il", 0), ("xl", 1)), HALO)
    spread = fold_margins(spread, 0, HALO)
    spread = fold_margins(spread, 1, HALO)
    spread = padded(spread, (("ta", 2),), HALO_T)
    return fold_margins(spread, 2, HALO_T)


def solution(mesh):
    placed = (P("il", "xl", "ta"), P("il", "xl"), P("il", None, "ta"), P())
    return jax.shard_map(
        shards, mesh=mesh, in_specs=placed, out_specs=P("il", "xl", "ta"), check_vma=False
    )
```

```python
import functools

import jax
import jax.numpy as jnp
import numpy as np
from jax import lax
from jax.experimental import pallas as pl
from jax.experimental.pallas import tpu as pltpu
from jax.sharding import PartitionSpec as P

f32=jnp.float32; bf16=jnp.bfloat16
DEAD=1e30
def dct(n):
    k=np.arange(n)[:,None]; j=np.arange(n)[None,:]
    c=np.sqrt(2.0/n)*np.cos(np.pi*(2*j+1)*k/(2*n)); c[0]*=np.sqrt(0.5); return c
def two(c):
    hi=np.asarray(c,np.float32).astype(jnp.bfloat16); lo=(c-hi.astype(np.float64)).astype(np.float32).astype(jnp.bfloat16)
    return hi,lo
def time_w(c):
    hi,lo=two(c)
    return np.concatenate([np.concatenate([hi,hi],0),np.concatenate([lo,np.zeros_like(lo)],0)],1)
def space_w(c):
    hi,lo=two(c)
    return np.concatenate([np.concatenate([hi,hi],1),np.concatenate([lo,np.zeros_like(lo)],1)],0)
def tables():
    ct=dct(128); cs=dct(64)
    tw=np.stack([time_w(ct.T),time_w(ct)])
    sw=np.stack([space_w(cs),space_w(cs.T)])
    return tw,sw
def split(x):
    hi=x.astype(bf16); return hi,(x-hi.astype(f32)).astype(bf16)
def tmul(x,w):
    hi,lo=split(x)
    y=jnp.dot(jnp.concatenate([hi,lo],1),w,preferred_element_type=f32)
    return y[:,:128]+y[:,128:]
def smul(x,w):
    hi,lo=split(x)
    y=jnp.dot(w,jnp.concatenate([hi,lo],0),preferred_element_type=f32)
    return y[:64]+y[64:]
def to_lanes(x,n):
    return jnp.concatenate([x[64*q:64*q+64] for q in range(n)],1)
def to_rows(x,n):
    return jnp.concatenate([x[:,128*q:128*q+128] for q in range(n)],0)
def swap(x,n):
    y=jnp.stack([x[:,128*q:128*q+128] for q in range(n)],0)
    return jnp.swapaxes(y,0,1)
C=8
def iterate(k,E,Z,Y,W,th,tw,sw,un):
    def p1(n,c):
        r=pl.ds(pl.multiple_of(n*(C*64),C*64),C*64)
        t=tmul(E[r,:],tw[0])
        u=smul(to_lanes(t,C),sw[0])
        Z[:,pl.ds(pl.multiple_of(n*C,C),C),:]=swap(u,C)
        return c
    lax.fori_loop(0,64//C,p1,0,unroll=un)
    def p2(n,c):
        x=Z[pl.ds(pl.multiple_of(n*C,C),C)].reshape(C*64,128)
        u=smul(to_lanes(x,C),sw[0])
        u=u-jnp.clip(u,-th,th)
        v=smul(u,sw[1])
        Y[:,pl.ds(pl.multiple_of(n*C,C),C),:]=swap(v,C)
        return c
    lax.fori_loop(0,64//C,p2,0,unroll=un)
    def p3(n,c):
        x=Y[pl.ds(pl.multiple_of(n*C,C),C)].reshape(C*64,128)
        u=smul(to_lanes(x,C),sw[1])
        g=tmul(to_rows(u,C),tw[1])
        r=pl.ds(pl.multiple_of(n*(C*64),C*64),C*64)
        w=W[r,:]
        E[r,:]=jnp.where(w>1e29,g,w)
        return c
    lax.fori_loop(0,64//C,p3,0,unroll=un)


Q = 32000.0
LN = float(np.log(2.0) / 128.0)
i32 = jnp.int32
i16 = jnp.int16


def lanes(rows=32):
    return lax.broadcasted_iota(i32, (rows, 128), 1)


def quarter(rows, *which):
    q = lanes(rows) // 32
    m = q == which[0]
    for w in which[1:]:
        m = m | (q == w)
    return m


def roll(x, s):
    return x if s == 0 else pltpu.roll(x, s, 1)


def b16(ref, b, n=16):
    return ref[pl.ds(pl.multiple_of(b * n, n), n), :]


def encode(src, dst, n, flagged, un=8):
    def top(b, m):
        x = b16(src, b)
        a = jnp.abs(x)
        if flagged:
            a = jnp.where(x > 1e29, 0.0, a)
        return jnp.maximum(m, a)

    m = lax.fori_loop(0, n, top, jnp.full((16, 128), 1e-30, f32), unroll=un)
    code = jnp.ceil(jnp.log(m) * (1.0 / LN))
    scale = Q * jnp.exp(code * -LN)

    def put(b, c):
        x = b16(src, b)
        q = jnp.round(x * scale)
        if flagged:
            q = jnp.where(x > 1e29, 0.0, jnp.where(q >= 0, q + 1.0, q))
        dst[pl.ds(pl.multiple_of(b * 16, 16), 16), :] = q.astype(i32).astype(i16)
        return c

    lax.fori_loop(0, n, put, 0, unroll=un)
    dst[pl.ds(n * 16, 16), :] = code.astype(i32).astype(i16)


def scale_of(ref, n):
    return jnp.exp(ref[pl.ds(n * 16, 16), :].astype(i32).astype(f32) * LN) * (1.0 / Q)


def decode(ref, b, scale, flagged):
    q = b16(ref, b).astype(i32).astype(f32)
    if flagged:
        return jnp.where(q == 0, DEAD, (q - jnp.where(q > 0, 1.0, 0.0)) * scale)
    return q * scale


def spread_live(live_ref):
    lt = live_ref[...].astype(f32).T
    return [jnp.broadcast_to(lt[:, i : i + 1], (32, 128)) > 0.5 for i in range(32)]


def pack_kernel(x_ref, live_ref, left, right, sl, sr):
    lv = spread_live(live_ref)
    q = lanes() // 32

    def pick(parts):
        out = parts[3]
        for n in (2, 1, 0):
            out = jnp.where(q == n, parts[n], out)
        return out

    for r in range(8):
        x = [jnp.where(lv[i], x_ref[i], 0.0) for i in (r, r + 8, r + 16, r + 24)]
        sr[r * 32 : r * 32 + 32, :] = pick([roll(x[0], 32), roll(x[2], 64), roll(x[1], 96), x[3]])
        sl[r * 32 : r * 32 + 32, :] = pick([x[2], roll(x[1], 32), roll(x[3], 64), roll(x[0], 96)])
    encode(sl, left, 16, False)
    encode(sr, right, 16, False)


def widen_kernel(x_ref, live_ref, fl, fr, main, side, lo, hi, slo, shi):
    lv = spread_live(live_ref)
    isl = quarter(32, 0, 2)
    first = quarter(32, 0, 3)
    kl, kr = scale_of(fl, 16), scale_of(fr, 16)
    for r in range(8):
        dl = jnp.concatenate([decode(fl, 2 * r + h, kl, False) for h in (0, 1)], 0)
        dr = jnp.concatenate([decode(fr, 2 * r + h, kr, False) for h in (0, 1)], 0)
        for g, s in ((0, slo), (1, shi)):
            a, b = (dl, dr) if g == 0 else (roll(dl, 96), roll(dr, 96))
            i = 16 * g + r
            alive = jnp.where(first, lv[i].astype(f32), lv[i + 8].astype(f32)) > 0.5
            v = jnp.where(alive, jnp.where(isl, a, b), DEAD)
            side[8 * g + r] = v
            s[pl.ds((16 + r) * 32, 32), :] = v
            for e in (0, 8):
                w = jnp.where(lv[i + e], x_ref[i + e], DEAD)
                main[i + e] = w
                s[pl.ds((r + e) * 32, 32), :] = w
    encode(slo, lo, 48, True)
    encode(shi, hi, 48, True)


def edge_kernel(main, side, f0, f3, lo, hi, slo, shi):
    k0, k3 = scale_of(f0, 48), scale_of(f3, 48)
    for f, k, g in ((f0, k0, 0), (f3, k3, 3)):

        def take(p, c, f=f, k=k, g=g):
            at = pl.ds(pl.multiple_of((24 * g + p) * 16, 16), 16)
            slo[at, :] = decode(f, 2 * p, k, True)
            shi[at, :] = decode(f, 2 * p + 1, k, True)
            return c

        lax.fori_loop(0, 24, take, 0, unroll=8)
    for g in (0, 1):
        for p in range(24):
            v = main[16 * g + p] if p < 16 else side[8 * g + p - 16]
            at = (24 * (g + 1) + p) * 16
            slo[at : at + 16, :] = v[:16]
            shi[at : at + 16, :] = v[16:]
    encode(slo, lo, 96, True)
    encode(shi, hi, 96, True)


def main_kernel(cnt, levels, main, side, f0, f3, fa, fb, tj, ti, tw, sw, lo, hi, cmain, cside, W, E, Z, Y, slo, shi):
    first, last = lanes(64) < 32, lanes(64) >= 96
    k0, k3, ka, kb = scale_of(f0, 48), scale_of(f3, 48), scale_of(fa, 96), scale_of(fb, 96)

    def whole(g, p, mid):
        a = decode(fa, 24 * g + p, ka, True)
        b = decode(fb, 24 * g + p, kb, True)
        return jnp.concatenate([a, mid, b], 0)

    for g in range(4):

        def build(r, c, g=g):
            def plane(p):
                if g == 0 or g == 3:
                    f, k = (f0, k0) if g == 0 else (f3, k3)
                    mid = jnp.concatenate([decode(f, 2 * p + h, k, True) for h in (0, 1)], 0)
                    return whole(g, p, mid)
                return None

            if g == 0 or g == 3:
                m0, m1, s = plane(r), plane(r + 8), plane(r + 16)
            else:
                m0 = whole(g, r, main[16 * (g - 1) + r])
                m1 = whole(g, r + 8, main[16 * (g - 1) + r + 8])
                s = whole(g, r + 16, side[8 * (g - 1) + r])
            for m, v, i in ((m0, s, r), (m1, roll(s, 64), r + 8)):
                at = pl.ds(pl.multiple_of((16 * g + i) * 64, 64), 64)
                W[0, at, :] = jnp.where(first, v, roll(m, 32))
                W[1, at, :] = jnp.where(last, v, roll(m, 96))
            return c

        lax.fori_loop(0, 8, build, 0, unroll=2)

    position = lax.axis_index("xl")

    def slot(s, c):
        Ws = W.at[s]

        def init(n, c):
            r = pl.ds(pl.multiple_of(n * 512, 512), 512)
            w = Ws[r, :]
            E[r, :] = jnp.where(w > 1e29, 0.0, w)
            return c

        lax.fori_loop(0, 8, init, 0)

        def step(q, c):
            iterate(q, E, Z, Y, Ws, levels[q].astype(f32) * 0.001, tw, sw, 8)
            return c

        lax.fori_loop(0, cnt[0, position, s], step, 0)

        def fin(i, c):
            r = pl.ds(pl.multiple_of(i * 64, 64), 64)
            Ws[r, :] = E[r, :] * (tj[...] * ti[pl.ds(i, 1), :])
            return c

        lax.fori_loop(0, 64, fin, 0, unroll=8)
        return c

    lax.fori_loop(0, 2, slot, 0)
    q = lanes(64) // 32

    def part(g, c):
        def split_up(p, v):
            slo[pl.ds(pl.multiple_of((24 * g + p) * 16, 16), 16), :] = v[:16]
            shi[pl.ds(pl.multiple_of((24 * g + p) * 16, 16), 16), :] = v[48:]

        for r in range(8):
            x = []
            for e in (0, 8):
                at = pl.ds(pl.multiple_of((16 * g + r + e) * 64, 64), 64)
                a, b = W[0, at, :], W[1, at, :]
                x += [a, b]
                v = jnp.where(q < 3, roll(a, 96), 0.0) + jnp.where(q > 0, roll(b, 32), 0.0)
                split_up(r + e, v)
                cmain[16 * g + r + e] = v[16:48]
            v = jnp.where(q == 0, x[0], jnp.where(q == 3, x[1], roll(jnp.where(q == 0, x[2], x[3]), 64)))
            split_up(16 + r, v)
            cside[8 * g + r] = v[16:48]
        return c

    lax.fori_loop(0, 4, part, 0)
    encode(slo, lo, 96, False)
    encode(shi, hi, 96, False)


def fold_kernel(cmain, cside, fa, fb, main, side, lo, hi, slo, shi):
    ka, kb = scale_of(fa, 96), scale_of(fb, 96)
    for g in range(4):

        def add(v, p, g=g):
            a = decode(fa, 24 * g + p, ka, False)
            b = decode(fb, 24 * g + p, kb, False)
            return v + jnp.concatenate([a, b], 0)

        def put(dst, s, p, v, at, g=g):
            if g == 0 or g == 3:
                s[pl.ds(pl.multiple_of(p * 32, 32), 32), :] = v
            else:
                dst[at] = v

        s = slo if g == 0 else shi

        def mains(p, c, g=g, s=s):
            put(main, s, p, add(cmain[16 * g + p], p), 16 * (g - 1) + p)
            return c

        def sides(p, c, g=g, s=s):
            put(side, s, 16 + p, add(cside[8 * g + p], 16 + p), 8 * (g - 1) + p)
            return c

        lax.fori_loop(0, 16, mains, 0, unroll=8)
        lax.fori_loop(0, 8, sides, 0, unroll=8)
    encode(slo, lo, 48, False)
    encode(shi, hi, 48, False)


def narrow_kernel(main, side, fa, fb, out, left, right, sl, sr):
    isl = quarter(32, 0, 2)
    ka, kb = scale_of(fa, 48), scale_of(fb, 48)

    def both(f, p, k):
        return jnp.concatenate([decode(f, 2 * p + h, k, False) for h in (0, 1)], 0)

    def mains(p, c):
        out[p] = main[p] + both(fa, p, ka)
        out[16 + p] = main[16 + p] + both(fb, p, kb)
        return c

    lax.fori_loop(0, 16, mains, 0, unroll=4)
    for r in range(8):
        a = side[r] + both(fa, 16 + r, ka)
        b = roll(side[8 + r] + both(fb, 16 + r, kb), 32)
        sl[r * 32 : r * 32 + 32, :] = jnp.where(isl, a, b)
        sr[r * 32 : r * 32 + 32, :] = jnp.where(isl, b, a)
    encode(sl, left, 16, False)
    encode(sr, right, 16, False)


def last_kernel(main, fl, fr, out):
    kl, kr = scale_of(fl, 16), scale_of(fr, 16)
    q = lanes() // 32
    for r in range(8):
        a = jnp.concatenate([decode(fl, 2 * r + h, kl, False) for h in (0, 1)], 0)
        b = jnp.concatenate([decode(fr, 2 * r + h, kr, False) for h in (0, 1)], 0)
        for i, sa, sb in ((r, 32, 96), (r + 8, 96, 32), (r + 16, 0, 64), (r + 24, 64, 0)):
            out[i] = main[i] + jnp.where(q == 0, roll(a, sa), jnp.where(q == 3, roll(b, sb), 0.0))


V = pl.BlockSpec(memory_space=pltpu.VMEM)
S = pl.BlockSpec(memory_space=pltpu.SMEM)


def call(kernel, name, outs, scratch, specs, *args):
    shapes = [jax.ShapeDtypeStruct(s, t) for s, t in outs]
    return pl.pallas_call(
        kernel,
        out_shape=shapes,
        in_specs=specs,
        out_specs=[V] * len(outs),
        scratch_shapes=[pltpu.VMEM(s, f32) for s in scratch],
        compiler_params=pltpu.CompilerParams(vmem_limit_bytes=60000 * 1024),
        name=name,
    )(*args)


def exchange(low, high, axis):
    count = lax.axis_size(axis)
    forward = [(i, i + 1) for i in range(count - 1)]
    backward = [(b, a) for a, b in forward]
    return lax.ppermute(high, axis, forward), lax.ppermute(low, axis, backward)


def rows(n):
    return ((n * 16 + 16, 128), i16)


def taper(order):
    return np.sin(np.pi * (np.arange(order) + 0.5) / order) ** 2


def shards(traces, live, counts, levels):
    tw, sw = tables()
    tj = jnp.asarray((taper(64)[:, None] * taper(128)[None, :]).astype(np.float32))
    ti = jnp.asarray(np.broadcast_to(taper(64)[:, None], (64, 128)).astype(np.float32))
    lo, hi = call(pack_kernel, "pack", [rows(16)] * 2, [(256, 128)] * 2, [V] * 2, traces, live)
    fl, fr = exchange(lo, hi, "ta")
    main, side, lo, hi = call(
        widen_kernel,
        "widen",
        [((32, 32, 128), f32), ((16, 32, 128), f32), rows(48), rows(48)],
        [(768, 128)] * 2,
        [V] * 4,
        traces,
        live,
        fl,
        fr,
    )
    f0, f3 = exchange(lo, hi, "il")
    lo, hi = call(edge_kernel, "edge", [rows(96)] * 2, [(1536, 128)] * 2, [V] * 4, main, side, f0, f3)
    fa, fb = exchange(lo, hi, "xl")
    lo, hi, cmain, cside = call(
        main_kernel,
        "windows",
        [rows(96), rows(96), ((64, 32, 128), f32), ((32, 32, 128), f32)],
        [(2, 4096, 128), (4096, 128), (64, 64, 128), (64, 64, 128), (1536, 128), (1536, 128)],
        [S, S] + [V] * 10,
        counts,
        levels,
        main,
        side,
        f0,
        f3,
        fa,
        fb,
        tj,
        ti,
        jnp.asarray(tw),
        jnp.asarray(sw),
    )
    fa, fb = exchange(lo, hi, "xl")
    main, side, lo, hi = call(
        fold_kernel,
        "fold",
        [((32, 32, 128), f32), ((16, 32, 128), f32), rows(48), rows(48)],
        [(768, 128)] * 2,
        [V] * 4,
        cmain,
        cside,
        fa,
        fb,
    )
    fa, fb = exchange(lo, hi, "il")
    main, lo, hi = call(
        narrow_kernel,
        "narrow",
        [((32, 32, 128), f32), rows(16), rows(16)],
        [(256, 128)] * 2,
        [V] * 4,
        main,
        side,
        fa,
        fb,
    )
    fl, fr = exchange(lo, hi, "ta")
    return call(last_kernel, "last", [((32, 32, 128), f32)], [], [V] * 3, main, fl, fr)[0]


def solution(mesh):
    placed = (P("il", "xl", "ta"), P("il", "xl"), P("il", None, "ta"), P())
    return jax.shard_map(
        shards, mesh=mesh, in_specs=placed, out_specs=P("il", "xl", "ta"), check_vma=False
    )
```

```python
import jax
import jax.numpy as jnp
import numpy as np
from jax import lax
from jax.experimental import pallas as pl
from jax.experimental.pallas import tpu as pltpu
from jax.sharding import PartitionSpec as P

f32=jnp.float32; bf16=jnp.bfloat16
DEAD=1e30
def dct(n):
    k=np.arange(n)[:,None]; j=np.arange(n)[None,:]
    c=np.sqrt(2.0/n)*np.cos(np.pi*(2*j+1)*k/(2*n)); c[0]*=np.sqrt(0.5); return c
def two(c):
    hi=np.asarray(c,np.float32).astype(jnp.bfloat16); lo=(c-hi.astype(np.float64)).astype(np.float32).astype(jnp.bfloat16)
    return hi,lo
def time_w(c):
    hi,lo=two(c)
    return np.concatenate([np.concatenate([hi,hi],0),np.concatenate([lo,np.zeros_like(lo)],0)],1)
def space_w(c):
    hi,lo=two(c)
    return np.concatenate([np.concatenate([hi,hi],1),np.concatenate([lo,np.zeros_like(lo)],1)],0)
def tables():
    ct=dct(128); cs=dct(64)
    tw=np.stack([time_w(ct.T),time_w(ct)])
    sw=np.stack([space_w(cs),space_w(cs.T)])
    return tw,sw
def split(x):
    hi=x.astype(bf16); return hi,(x-hi.astype(f32)).astype(bf16)
def tmul(x,w):
    hi,lo=split(x)
    y=jnp.dot(jnp.concatenate([hi,lo],1),w,preferred_element_type=f32)
    return y[:,:128]+y[:,128:]
def smul(x,w):
    hi,lo=split(x)
    y=jnp.dot(w,jnp.concatenate([hi,lo],0),preferred_element_type=f32)
    return y[:64]+y[64:]
def to_lanes(x,n):
    return jnp.concatenate([x[64*q:64*q+64] for q in range(n)],1)
def to_rows(x,n):
    return jnp.concatenate([x[:,128*q:128*q+128] for q in range(n)],0)
def swap(x,n):
    y=jnp.stack([x[:,128*q:128*q+128] for q in range(n)],0)
    return jnp.swapaxes(y,0,1)
C=8
def iterate(E,Z,Y,R,off,th,tw,sw,un):
    def p1(n,c):
        r=pl.ds(pl.multiple_of(n*(C*64),C*64),C*64)
        t=tmul(E[r,:],tw[0])
        u=smul(to_lanes(t,C),sw[0])
        Z[:,pl.ds(pl.multiple_of(n*C,C),C),:]=swap(u,C)
        return c
    lax.fori_loop(0,64//C,p1,0,unroll=un)
    def p2(n,c):
        x=Z[pl.ds(pl.multiple_of(n*C,C),C)].reshape(C*64,128)
        u=smul(to_lanes(x,C),sw[0])
        u=u-jnp.clip(u,-th,th)
        v=smul(u,sw[1])
        Y[:,pl.ds(pl.multiple_of(n*C,C),C),:]=swap(v,C)
        return c
    lax.fori_loop(0,64//C,p2,0,unroll=un)
    def p3(n,c):
        x=Y[pl.ds(pl.multiple_of(n*C,C),C)].reshape(C*64,128)
        u=smul(to_lanes(x,C),sw[1])
        g=tmul(to_rows(u,C),tw[1])
        r=pl.ds(pl.multiple_of(n*(C*64),C*64),C*64)
        w=R[pl.ds(pl.multiple_of(n*C,C),C),pl.ds(off,64),:].reshape(C*64,128)
        E[r,:]=jnp.where(w>1e29,g,w)
        return c
    lax.fori_loop(0,64//C,p3,0,unroll=un)


Q = 32000.0
LN = float(np.log(2.0) / 128.0)
i32 = jnp.int32
i16 = jnp.int16


def parity():
    return lax.rem(lax.axis_index("xl"), 2)


def roll(x, s):
    if isinstance(s, int):
        s %= 128
        if s == 0:
            return x
    return pltpu.roll(x, s, 1)


def at(b, n):
    return pl.ds(pl.multiple_of(b * n, n), n)


def encode(get, dst, n, flagged, un=8):
    def top(b, m):
        x = get(b)
        a = jnp.abs(x)
        if flagged:
            a = jnp.where(x > 1e29, 0.0, a)
        return jnp.maximum(m, a)

    m = lax.fori_loop(0, n, top, jnp.full((16, 128), 1e-30, f32), unroll=un)
    code = jnp.ceil(jnp.log(m) * (1.0 / LN))
    scale = Q * jnp.exp(code * -LN)

    def put(b, c):
        x = get(b)
        q = jnp.round(x * scale)
        if flagged:
            q = jnp.where(x > 1e29, 0.0, jnp.where(q >= 0, q + 1.0, q))
        dst[at(b, 16), :] = q.astype(i32).astype(i16)
        return c

    lax.fori_loop(0, n, put, 0, unroll=un)
    dst[pl.ds(n * 16, 16), :] = code.astype(i32).astype(i16)


def blocks(ref, first=0):
    return lambda b: ref[at(b + first, 16), :]


def scale_of(ref, n):
    return jnp.exp(ref[pl.ds(n * 16, 16), :].astype(i32).astype(f32) * LN) * (1.0 / Q)


def decode(ref, b, scale, flagged=False):
    q = ref[at(b, 16), :].astype(i32).astype(f32)
    if flagged:
        return jnp.where(q == 0, DEAD, (q - jnp.where(q > 0, 1.0, 0.0)) * scale)
    return q * scale


def pair_rows(ref, r, scale):
    return jnp.concatenate([decode(ref, 2 * r + h, scale) for h in (0, 1)], 0)


def spread(parts, q):
    out = parts[3]
    for n in (2, 1, 0):
        out = jnp.where(q == n, parts[n], out)
    return out


def lane_quarter():
    return lax.broadcasted_iota(i32, (32, 128), 1) // 32


def pack_kernel(x_ref, live_ref, flagged, a_out, b_out, sa, sb):
    odd = parity()
    lt = live_ref[...].astype(f32).T
    q = lane_quarter()
    for r in range(8):
        x = []
        for i in (r, r + 8, r + 16, r + 24):
            alive = jnp.broadcast_to(lt[:, i : i + 1], (32, 128)) > 0.5
            flagged[i] = jnp.where(alive, x_ref[i], DEAD)
            x.append(jnp.where(alive, x_ref[i], 0.0))
        sa[r * 32 : r * 32 + 32, :] = spread([roll(v, (32 * n + 32 * (1 - odd)) % 128) for n, v in enumerate(x)], q)
        sb[r * 32 : r * 32 + 32, :] = spread([roll(v, (32 * n + 32 * odd) % 128) for n, v in enumerate(x)], q)
    encode(blocks(sa), a_out, 16, False)
    encode(blocks(sb), b_out, 16, False)


def widen_kernel(own, other, fa, fb, tile, lo, hi):
    odd = parity()
    halo = lane_quarter() == 3 * odd
    for x, f, column in ((own, fa, 32 * odd), (other, fb, 32 - 32 * odd)):
        k = scale_of(f, 16)
        for r in range(8):
            h = pair_rows(f, r, k)
            for n in range(4):
                i = r + 8 * n
                v = x[i]
                h_n = jnp.where(v > 1e29, DEAD, roll(h, (128 - 32 * n + 96 * odd) % 128))
                rows = pl.ds(pl.multiple_of(i * 64 + column, 32), 32)
                tile[rows, :] = jnp.where(halo, h_n, roll(v, 32 + 64 * odd))
    encode(blocks(tile), lo, 64, True)
    encode(blocks(tile, 64), hi, 64, True)


def edge_kernel(tile, f0, f3, lo, hi, slo, shi):
    for f, base in ((f0, 0), (f3, 48)):
        k = scale_of(f, 64)

        def take(i, c, f=f, k=k, base=base):
            slo[at(base + i, 16), :] = decode(f, 4 * i, k, True)
            shi[at(base + i, 16), :] = decode(f, 4 * i + 3, k, True)
            return c

        lax.fori_loop(0, 16, take, 0, unroll=8)

    def copy(i, c):
        slo[at(16 + i, 16), :] = tile[at(4 * i, 16), :]
        shi[at(16 + i, 16), :] = tile[at(4 * i + 3, 16), :]
        return c

    lax.fori_loop(0, 32, copy, 0, unroll=8)
    encode(blocks(slo), lo, 64, True)
    encode(blocks(shi), hi, 64, True)


def main_kernel(cnt, levels, tile, f0, f3, fa, fb, tj, ti, tw, sw, lo, hi, core, R, acc, E, Z, Y):
    ka, kb = scale_of(fa, 64), scale_of(fb, 64)

    def sides(i, c):
        R[i, 0:16, :] = decode(fa, i, ka, True)
        R[i, 80:96, :] = decode(fb, i, kb, True)
        return c

    lax.fori_loop(0, 64, sides, 0, unroll=8)
    for f, base in ((f0, 0), (f3, 48)):
        k = scale_of(f, 64)

        def take(i, c, f=f, k=k, base=base):
            for x in range(4):
                R[base + i, 16 + 16 * x : 32 + 16 * x, :] = decode(f, 4 * i + x, k, True)
            return c

        lax.fori_loop(0, 16, take, 0, unroll=4)

    def copy(i, c):
        R[16 + i, 16:80, :] = tile[at(i, 64), :]
        return c

    lax.fori_loop(0, 32, copy, 0, unroll=8)
    position = lax.axis_index("xl")
    odd = lax.rem(position, 2)
    zeros = jnp.zeros((32, 128), f32)

    def window(s, c):
        off = pl.multiple_of(s * 32, 32)

        def init(i, c):
            w = R[i, pl.ds(off, 64), :]
            E[at(i, 64), :] = jnp.where(w > 1e29, 0.0, w)
            return c

        lax.fori_loop(0, 64, init, 0, unroll=8)

        def step(q, c):
            iterate(E, Z, Y, R, off, levels[q].astype(f32) * 0.001, tw, sw, 8)
            return c

        lax.fori_loop(0, cnt[0, odd, position - odd + s], step, 0)

        def finish(i, c):
            v = E[at(i, 64), :] * (tj[...] * ti[pl.ds(i, 1), :])
            acc[i, pl.ds(off, 32), :] = jnp.where(s > 0, acc[i, pl.ds(off, 32), :], zeros) + v[:32]
            acc[i, pl.ds(off + 32, 32), :] = v[32:]
            return c

        lax.fori_loop(0, 64, finish, 0, unroll=8)
        return c

    lax.fori_loop(0, 2, window, 0)
    encode(lambda i: acc[i, 0:16, :], lo, 64, False)
    encode(lambda i: acc[i, 80:96, :], hi, 64, False)

    def give(i, c):
        core[at(i, 64), :] = acc[i, 16:80, :]
        return c

    lax.fori_loop(0, 64, give, 0, unroll=8)


def fold_kernel(core, fa, fb, inner, lo, hi, slo, shi):
    ka, kb = scale_of(fa, 64), scale_of(fb, 64)
    for first, n, dst in ((0, 16, slo), (16, 32, inner), (48, 16, shi)):

        def add(i, c, first=first, dst=dst):
            p = first + i
            v = core[at(p, 64), :]
            dst[at(4 * i, 16), :] = v[:16] + decode(fa, p, ka)
            dst[pl.ds(pl.multiple_of(i * 64 + 16, 16), 32), :] = v[16:48]
            dst[at(4 * i + 3, 16), :] = v[48:] + decode(fb, p, kb)
            return c

        lax.fori_loop(0, n, add, 0, unroll=8)
    encode(blocks(slo), lo, 64, False)
    encode(blocks(shi), hi, 64, False)


def narrow_kernel(inner, fa, fb, own, other, a_out, b_out, sa, sb):
    odd = parity()
    q = lane_quarter()
    ka, kb = scale_of(fa, 64), scale_of(fb, 64)
    for dst, s, column in ((own, sa, odd), (other, sb, 1 - odd)):
        for r in range(8):
            parts = []
            for n in range(4):
                i = r + 8 * n
                f, k, p = (fa, ka, i) if i < 16 else (fb, kb, i - 16)
                b = 4 * p + 2 * column
                v = inner[pl.ds(pl.multiple_of(i * 64 + 32 * column, 32), 32), :]
                v = v + jnp.concatenate([decode(f, b, k), decode(f, b + 1, k)], 0)
                dst[i] = v
                parts.append(roll(v, (32 * n + 32 * odd) % 128))
            s[r * 32 : r * 32 + 32, :] = spread(parts, q)
    encode(blocks(sa), a_out, 16, False)
    encode(blocks(sb), b_out, 16, False)


def last_kernel(own, other, fa, fb, out):
    odd = parity()
    q = lane_quarter()
    low, high = 3 - 3 * odd, 3 * odd
    ka, kb = scale_of(fa, 16), scale_of(fb, 16)
    for r in range(8):
        a, b = pair_rows(fa, r, ka), pair_rows(fb, r, kb)
        for n in range(4):
            i = r + 8 * n
            v = jnp.where(q == low, roll(a, (224 - 32 * n + 32 * odd) % 128), roll(own[i], (96 + 64 * odd) % 128))
            w = jnp.where(q == high, roll(b, (256 - 32 * n + 96 * odd) % 128), roll(other[i], (32 + 64 * odd) % 128))
            out[i] = v + w


V = pl.BlockSpec(memory_space=pltpu.VMEM)
S = pl.BlockSpec(memory_space=pltpu.SMEM)


def call(kernel, name, mib, outs, scratch, specs, *args):
    shapes = [jax.ShapeDtypeStruct(s, t) for s, t in outs]
    return pl.pallas_call(
        kernel,
        out_shape=shapes,
        in_specs=specs,
        out_specs=[V] * len(outs),
        scratch_shapes=[pltpu.VMEM(s, f32) for s in scratch],
        compiler_params=pltpu.CompilerParams(vmem_limit_bytes=mib * 1024 * 1024),
        name=name,
    )(*args)


def exchange(low, high, axis, step):
    count = lax.axis_size(axis)
    forward = [(i, i + step) for i in range(count - step)]
    backward = [(b, a) for a, b in forward]
    return lax.ppermute(high, axis, forward), lax.ppermute(low, axis, backward)


def swap_pair(x):
    return lax.ppermute(x, "xl", [(i, i ^ 1) for i in range(lax.axis_size("xl"))])


def exchange_time(a, b, outward):
    nx, nt = lax.axis_size("xl"), lax.axis_size("ta")
    straight, cross = [], []
    for x in range(nx):
        for t in range(nt):
            s = t + (1 if (x % 2 == 0) == outward else -1)
            if 0 <= s < nt:
                straight.append((x * nt + t, x * nt + s))
            s = t + (-1 if x % 2 == 0 else 1)
            if 0 <= s < nt:
                cross.append((x * nt + t, (x ^ 1) * nt + s))
    return lax.ppermute(a, ("xl", "ta"), straight), lax.ppermute(b, ("xl", "ta"), cross)


def codes(n):
    return ((n * 16 + 16, 128), i16)


def taper(order):
    return np.sin(np.pi * (np.arange(order) + 0.5) / order) ** 2


TILE = ((32, 32, 128), f32)


def shards(traces, live, counts, levels):
    tw, sw = tables()
    tj = jnp.asarray((taper(64)[:, None] * taper(128)[None, :]).astype(np.float32))
    ti = jnp.asarray(np.broadcast_to(taper(64)[:, None], (64, 128)).astype(np.float32))
    own, a, b = call(pack_kernel, "pack", 4, [TILE, codes(16), codes(16)], [(256, 128)] * 2, [V] * 2, traces, live)
    fa, fb = exchange_time(a, b, True)
    other = swap_pair(own)
    tile, lo, hi = call(
        widen_kernel, "widen", 6, [((2048, 128), f32), codes(64), codes(64)], [], [V] * 4, own, other, fa, fb
    )
    f0, f3 = exchange(lo, hi, "il", 1)
    lo, hi = call(edge_kernel, "edge", 6, [codes(64)] * 2, [(1024, 128)] * 2, [V] * 3, tile, f0, f3)
    fa, fb = exchange(lo, hi, "xl", 2)
    lo, hi, core = call(
        main_kernel,
        "windows",
        32,
        [codes(64), codes(64), ((4096, 128), f32)],
        [(64, 96, 128), (64, 96, 128), (4096, 128), (64, 64, 128), (64, 64, 128)],
        [S, S] + [V] * 9,
        counts.transpose(0, 2, 1),
        levels,
        tile,
        f0,
        f3,
        fa,
        fb,
        tj,
        ti,
        jnp.asarray(tw),
        jnp.asarray(sw),
    )
    fa, fb = exchange(lo, hi, "xl", 2)
    inner, lo, hi = call(
        fold_kernel, "fold", 8, [((2048, 128), f32), codes(64), codes(64)], [(1024, 128)] * 2, [V] * 3, core, fa, fb
    )
    fa, fb = exchange(lo, hi, "il", 1)
    own, other, a, b = call(
        narrow_kernel, "narrow", 6, [TILE, TILE, codes(16), codes(16)], [(256, 128)] * 2, [V] * 3, inner, fa, fb
    )
    fa, fb = exchange_time(a, b, False)
    other = swap_pair(other)
    return call(last_kernel, "last", 4, [TILE], [], [V] * 4, own, other, fa, fb)[0]


def solution(mesh):
    placed = (P("il", "xl", "ta"), P("il", "xl"), P("il", None, "ta"), P())
    return jax.shard_map(
        shards, mesh=mesh, in_specs=placed, out_specs=P("il", "xl", "ta"), check_vma=False
    )
```

```python
import jax
import jax.numpy as jnp
import numpy as np
from jax import lax
from jax.experimental import pallas as pl
from jax.experimental.pallas import tpu as pltpu
from jax.sharding import PartitionSpec as P

f32=jnp.float32; bf16=jnp.bfloat16
DEAD=1e30
def dct(n):
    k=np.arange(n)[:,None]; j=np.arange(n)[None,:]
    c=np.sqrt(2.0/n)*np.cos(np.pi*(2*j+1)*k/(2*n)); c[0]*=np.sqrt(0.5); return c
def two(c):
    hi=np.asarray(c,np.float32).astype(jnp.bfloat16); lo=(c-hi.astype(np.float64)).astype(np.float32).astype(jnp.bfloat16)
    return hi,lo
def time_w(c):
    hi,lo=two(c)
    return np.concatenate([np.concatenate([hi,hi],0),np.concatenate([lo,np.zeros_like(lo)],0)],1)
def space_w(c):
    hi,lo=two(c)
    return np.concatenate([np.concatenate([hi,hi],1),np.concatenate([lo,np.zeros_like(lo)],1)],0)
def tables():
    ct=dct(128); cs=dct(64)
    tw=np.stack([time_w(ct.T),time_w(ct)])
    sw=np.stack([space_w(cs),space_w(cs.T)])
    return tw,sw
def split(x):
    hi=x.astype(bf16); return hi,(x-hi.astype(f32)).astype(bf16)
def tmul(x,w):
    hi,lo=split(x)
    y=jnp.dot(jnp.concatenate([hi,lo],1),w,preferred_element_type=f32)
    return y[:,:128]+y[:,128:]
def smul(x,w):
    hi,lo=split(x)
    y=jnp.dot(w,jnp.concatenate([hi,lo],0),preferred_element_type=f32)
    return y[:64]+y[64:]
def swap(x,n):
    y=jnp.stack([x[:,128*q:128*q+128] for q in range(n)],0)
    return jnp.swapaxes(y,0,1)


C = 32


def load_chunk(ref, n):
    return jnp.concatenate([ref[n * C + q] for q in range(C)], 1)


def windows(count, off, R, Z, Y, put, threshold, sw):
    def own(n):
        return jnp.concatenate([R[n * C + q, pl.ds(off, 64), :] for q in range(C)], 1)

    def forth(x, n):
        Z[:, pl.ds(pl.multiple_of(n * C, C), C), :] = swap(smul(x, sw[0]), C)

    def back(n):
        w = own(n)
        return jnp.where(w > 1e29, smul(load_chunk(Y, n), sw[1]), w)

    def first(n, c):
        w = own(n)
        forth(jnp.where(w > 1e29, 0.0, w), n)
        return c

    def shrink(q):
        t = threshold(q)

        def f(n, c):
            u = smul(load_chunk(Z, n), sw[0])
            u = u - jnp.clip(u, -t, t)
            Y[:, pl.ds(pl.multiple_of(n * C, C), C), :] = swap(smul(u, sw[1]), C)
            return c

        lax.fori_loop(0, 64 // C, f, 0, unroll=True)

    def again(n, c):
        forth(back(n), n)
        return c

    def step(q, c):
        shrink(q)
        lax.fori_loop(0, 64 // C, again, 0, unroll=True)
        return c

    def last(n, c):
        put(n, back(n))
        return c

    lax.fori_loop(0, 64 // C, first, 0, unroll=True)
    lax.fori_loop(0, count - 1, step, 0)
    shrink(count - 1)
    lax.fori_loop(0, 64 // C, last, 0, unroll=True)


Q = 32000.0
LN = float(np.log(2.0) / 128.0)
i32 = jnp.int32
i16 = jnp.int16


def parity():
    return lax.rem(lax.axis_index("xl"), 2)


def roll(x, s):
    if isinstance(s, int):
        s %= 128
        if s == 0:
            return x
    return pltpu.roll(x, s, 1)


def at(b, n):
    return pl.ds(pl.multiple_of(b * n, n), n)


def encode(get, dst, n, flagged, un=8):
    def top(b, m):
        x = get(b)
        a = jnp.abs(x)
        if flagged:
            a = jnp.where(x > 1e29, 0.0, a)
        return jnp.maximum(m, a)

    m = lax.fori_loop(0, n, top, jnp.full((16, 128), 1e-30, f32), unroll=un)
    code = jnp.ceil(jnp.log(m) * (1.0 / LN))
    scale = Q * jnp.exp(code * -LN)

    def put(b, c):
        x = get(b)
        q = jnp.round(x * scale)
        if flagged:
            q = jnp.where(x > 1e29, 0.0, jnp.where(q >= 0, q + 1.0, q))
        dst[at(b, 16), :] = q.astype(i32).astype(i16)
        return c

    lax.fori_loop(0, n, put, 0, unroll=un)
    dst[pl.ds(n * 16, 16), :] = code.astype(i32).astype(i16)


def blocks(ref, first=0):
    return lambda b: ref[at(b + first, 16), :]


def scale_of(ref, n):
    return jnp.exp(ref[pl.ds(n * 16, 16), :].astype(i32).astype(f32) * LN) * (1.0 / Q)


def decode(ref, b, scale, flagged=False):
    q = ref[at(b, 16), :].astype(i32).astype(f32)
    if flagged:
        return jnp.where(q == 0, DEAD, (q - jnp.where(q > 0, 1.0, 0.0)) * scale)
    return q * scale


def pair_rows(ref, r, scale):
    return jnp.concatenate([decode(ref, 2 * r + h, scale) for h in (0, 1)], 0)


def spread(parts, q):
    out = parts[3]
    for n in (2, 1, 0):
        out = jnp.where(q == n, parts[n], out)
    return out


def lane_quarter():
    return lax.broadcasted_iota(i32, (32, 128), 1) // 32


def pack_kernel(x_ref, live_ref, flagged, a_out, b_out, sa, sb):
    odd = parity()
    lt = live_ref[...].astype(f32).T
    q = lane_quarter()
    for r in range(8):
        x = []
        for i in (r, r + 8, r + 16, r + 24):
            alive = jnp.broadcast_to(lt[:, i : i + 1], (32, 128)) > 0.5
            flagged[i] = jnp.where(alive, x_ref[i], DEAD)
            x.append(jnp.where(alive, x_ref[i], 0.0))
        sa[r * 32 : r * 32 + 32, :] = spread([roll(v, (32 * n + 32 * (1 - odd)) % 128) for n, v in enumerate(x)], q)
        sb[r * 32 : r * 32 + 32, :] = spread([roll(v, (32 * n + 32 * odd) % 128) for n, v in enumerate(x)], q)
    encode(blocks(sa), a_out, 16, False)
    encode(blocks(sb), b_out, 16, False)


def widen_kernel(own, other, fa, fb, tw, tile, lo, hi):
    odd = parity()
    halo = lane_quarter() == 3 * odd
    for x, f, column in ((own, fa, 32 * odd), (other, fb, 32 - 32 * odd)):
        k = scale_of(f, 16)
        for r in range(8):
            h = pair_rows(f, r, k)
            for n in range(4):
                i = r + 8 * n
                v = x[i]
                h_n = jnp.where(v > 1e29, DEAD, roll(h, (128 - 32 * n + 96 * odd) % 128))
                rows = pl.ds(pl.multiple_of(i * 64 + column, 32), 32)
                tile[rows, :] = jnp.where(halo, h_n, roll(v, 32 + 64 * odd))
    for n in range(4):
        v = tile[n * 512 : n * 512 + 512, :]
        t = tmul(jnp.where(v > 1e29, 0.0, v), tw[0])
        tile[n * 512 : n * 512 + 512, :] = jnp.where(v > 1e29, DEAD, t)
    encode(blocks(tile), lo, 64, True)
    encode(blocks(tile, 64), hi, 64, True)


def edge_kernel(tile, f0, f3, lo, hi, slo, shi):
    for f, base in ((f0, 0), (f3, 48)):
        k = scale_of(f, 64)

        def take(i, c, f=f, k=k, base=base):
            slo[at(base + i, 16), :] = decode(f, 4 * i, k, True)
            shi[at(base + i, 16), :] = decode(f, 4 * i + 3, k, True)
            return c

        lax.fori_loop(0, 16, take, 0, unroll=8)

    def copy(i, c):
        slo[at(16 + i, 16), :] = tile[at(4 * i, 16), :]
        shi[at(16 + i, 16), :] = tile[at(4 * i + 3, 16), :]
        return c

    lax.fori_loop(0, 32, copy, 0, unroll=8)
    encode(blocks(slo), lo, 64, True)
    encode(blocks(shi), hi, 64, True)


def main_kernel(cnt, levels, tile, f0, f3, fa, fb, tj, ti, sw, lo, hi, core, R, acc, Z, Y):
    ka, kb = scale_of(fa, 64), scale_of(fb, 64)

    def sides(i, c):
        R[i, 0:16, :] = decode(fa, i, ka, True)
        R[i, 80:96, :] = decode(fb, i, kb, True)
        return c

    lax.fori_loop(0, 64, sides, 0, unroll=8)
    for f, base in ((f0, 0), (f3, 48)):
        k = scale_of(f, 64)

        def take(i, c, f=f, k=k, base=base):
            for x in range(4):
                R[base + i, 16 + 16 * x : 32 + 16 * x, :] = decode(f, 4 * i + x, k, True)
            return c

        lax.fori_loop(0, 16, take, 0, unroll=4)

    def copy(i, c):
        R[16 + i, 16:80, :] = tile[at(i, 64), :]
        return c

    lax.fori_loop(0, 32, copy, 0, unroll=8)
    position = lax.axis_index("xl")
    odd = lax.rem(position, 2)
    zeros = jnp.zeros((32, 128), f32)

    def window(s, c):
        off = pl.multiple_of(s * 32, 32)

        def put(n, v):
            for q in range(C):
                i = n * C + q
                t = v[:, q * 128 : q * 128 + 128] * (tj[...] * ti[pl.ds(i, 1), :])
                acc[i, pl.ds(off, 32), :] = jnp.where(s > 0, acc[i, pl.ds(off, 32), :], zeros) + t[:32]
                acc[i, pl.ds(off + 32, 32), :] = t[32:]

        count = cnt[0, odd, position - odd + s]
        windows(count, off, R, Z, Y, put, lambda q: levels[q].astype(f32) * 0.001, sw)
        return c

    lax.fori_loop(0, 2, window, 0)
    encode(lambda i: acc[i, 0:16, :], lo, 64, False)
    encode(lambda i: acc[i, 80:96, :], hi, 64, False)

    def give(i, c):
        core[at(i, 64), :] = acc[i, 16:80, :]
        return c

    lax.fori_loop(0, 64, give, 0, unroll=8)


def fold_kernel(core, fa, fb, inner, lo, hi, slo, shi):
    ka, kb = scale_of(fa, 64), scale_of(fb, 64)
    for first, n, dst in ((0, 16, slo), (16, 32, inner), (48, 16, shi)):

        def add(i, c, first=first, dst=dst):
            p = first + i
            v = core[at(p, 64), :]
            dst[at(4 * i, 16), :] = v[:16] + decode(fa, p, ka)
            dst[pl.ds(pl.multiple_of(i * 64 + 16, 16), 32), :] = v[16:48]
            dst[at(4 * i + 3, 16), :] = v[48:] + decode(fb, p, kb)
            return c

        lax.fori_loop(0, n, add, 0, unroll=8)
    encode(blocks(slo), lo, 64, False)
    encode(blocks(shi), hi, 64, False)


def narrow_kernel(inner, fa, fb, tt, tw, own, other, a_out, b_out, sa, sb, sv):
    odd = parity()
    q = lane_quarter()
    for f, base in ((fa, 0), (fb, 64)):
        k = scale_of(f, 64)
        for n in range(2):
            rows = [inner[at(base + 32 * n + b, 16), :] + decode(f, 32 * n + b, k) for b in range(32)]
            at_rows = (base + 32 * n) * 16
            sv[at_rows : at_rows + 512, :] = tmul(jnp.concatenate(rows, 0), tw[1]) * tt[0:1, :]
    for dst, s, column in ((own, sa, odd), (other, sb, 1 - odd)):
        for r in range(8):
            parts = []
            for n in range(4):
                i = r + 8 * n
                v = sv[pl.ds(pl.multiple_of(i * 64 + 32 * column, 32), 32), :]
                dst[i] = v
                parts.append(roll(v, (32 * n + 32 * odd) % 128))
            s[r * 32 : r * 32 + 32, :] = spread(parts, q)
    encode(blocks(sa), a_out, 16, False)
    encode(blocks(sb), b_out, 16, False)


def last_kernel(own, other, fa, fb, out):
    odd = parity()
    q = lane_quarter()
    low, high = 3 - 3 * odd, 3 * odd
    ka, kb = scale_of(fa, 16), scale_of(fb, 16)
    for r in range(8):
        a, b = pair_rows(fa, r, ka), pair_rows(fb, r, kb)
        for n in range(4):
            i = r + 8 * n
            v = jnp.where(q == low, roll(a, (224 - 32 * n + 32 * odd) % 128), roll(own[i], (96 + 64 * odd) % 128))
            w = jnp.where(q == high, roll(b, (256 - 32 * n + 96 * odd) % 128), roll(other[i], (32 + 64 * odd) % 128))
            out[i] = v + w


V = pl.BlockSpec(memory_space=pltpu.VMEM)
S = pl.BlockSpec(memory_space=pltpu.SMEM)


def call(kernel, name, mib, outs, scratch, specs, *args):
    shapes = [jax.ShapeDtypeStruct(s, t) for s, t in outs]
    return pl.pallas_call(
        kernel,
        out_shape=shapes,
        in_specs=specs,
        out_specs=[V] * len(outs),
        scratch_shapes=[pltpu.VMEM(s, f32) for s in scratch],
        compiler_params=pltpu.CompilerParams(vmem_limit_bytes=mib * 1024 * 1024),
        name=name,
    )(*args)


def exchange(low, high, axis, step):
    count = lax.axis_size(axis)
    forward = [(i, i + step) for i in range(count - step)]
    backward = [(b, a) for a, b in forward]
    return lax.ppermute(high, axis, forward), lax.ppermute(low, axis, backward)


def swap_pair(x):
    return lax.ppermute(x, "xl", [(i, i ^ 1) for i in range(lax.axis_size("xl"))])


def exchange_time(a, b, outward):
    nx, nt = lax.axis_size("xl"), lax.axis_size("ta")
    straight, cross = [], []
    for x in range(nx):
        for t in range(nt):
            s = t + (1 if (x % 2 == 0) == outward else -1)
            if 0 <= s < nt:
                straight.append((x * nt + t, x * nt + s))
            s = t + (-1 if x % 2 == 0 else 1)
            if 0 <= s < nt:
                cross.append((x * nt + t, (x ^ 1) * nt + s))
    return lax.ppermute(a, ("xl", "ta"), straight), lax.ppermute(b, ("xl", "ta"), cross)


def codes(n):
    return ((n * 16 + 16, 128), i16)


def taper(order):
    return np.sin(np.pi * (np.arange(order) + 0.5) / order) ** 2


TILE = ((32, 32, 128), f32)


def shards(traces, live, counts, levels):
    tw, sw = tables()
    tj = jnp.asarray(np.broadcast_to(taper(64)[:, None], (64, 128)).astype(np.float32))
    tt = jnp.asarray(np.broadcast_to(taper(128)[None, :], (8, 128)).astype(np.float32))
    tw, sw = jnp.asarray(tw), jnp.asarray(sw)
    own, a, b = call(pack_kernel, "pack", 4, [TILE, codes(16), codes(16)], [(256, 128)] * 2, [V] * 2, traces, live)
    fa, fb = exchange_time(a, b, True)
    other = swap_pair(own)
    tile, lo, hi = call(
        widen_kernel, "widen", 6, [((2048, 128), f32), codes(64), codes(64)], [], [V] * 5, own, other, fa, fb, tw
    )
    f0, f3 = exchange(lo, hi, "il", 1)
    lo, hi = call(edge_kernel, "edge", 6, [codes(64)] * 2, [(1024, 128)] * 2, [V] * 3, tile, f0, f3)
    fa, fb = exchange(lo, hi, "xl", 2)
    lo, hi, core = call(
        main_kernel,
        "windows",
        32,
        [codes(64), codes(64), ((4096, 128), f32)],
        [(64, 96, 128), (64, 96, 128), (64, 64, 128), (64, 64, 128)],
        [S, S] + [V] * 8,
        counts.transpose(0, 2, 1),
        levels,
        tile,
        f0,
        f3,
        fa,
        fb,
        tj,
        tj,
        sw,
    )
    fa, fb = exchange(lo, hi, "xl", 2)
    inner, lo, hi = call(
        fold_kernel, "fold", 8, [((2048, 128), f32), codes(64), codes(64)], [(1024, 128)] * 2, [V] * 3, core, fa, fb
    )
    fa, fb = exchange(lo, hi, "il", 1)
    own, other, a, b = call(
        narrow_kernel,
        "narrow",
        8,
        [TILE, TILE, codes(16), codes(16)],
        [(256, 128), (256, 128), (2048, 128)],
        [V] * 5,
        inner,
        fa,
        fb,
        tt,
        tw,
    )
    fa, fb = exchange_time(a, b, False)
    other = swap_pair(other)
    return call(last_kernel, "last", 4, [TILE], [], [V] * 4, own, other, fa, fb)[0]


def solution(mesh):
    placed = (P("il", "xl", "ta"), P("il", "xl"), P("il", None, "ta"), P())
    return jax.shard_map(
        shards, mesh=mesh, in_specs=placed, out_specs=P("il", "xl", "ta"), check_vma=False
    )
```

```python
import jax
import jax.numpy as jnp
import numpy as np
from jax import lax
from jax.experimental import pallas as pl
from jax.experimental.pallas import tpu as pltpu
from jax.sharding import PartitionSpec as P

f32=jnp.float32; bf16=jnp.bfloat16
DEAD=1e30
def dct(n):
    k=np.arange(n)[:,None]; j=np.arange(n)[None,:]
    c=np.sqrt(2.0/n)*np.cos(np.pi*(2*j+1)*k/(2*n)); c[0]*=np.sqrt(0.5); return c
def two(c):
    hi=np.asarray(c,np.float32).astype(jnp.bfloat16); lo=(c-hi.astype(np.float64)).astype(np.float32).astype(jnp.bfloat16)
    return hi,lo
def time_w(c):
    hi,lo=two(c)
    return np.concatenate([np.concatenate([hi,hi],0),np.concatenate([lo,np.zeros_like(lo)],0)],1)
def space_w(c):
    hi,lo=two(c)
    return np.concatenate([np.concatenate([hi,hi],1),np.concatenate([lo,np.zeros_like(lo)],1)],0)
def tables():
    ct=dct(128); cs=dct(64)
    tw=np.stack([time_w(ct.T),time_w(ct)])
    sw=np.stack([space_w(cs),space_w(cs.T)])
    return tw,sw
def split(x):
    hi=x.astype(bf16); return hi,(x-hi.astype(f32)).astype(bf16)
def tmul(x,w):
    hi,lo=split(x)
    y=jnp.dot(jnp.concatenate([hi,lo],1),w,preferred_element_type=f32)
    return y[:,:128]+y[:,128:]
def smul(x,w):
    hi,lo=split(x)
    y=jnp.dot(w,jnp.concatenate([hi,lo],0),preferred_element_type=f32)
    return y[:64]+y[64:]
def swap(x,n):
    y=jnp.stack([x[:,128*q:128*q+128] for q in range(n)],0)
    return jnp.swapaxes(y,0,1)


C = 32


def load_chunk(ref, n):
    return jnp.concatenate([ref[n * C + q] for q in range(C)], 1)


def windows(count, off, R, Z, Y, put, threshold, sw):
    def own(n):
        return jnp.concatenate([R[n * C + q, pl.ds(off, 64), :] for q in range(C)], 1)

    def forth(x, n):
        Z[:, pl.ds(pl.multiple_of(n * C, C), C), :] = swap(smul(x, sw[0]), C)

    def back(n):
        w = own(n)
        return jnp.where(w > 1e29, smul(load_chunk(Y, n), sw[1]), w)

    def first(n, c):
        w = own(n)
        forth(jnp.where(w > 1e29, 0.0, w), n)
        return c

    def shrink(q):
        t = threshold(q)

        def f(n, c):
            u = smul(load_chunk(Z, n), sw[0])
            u = u - jnp.clip(u, -t, t)
            Y[:, pl.ds(pl.multiple_of(n * C, C), C), :] = swap(smul(u, sw[1]), C)
            return c

        lax.fori_loop(0, 64 // C, f, 0, unroll=True)

    def again(n, c):
        forth(back(n), n)
        return c

    def step(q, c):
        shrink(q)
        lax.fori_loop(0, 64 // C, again, 0, unroll=True)
        return c

    def last(n, c):
        put(n, back(n))
        return c

    lax.fori_loop(0, 64 // C, first, 0, unroll=True)
    lax.fori_loop(0, count - 1, step, 0)
    shrink(count - 1)
    lax.fori_loop(0, 64 // C, last, 0, unroll=True)


Q = 32000.0
LN = float(np.log(2.0) / 128.0)
i32 = jnp.int32
i16 = jnp.int16


def parity():
    return lax.rem(lax.axis_index("xl"), 2)


def roll(x, s):
    if isinstance(s, int):
        s %= 128
        if s == 0:
            return x
    return pltpu.roll(x, s, 1)


def at(b, n):
    return pl.ds(pl.multiple_of(b * n, n), n)


def encode(get, dst, n, flagged, un=8):
    def top(b, m):
        x = get(b)
        a = jnp.abs(x)
        if flagged:
            a = jnp.where(x > 1e29, 0.0, a)
        return jnp.maximum(m, a)

    m = lax.fori_loop(0, n, top, jnp.full((16, 128), 1e-30, f32), unroll=un)
    code = jnp.ceil(jnp.log(m) * (1.0 / LN))
    scale = Q * jnp.exp(code * -LN)

    def put(b, c):
        x = get(b)
        q = jnp.round(x * scale)
        if flagged:
            q = jnp.where(x > 1e29, 0.0, jnp.where(q >= 0, q + 1.0, q))
        dst[at(b, 16), :] = q.astype(i32).astype(i16)
        return c

    lax.fori_loop(0, n, put, 0, unroll=un)
    dst[pl.ds(n * 16, 16), :] = code.astype(i32).astype(i16)


def blocks(ref, first=0):
    return lambda b: ref[at(b + first, 16), :]


def scale_of(ref, n):
    return jnp.exp(ref[pl.ds(n * 16, 16), :].astype(i32).astype(f32) * LN) * (1.0 / Q)


def decode(ref, b, scale, flagged=False):
    q = ref[at(b, 16), :].astype(i32).astype(f32)
    if flagged:
        return jnp.where(q == 0, DEAD, (q - jnp.where(q > 0, 1.0, 0.0)) * scale)
    return q * scale


def pair_rows(ref, r, scale):
    return jnp.concatenate([decode(ref, 2 * r + h, scale) for h in (0, 1)], 0)


def spread(parts, q):
    out = parts[3]
    for n in (2, 1, 0):
        out = jnp.where(q == n, parts[n], out)
    return out


def lane_quarter():
    return lax.broadcasted_iota(i32, (32, 128), 1) // 32


def pack_kernel(x_hbm, live_hbm, x_other, live_other, flagged, out, s, x_own, live_own, sem):
    odd = parity()
    copies = [pltpu.make_async_copy(x_hbm, x_own, sem.at[0]), pltpu.make_async_copy(live_hbm, live_own, sem.at[1])]
    for copy in copies:
        copy.start()
    q = lane_quarter()
    for x_ref, live_ref, column in ((x_other, live_other, 1 - odd), (x_own, live_own, odd)):
        if x_ref is x_own:
            for copy in copies:
                copy.wait()
        lt = live_ref[...].astype(f32).T
        for r in range(8):
            x = []
            for i in (r, r + 8, r + 16, r + 24):
                alive = jnp.broadcast_to(lt[:, i : i + 1], (32, 128)) > 0.5
                flagged[32 * column + i] = jnp.where(alive, x_ref[i], DEAD)
                x.append(jnp.where(alive, x_ref[i], 0.0))
            s[pl.ds(pl.multiple_of(256 * column + 32 * r, 32), 32), :] = spread(
                [roll(v, (32 * n + 32 * odd) % 128) for n, v in enumerate(x)], q
            )
    encode(blocks(s), out, 32, False)


def widen_kernel(flagged, f, tw_hbm, tile, lo, hi, tw, sem):
    odd = parity()
    copy = pltpu.make_async_copy(tw_hbm.at[0], tw, sem)
    copy.start()
    halo = lane_quarter() == 3 * odd
    k = scale_of(f, 32)
    for column in (0, 1):
        for r in range(8):
            h = pair_rows(f, 8 * column + r, k)
            for n in range(4):
                i = r + 8 * n
                v = flagged[32 * column + i]
                h_n = jnp.where(v > 1e29, DEAD, roll(h, (128 - 32 * n + 96 * odd) % 128))
                rows = pl.ds(i * 64 + 32 * column, 32)
                tile[rows, :] = jnp.where(halo, h_n, roll(v, 32 + 64 * odd))
    copy.wait()
    for n in range(4):
        v = tile[n * 512 : n * 512 + 512, :]
        t = tmul(jnp.where(v > 1e29, 0.0, v), tw[...])
        tile[n * 512 : n * 512 + 512, :] = jnp.where(v > 1e29, DEAD, t)
    encode(blocks(tile), lo, 64, True)
    encode(blocks(tile, 64), hi, 64, True)


def edge_kernel(tile, f0, f3, lo, hi, slo, shi):
    for f, base in ((f0, 0), (f3, 48)):
        k = scale_of(f, 64)

        def take(i, c, f=f, k=k, base=base):
            slo[at(base + i, 16), :] = decode(f, 4 * i, k, True)
            shi[at(base + i, 16), :] = decode(f, 4 * i + 3, k, True)
            return c

        lax.fori_loop(0, 16, take, 0, unroll=8)

    def copy(i, c):
        slo[at(16 + i, 16), :] = tile[at(4 * i, 16), :]
        shi[at(16 + i, 16), :] = tile[at(4 * i + 3, 16), :]
        return c

    lax.fori_loop(0, 32, copy, 0, unroll=8)
    encode(blocks(slo), lo, 64, True)
    encode(blocks(shi), hi, 64, True)


def main_kernel(cnt, levels, tile, f0, f3, fa, fb, tj, ti, sw, lo, hi, core, R, acc, Z, Y):
    ka, kb = scale_of(fa, 64), scale_of(fb, 64)

    def sides(i, c):
        R[i, 0:16, :] = decode(fa, i, ka, True)
        R[i, 80:96, :] = decode(fb, i, kb, True)
        return c

    lax.fori_loop(0, 64, sides, 0, unroll=8)
    for f, base in ((f0, 0), (f3, 48)):
        k = scale_of(f, 64)

        def take(i, c, f=f, k=k, base=base):
            for x in range(4):
                R[base + i, 16 + 16 * x : 32 + 16 * x, :] = decode(f, 4 * i + x, k, True)
            return c

        lax.fori_loop(0, 16, take, 0, unroll=4)

    def copy(i, c):
        R[16 + i, 16:80, :] = tile[at(i, 64), :]
        return c

    lax.fori_loop(0, 32, copy, 0, unroll=8)
    position = lax.axis_index("xl")
    odd = lax.rem(position, 2)
    zeros = jnp.zeros((32, 128), f32)

    def window(s, c):
        off = pl.multiple_of(s * 32, 32)

        def put(n, v):
            for q in range(C):
                i = n * C + q
                t = v[:, q * 128 : q * 128 + 128] * (tj[...] * ti[pl.ds(i, 1), :])
                acc[i, pl.ds(off, 32), :] = jnp.where(s > 0, acc[i, pl.ds(off, 32), :], zeros) + t[:32]
                acc[i, pl.ds(off + 32, 32), :] = t[32:]

        count = cnt[0, odd, position - odd + s]
        windows(count, off, R, Z, Y, put, lambda q: levels[q].astype(f32) * 0.001, sw)
        return c

    lax.fori_loop(0, 2, window, 0)
    encode(lambda i: acc[i, 0:16, :], lo, 64, False)
    encode(lambda i: acc[i, 80:96, :], hi, 64, False)

    def give(i, c):
        core[at(i, 64), :] = acc[i, 16:80, :]
        return c

    lax.fori_loop(0, 64, give, 0, unroll=8)


def fold_kernel(core, fa, fb, inner, lo, hi, slo, shi):
    ka, kb = scale_of(fa, 64), scale_of(fb, 64)
    for first, n, dst in ((0, 16, slo), (16, 32, inner), (48, 16, shi)):

        def add(i, c, first=first, dst=dst):
            p = first + i
            v = core[at(p, 64), :]
            dst[at(4 * i, 16), :] = v[:16] + decode(fa, p, ka)
            dst[pl.ds(pl.multiple_of(i * 64 + 16, 16), 32), :] = v[16:48]
            dst[at(4 * i + 3, 16), :] = v[48:] + decode(fb, p, kb)
            return c

        lax.fori_loop(0, n, add, 0, unroll=8)
    encode(blocks(slo), lo, 64, False)
    encode(blocks(shi), hi, 64, False)


def narrow_kernel(inner, fa, fb, tt_hbm, tw_hbm, own, other, out, s, sv, tt, tw, sem):
    odd = parity()
    copies = [pltpu.make_async_copy(tw_hbm.at[1], tw, sem.at[0]), pltpu.make_async_copy(tt_hbm, tt, sem.at[1])]
    for copy in copies:
        copy.start()
    q = lane_quarter()
    for f, base in ((fa, 0), (fb, 64)):
        k = scale_of(f, 64)
        for n in range(2):
            for b in range(32):
                sv[at(base + 32 * n + b, 16), :] = inner[at(base + 32 * n + b, 16), :] + decode(f, 32 * n + b, k)
    for copy in copies:
        copy.wait()
    for n in range(4):
        sv[n * 512 : n * 512 + 512, :] = tmul(sv[n * 512 : n * 512 + 512, :], tw[...]) * tt[0:1, :]
    for column in (0, 1):
        for r in range(8):
            parts = []
            for n in range(4):
                v = sv[pl.ds((r + 8 * n) * 64 + 32 * column, 32), :]
                parts.append(roll(v, (32 * n + 32 * odd) % 128))
            s[pl.ds(256 * column + 32 * r, 32), :] = spread(parts, q)
    for i in range(32):
        own[i] = sv[pl.ds(pl.multiple_of(i * 64 + 32 * odd, 32), 32), :]
        other[i] = sv[pl.ds(pl.multiple_of(i * 64 + 32 - 32 * odd, 32), 32), :]
    encode(blocks(s), out, 32, False)


def last_kernel(own, other, fa, fb, out):
    odd = parity()
    q = lane_quarter()
    low, high = 3 - 3 * odd, 3 * odd
    ka, kb = scale_of(fa, 32), scale_of(fb, 32)
    for r in range(8):
        a, b = pair_rows(fa, 8 * odd + r, ka), pair_rows(fb, 8 * odd + r, kb)
        for n in range(4):
            i = r + 8 * n
            v = jnp.where(q == low, roll(a, (224 - 32 * n + 32 * odd) % 128), roll(own[i], (96 + 64 * odd) % 128))
            w = jnp.where(q == high, roll(b, (256 - 32 * n + 96 * odd) % 128), roll(other[i], (32 + 64 * odd) % 128))
            out[i] = v + w


V = pl.BlockSpec(memory_space=pltpu.VMEM)
S = pl.BlockSpec(memory_space=pltpu.SMEM)
H = pl.BlockSpec(memory_space=pltpu.HBM)
SEM = pltpu.SemaphoreType.DMA


def call(kernel, name, mib, outs, scratch, specs, *args):
    shapes = [jax.ShapeDtypeStruct(s, t) for s, t in outs]
    args = [pltpu.with_memory_space_constraint(a, pltpu.HBM) if p is H else a for a, p in zip(args, specs)]
    return pl.pallas_call(
        kernel,
        out_shape=shapes,
        in_specs=specs,
        out_specs=[V] * len(outs),
        scratch_shapes=[pltpu.VMEM(s, f32) if isinstance(s, tuple) else s for s in scratch],
        compiler_params=pltpu.CompilerParams(vmem_limit_bytes=mib * 1024 * 1024),
        name=name,
    )(*args)


def exchange(low, high, axis, step):
    count = lax.axis_size(axis)
    forward = [(i, i + step) for i in range(count - step)]
    backward = [(b, a) for a, b in forward]
    return lax.ppermute(high, axis, forward), lax.ppermute(low, axis, backward)


def swap_pair(x):
    return lax.ppermute(x, "xl", [(i, i ^ 1) for i in range(lax.axis_size("xl"))])


def exchange_time(x):
    nx, nt = lax.axis_size("xl"), lax.axis_size("ta")
    pairs = []
    for x_at in range(nx):
        for t in range(nt):
            other = t + (-1 if x_at % 2 == 0 else 1)
            if 0 <= other < nt:
                pairs.append((x_at * nt + t, (x_at ^ 1) * nt + other))
    return lax.ppermute(x, ("xl", "ta"), pairs)


def codes(n):
    return ((n * 16 + 16, 128), i16)


def taper(order):
    return np.sin(np.pi * (np.arange(order) + 0.5) / order) ** 2


TILE = ((32, 32, 128), f32)


def shards(traces, live, counts, levels):
    tw, sw = tables()
    tj = jnp.asarray(np.broadcast_to(taper(64)[:, None], (64, 128)).astype(np.float32))
    tt = jnp.asarray(np.broadcast_to(taper(128)[None, :], (8, 128)).astype(np.float32))
    tw, sw = jnp.asarray(tw), jnp.asarray(sw)
    traces_other, live_other = swap_pair(traces), swap_pair(live)
    flagged, msg = call(
        pack_kernel,
        "pack",
        6,
        [((64, 32, 128), f32), codes(32)],
        [(512, 128), (32, 32, 128), pltpu.VMEM((32, 32), i32), SEM((2,))],
        [H, H, V, V],
        traces,
        live,
        traces_other,
        live_other,
    )
    msg = exchange_time(msg)
    tile, lo, hi = call(
        widen_kernel,
        "widen",
        6,
        [((2048, 128), f32), codes(64), codes(64)],
        [pltpu.VMEM((256, 256), bf16), SEM],
        [V, V, H],
        flagged,
        msg,
        tw,
    )
    f0, f3 = exchange(lo, hi, "il", 1)
    lo, hi = call(edge_kernel, "edge", 6, [codes(64)] * 2, [(1024, 128)] * 2, [V] * 3, tile, f0, f3)
    fa, fb = exchange(lo, hi, "xl", 2)
    lo, hi, core = call(
        main_kernel,
        "windows",
        32,
        [codes(64), codes(64), ((4096, 128), f32)],
        [(64, 96, 128), (64, 96, 128), (64, 64, 128), (64, 64, 128)],
        [S, S] + [V] * 8,
        counts.transpose(0, 2, 1),
        levels,
        tile,
        f0,
        f3,
        fa,
        fb,
        tj,
        tj,
        sw,
    )
    fa, fb = exchange(lo, hi, "xl", 2)
    inner, lo, hi = call(
        fold_kernel, "fold", 8, [((2048, 128), f32), codes(64), codes(64)], [(1024, 128)] * 2, [V] * 3, core, fa, fb
    )
    fa, fb = exchange(lo, hi, "il", 1)
    own, other, msg = call(
        narrow_kernel,
        "narrow",
        8,
        [TILE, TILE, codes(32)],
        [(512, 128), (2048, 128), (8, 128), pltpu.VMEM((256, 256), bf16), SEM((2,))],
        [V, V, V, H, H],
        inner,
        fa,
        fb,
        tt,
        tw,
    )
    msg = exchange_time(msg)
    other, msg_other = swap_pair(other), swap_pair(msg)
    return call(last_kernel, "last", 4, [TILE], [], [V] * 4, own, other, msg_other, msg)[0]


def solution(mesh):
    placed = (P("il", "xl", "ta"), P("il", "xl"), P("il", None, "ta"), P())
    return jax.shard_map(
        shards, mesh=mesh, in_specs=placed, out_specs=P("il", "xl", "ta"), check_vma=False
    )
```

```python
import jax
import jax.numpy as jnp
import numpy as np
from jax import lax
from jax.experimental import pallas as pl
from jax.experimental.pallas import tpu as pltpu
from jax.sharding import PartitionSpec as P

f32=jnp.float32; bf16=jnp.bfloat16
DEAD=1e30
def dct(n):
    k=np.arange(n)[:,None]; j=np.arange(n)[None,:]
    c=np.sqrt(2.0/n)*np.cos(np.pi*(2*j+1)*k/(2*n)); c[0]*=np.sqrt(0.5); return c
def two(c):
    hi=np.asarray(c,np.float32).astype(jnp.bfloat16); lo=(c-hi.astype(np.float64)).astype(np.float32).astype(jnp.bfloat16)
    return hi,lo
def time_w(c):
    hi,lo=two(c)
    return np.concatenate([np.concatenate([hi,hi],0),np.concatenate([lo,np.zeros_like(lo)],0)],1)
def space_w(c):
    hi,lo=two(c)
    return np.concatenate([np.concatenate([hi,hi],1),np.concatenate([lo,np.zeros_like(lo)],1)],0)
def tables():
    ct=dct(128); cs=dct(64)
    tw=np.stack([time_w(ct.T),time_w(ct)])
    sw=np.stack([space_w(cs),space_w(cs.T)])
    return tw,sw
def split(x):
    hi=x.astype(bf16); return hi,(x-hi.astype(f32)).astype(bf16)
def tmul(x,w):
    hi,lo=split(x)
    y=jnp.dot(jnp.concatenate([hi,lo],1),w,preferred_element_type=f32)
    return y[:,:128]+y[:,128:]
def smul(x,w):
    hi,lo=split(x)
    y=jnp.dot(w,jnp.concatenate([hi,lo],0),preferred_element_type=f32)
    return y[:64]+y[64:]
def swap(x,n):
    y=jnp.stack([x[:,128*q:128*q+128] for q in range(n)],0)
    return jnp.swapaxes(y,0,1)


C = 32


def load_chunk(ref, n):
    return jnp.concatenate([ref[n * C + q] for q in range(C)], 1)


def windows(count, off, R, Z, Y, put, threshold, sw):
    def own(n):
        return jnp.concatenate([R[n * C + q, pl.ds(off, 64), :] for q in range(C)], 1)

    def forth(x, n):
        Z[:, pl.ds(pl.multiple_of(n * C, C), C), :] = swap(smul(x, sw[0]), C)

    def back(n):
        w = own(n)
        return jnp.where(w > 1e29, smul(load_chunk(Y, n), sw[1]), w)

    def first(n, c):
        w = own(n)
        forth(jnp.where(w > 1e29, 0.0, w), n)
        return c

    def shrink(q):
        t = threshold(q)

        def f(n, c):
            u = smul(load_chunk(Z, n), sw[0])
            u = u - jnp.clip(u, -t, t)
            Y[:, pl.ds(pl.multiple_of(n * C, C), C), :] = swap(smul(u, sw[1]), C)
            return c

        lax.fori_loop(0, 64 // C, f, 0, unroll=True)

    def again(n, c):
        forth(back(n), n)
        return c

    def step(q, c):
        shrink(q)
        lax.fori_loop(0, 64 // C, again, 0, unroll=True)
        return c

    def last(n, c):
        put(n, back(n))
        return c

    lax.fori_loop(0, 64 // C, first, 0, unroll=True)
    lax.fori_loop(0, count - 1, step, 0)
    shrink(count - 1)
    lax.fori_loop(0, 64 // C, last, 0, unroll=True)


Q = 32000.0
LN = float(np.log(2.0) / 128.0)
i32 = jnp.int32
i16 = jnp.int16


def parity():
    return lax.rem(lax.axis_index("xl"), 2)


def roll(x, s):
    if isinstance(s, int):
        s %= 128
        if s == 0:
            return x
    return pltpu.roll(x, s, 1)


def at(b, n):
    return pl.ds(pl.multiple_of(b * n, n), n)


def encode(get, dst, n, flagged, un=8):
    def top(b, m):
        x = get(b)
        a = jnp.abs(x)
        if flagged:
            a = jnp.where(x > 1e29, 0.0, a)
        return jnp.maximum(m, a)

    m = lax.fori_loop(0, n, top, jnp.full((16, 128), 1e-30, f32), unroll=un)
    code = jnp.ceil(jnp.log(m) * (1.0 / LN))
    scale = Q * jnp.exp(code * -LN)

    def put(b, c):
        x = get(b)
        q = jnp.round(x * scale)
        if flagged:
            q = jnp.where(x > 1e29, 0.0, jnp.where(q >= 0, q + 1.0, q))
        dst[at(b, 16), :] = q.astype(i32).astype(i16)
        return c

    lax.fori_loop(0, n, put, 0, unroll=un)
    dst[pl.ds(n * 16, 16), :] = code.astype(i32).astype(i16)


def blocks(ref, first=0):
    return lambda b: ref[at(b + first, 16), :]


def scale_of(ref, n):
    return jnp.exp(ref[pl.ds(n * 16, 16), :].astype(i32).astype(f32) * LN) * (1.0 / Q)


def decode(ref, b, scale, flagged=False):
    q = ref[at(b, 16), :].astype(i32).astype(f32)
    if flagged:
        return jnp.where(q == 0, DEAD, (q - jnp.where(q > 0, 1.0, 0.0)) * scale)
    return q * scale


def pair_rows(ref, r, scale):
    return jnp.concatenate([decode(ref, 2 * r + h, scale) for h in (0, 1)], 0)


def spread(parts, q):
    out = parts[3]
    for n in (2, 1, 0):
        out = jnp.where(q == n, parts[n], out)
    return out


def lane_quarter():
    return lax.broadcasted_iota(i32, (32, 128), 1) // 32


def load_kernel(x_hbm, live_hbm, tw_hbm, tt_hbm, own, tw, tt, x, live, sem):
    pairs = ((live_hbm, live), (x_hbm, x), (tw_hbm, tw), (tt_hbm, tt))
    copies = [pltpu.make_async_copy(a, b, sem.at[n]) for n, (a, b) in enumerate(pairs)]
    for copy in copies:
        copy.start()
    copies[0].wait()
    copies[1].wait()
    lt = live[...].astype(f32).T
    for i in range(32):
        own[i] = jnp.where(jnp.broadcast_to(lt[:, i : i + 1], (32, 128)) > 0.5, x[i], DEAD)
    copies[2].wait()
    copies[3].wait()


def pack_kernel(own, x_other, live_other, flagged, out, s):
    odd = parity()
    q = lane_quarter()
    lt = live_other[...].astype(f32).T
    for mine in (True, False):
        column = odd if mine else 1 - odd
        for r in range(8):
            x = []
            for i in (r, r + 8, r + 16, r + 24):
                if mine:
                    v = own[i]
                else:
                    alive = jnp.broadcast_to(lt[:, i : i + 1], (32, 128)) > 0.5
                    v = jnp.where(alive, x_other[i], DEAD)
                flagged[32 * column + i] = v
                x.append(jnp.where(v > 1e29, 0.0, v))
            s[pl.ds(pl.multiple_of(256 * column + 32 * r, 32), 32), :] = spread(
                [roll(v, (32 * n + 32 * odd) % 128) for n, v in enumerate(x)], q
            )
    encode(blocks(s), out, 32, False)


def widen_kernel(flagged, f, tw, tile, lo, hi):
    odd = parity()
    halo = lane_quarter() == 3 * odd
    k = scale_of(f, 32)
    for column in (0, 1):
        for r in range(8):
            h = pair_rows(f, 8 * column + r, k)
            for n in range(4):
                i = r + 8 * n
                v = flagged[32 * column + i]
                h_n = jnp.where(v > 1e29, DEAD, roll(h, (128 - 32 * n + 96 * odd) % 128))
                rows = pl.ds(i * 64 + 32 * column, 32)
                tile[rows, :] = jnp.where(halo, h_n, roll(v, 32 + 64 * odd))
    for n in range(4):
        v = tile[n * 512 : n * 512 + 512, :]
        t = tmul(jnp.where(v > 1e29, 0.0, v), tw[0])
        tile[n * 512 : n * 512 + 512, :] = jnp.where(v > 1e29, DEAD, t)
    encode(blocks(tile), lo, 64, True)
    encode(blocks(tile, 64), hi, 64, True)


def edge_kernel(tile, f0, f3, lo, hi, slo, shi):
    for f, base in ((f0, 0), (f3, 48)):
        k = scale_of(f, 64)

        def take(i, c, f=f, k=k, base=base):
            slo[at(base + i, 16), :] = decode(f, 4 * i, k, True)
            shi[at(base + i, 16), :] = decode(f, 4 * i + 3, k, True)
            return c

        lax.fori_loop(0, 16, take, 0, unroll=8)

    def copy(i, c):
        slo[at(16 + i, 16), :] = tile[at(4 * i, 16), :]
        shi[at(16 + i, 16), :] = tile[at(4 * i + 3, 16), :]
        return c

    lax.fori_loop(0, 32, copy, 0, unroll=8)
    encode(blocks(slo), lo, 64, True)
    encode(blocks(shi), hi, 64, True)


def main_kernel(cnt, levels, tile, f0, f3, fa, fb, tj, ti, sw, lo, hi, core, R, acc, Z, Y):
    ka, kb = scale_of(fa, 64), scale_of(fb, 64)

    def sides(i, c):
        R[i, 0:16, :] = decode(fa, i, ka, True)
        R[i, 80:96, :] = decode(fb, i, kb, True)
        return c

    lax.fori_loop(0, 64, sides, 0, unroll=8)
    for f, base in ((f0, 0), (f3, 48)):
        k = scale_of(f, 64)

        def take(i, c, f=f, k=k, base=base):
            for x in range(4):
                R[base + i, 16 + 16 * x : 32 + 16 * x, :] = decode(f, 4 * i + x, k, True)
            return c

        lax.fori_loop(0, 16, take, 0, unroll=4)

    def copy(i, c):
        R[16 + i, 16:80, :] = tile[at(i, 64), :]
        return c

    lax.fori_loop(0, 32, copy, 0, unroll=8)
    position = lax.axis_index("xl")
    odd = lax.rem(position, 2)
    zeros = jnp.zeros((32, 128), f32)

    def window(s, c):
        off = pl.multiple_of(s * 32, 32)

        def put(n, v):
            for q in range(C):
                i = n * C + q
                t = v[:, q * 128 : q * 128 + 128] * (tj[...] * ti[pl.ds(i, 1), :])
                acc[i, pl.ds(off, 32), :] = jnp.where(s > 0, acc[i, pl.ds(off, 32), :], zeros) + t[:32]
                acc[i, pl.ds(off + 32, 32), :] = t[32:]

        count = cnt[0, odd, position - odd + s]
        windows(count, off, R, Z, Y, put, lambda q: levels[q].astype(f32) * 0.001, sw)
        return c

    lax.fori_loop(0, 2, window, 0)
    encode(lambda i: acc[i, 0:16, :], lo, 64, False)
    encode(lambda i: acc[i, 80:96, :], hi, 64, False)

    def give(i, c):
        core[at(i, 64), :] = acc[i, 16:80, :]
        return c

    lax.fori_loop(0, 64, give, 0, unroll=8)


def fold_kernel(core, fa, fb, inner, lo, hi, slo, shi):
    ka, kb = scale_of(fa, 64), scale_of(fb, 64)
    for first, n, dst in ((0, 16, slo), (16, 32, inner), (48, 16, shi)):

        def add(i, c, first=first, dst=dst):
            p = first + i
            v = core[at(p, 64), :]
            dst[at(4 * i, 16), :] = v[:16] + decode(fa, p, ka)
            dst[pl.ds(pl.multiple_of(i * 64 + 16, 16), 32), :] = v[16:48]
            dst[at(4 * i + 3, 16), :] = v[48:] + decode(fb, p, kb)
            return c

        lax.fori_loop(0, n, add, 0, unroll=8)
    encode(blocks(slo), lo, 64, False)
    encode(blocks(shi), hi, 64, False)


def narrow_kernel(inner, fa, fb, tt, tw, own, other, out, s, sv):
    odd = parity()
    q = lane_quarter()
    for f, base in ((fa, 0), (fb, 64)):
        k = scale_of(f, 64)
        for n in range(2):
            for b in range(32):
                sv[at(base + 32 * n + b, 16), :] = inner[at(base + 32 * n + b, 16), :] + decode(f, 32 * n + b, k)
    for n in range(4):
        sv[n * 512 : n * 512 + 512, :] = tmul(sv[n * 512 : n * 512 + 512, :], tw[1]) * tt[0:1, :]
    for column in (0, 1):
        for r in range(8):
            parts = []
            for n in range(4):
                v = sv[pl.ds((r + 8 * n) * 64 + 32 * column, 32), :]
                parts.append(roll(v, (32 * n + 32 * odd) % 128))
            s[pl.ds(256 * column + 32 * r, 32), :] = spread(parts, q)
    for i in range(32):
        own[i] = sv[pl.ds(pl.multiple_of(i * 64 + 32 * odd, 32), 32), :]
        other[i] = sv[pl.ds(pl.multiple_of(i * 64 + 32 - 32 * odd, 32), 32), :]
    encode(blocks(s), out, 32, False)


def last_kernel(own, other, fa, fb, out):
    odd = parity()
    q = lane_quarter()
    low, high = 3 - 3 * odd, 3 * odd
    ka, kb = scale_of(fa, 32), scale_of(fb, 32)
    for r in range(8):
        a, b = pair_rows(fa, 8 * odd + r, ka), pair_rows(fb, 8 * odd + r, kb)
        for n in range(4):
            i = r + 8 * n
            v = jnp.where(q == low, roll(a, (224 - 32 * n + 32 * odd) % 128), roll(own[i], (96 + 64 * odd) % 128))
            w = jnp.where(q == high, roll(b, (256 - 32 * n + 96 * odd) % 128), roll(other[i], (32 + 64 * odd) % 128))
            out[i] = v + w


V = pl.BlockSpec(memory_space=pltpu.VMEM)
S = pl.BlockSpec(memory_space=pltpu.SMEM)
H = pl.BlockSpec(memory_space=pltpu.HBM)
SEM = pltpu.SemaphoreType.DMA


def call(kernel, name, mib, outs, scratch, specs, *args, cost=None):
    shapes = [jax.ShapeDtypeStruct(s, t) for s, t in outs]
    args = [pltpu.with_memory_space_constraint(a, pltpu.HBM) if p is H else a for a, p in zip(args, specs)]
    return pl.pallas_call(
        kernel,
        out_shape=shapes,
        in_specs=specs,
        out_specs=[V] * len(outs),
        scratch_shapes=[pltpu.VMEM(s, f32) if isinstance(s, tuple) else s for s in scratch],
        compiler_params=pltpu.CompilerParams(vmem_limit_bytes=mib * 1024 * 1024),
        name=name,
        cost_estimate=cost,
    )(*args)


def exchange(low, high, axis, step):
    count = lax.axis_size(axis)
    forward = [(i, i + step) for i in range(count - step)]
    backward = [(b, a) for a, b in forward]
    return lax.ppermute(high, axis, forward), lax.ppermute(low, axis, backward)


def swap_pair(x):
    return lax.ppermute(x, "xl", [(i, i ^ 1) for i in range(lax.axis_size("xl"))])


def exchange_time(x):
    nx, nt = lax.axis_size("xl"), lax.axis_size("ta")
    pairs = []
    for x_at in range(nx):
        for t in range(nt):
            other = t + (-1 if x_at % 2 == 0 else 1)
            if 0 <= other < nt:
                pairs.append((x_at * nt + t, (x_at ^ 1) * nt + other))
    return lax.ppermute(x, ("xl", "ta"), pairs)


def codes(n):
    return ((n * 16 + 16, 128), i16)


def taper(order):
    return np.sin(np.pi * (np.arange(order) + 0.5) / order) ** 2


TILE = ((32, 32, 128), f32)


def shards(traces, live, counts, levels):
    tw, sw = tables()
    tj = jnp.asarray(np.broadcast_to(taper(64)[:, None], (64, 128)).astype(np.float32))
    tt = jnp.asarray(np.broadcast_to(taper(128)[None, :], (8, 128)).astype(np.float32))
    tw, sw = jnp.asarray(tw), jnp.asarray(sw)
    traces_other, live_other = swap_pair(traces), swap_pair(live)
    own, tw, tt = call(
        load_kernel,
        "load",
        4,
        [TILE, ((2, 256, 256), bf16), ((8, 128), f32)],
        [(32, 32, 128), pltpu.VMEM((32, 32), i32), SEM((4,))],
        [H] * 4,
        traces,
        live,
        tw,
        tt,
        cost=pl.CostEstimate(flops=1000000, bytes_accessed=6000000, transcendentals=0),
    )
    flagged, msg = call(
        pack_kernel,
        "pack",
        6,
        [((64, 32, 128), f32), codes(32)],
        [(512, 128)],
        [V] * 3,
        own,
        traces_other,
        live_other,
    )
    msg = exchange_time(msg)
    tile, lo, hi = call(
        widen_kernel,
        "widen",
        6,
        [((2048, 128), f32), codes(64), codes(64)],
        [],
        [V] * 3,
        flagged,
        msg,
        tw,
    )
    f0, f3 = exchange(lo, hi, "il", 1)
    lo, hi = call(edge_kernel, "edge", 6, [codes(64)] * 2, [(1024, 128)] * 2, [V] * 3, tile, f0, f3)
    fa, fb = exchange(lo, hi, "xl", 2)
    lo, hi, core = call(
        main_kernel,
        "windows",
        32,
        [codes(64), codes(64), ((4096, 128), f32)],
        [(64, 96, 128), (64, 96, 128), (64, 64, 128), (64, 64, 128)],
        [S, S] + [V] * 8,
        counts.transpose(0, 2, 1),
        levels,
        tile,
        f0,
        f3,
        fa,
        fb,
        tj,
        tj,
        sw,
    )
    fa, fb = exchange(lo, hi, "xl", 2)
    inner, lo, hi = call(
        fold_kernel, "fold", 8, [((2048, 128), f32), codes(64), codes(64)], [(1024, 128)] * 2, [V] * 3, core, fa, fb
    )
    fa, fb = exchange(lo, hi, "il", 1)
    own, other, msg = call(
        narrow_kernel,
        "narrow",
        8,
        [TILE, TILE, codes(32)],
        [(512, 128), (2048, 128)],
        [V] * 5,
        inner,
        fa,
        fb,
        tt,
        tw,
    )
    msg = exchange_time(msg)
    other, msg_other = swap_pair(other), swap_pair(msg)
    return call(last_kernel, "last", 4, [TILE], [], [V] * 4, own, other, msg_other, msg)[0]


def solution(mesh):
    placed = (P("il", "xl", "ta"), P("il", "xl"), P("il", None, "ta"), P())
    return jax.shard_map(
        shards, mesh=mesh, in_specs=placed, out_specs=P("il", "xl", "ta"), check_vma=False
    )
```

```python
import jax
import jax.numpy as jnp
import numpy as np
from jax import lax
from jax.experimental import pallas as pl
from jax.experimental.pallas import tpu as pltpu
from jax.sharding import PartitionSpec as P

f32=jnp.float32; bf16=jnp.bfloat16
DEAD=1e30
def dct(n):
    k=np.arange(n)[:,None]; j=np.arange(n)[None,:]
    c=np.sqrt(2.0/n)*np.cos(np.pi*(2*j+1)*k/(2*n)); c[0]*=np.sqrt(0.5); return c
def two(c):
    hi=np.asarray(c,np.float32).astype(jnp.bfloat16); lo=(c-hi.astype(np.float64)).astype(np.float32).astype(jnp.bfloat16)
    return hi,lo
def time_w(c):
    hi,lo=two(c)
    return np.concatenate([np.concatenate([hi,hi],0),np.concatenate([lo,np.zeros_like(lo)],0)],1)
def space_w(c):
    hi,lo=two(c)
    return np.concatenate([np.concatenate([hi,hi],1),np.concatenate([lo,np.zeros_like(lo)],1)],0)
def tables():
    ct=dct(128); cs=dct(64)
    tw=np.stack([time_w(ct.T),time_w(ct)])
    sw=np.stack([space_w(cs),space_w(cs.T)])
    return tw,sw
def split(x):
    hi=x.astype(bf16); return hi,(x-hi.astype(f32)).astype(bf16)
def tmul(x,w):
    hi,lo=split(x)
    y=jnp.dot(jnp.concatenate([hi,lo],1),w,preferred_element_type=f32)
    return y[:,:128]+y[:,128:]
def smul(x,w):
    hi,lo=split(x)
    y=jnp.dot(w,jnp.concatenate([hi,lo],0),preferred_element_type=f32)
    return y[:64]+y[64:]
def swap(x,n):
    y=jnp.stack([x[:,128*q:128*q+128] for q in range(n)],0)
    return jnp.swapaxes(y,0,1)


C = 32


def load_chunk(ref, n):
    return jnp.concatenate([ref[n * C + q] for q in range(C)], 1)


def windows(count, off, R, Z, Y, put, threshold, sw):
    def own(n):
        return jnp.concatenate([R[n * C + q, pl.ds(off, 64), :] for q in range(C)], 1)

    def forth(x, n):
        Z[:, pl.ds(pl.multiple_of(n * C, C), C), :] = swap(smul(x, sw[0]), C)

    def back(n):
        w = own(n)
        return jnp.where(w > 1e29, smul(load_chunk(Y, n), sw[1]), w)

    def first(n, c):
        w = own(n)
        forth(jnp.where(w > 1e29, 0.0, w), n)
        return c

    def shrink(q):
        t = threshold(q)

        def f(n, c):
            u = smul(load_chunk(Z, n), sw[0])
            u = u - jnp.clip(u, -t, t)
            Y[:, pl.ds(pl.multiple_of(n * C, C), C), :] = swap(smul(u, sw[1]), C)
            return c

        lax.fori_loop(0, 64 // C, f, 0, unroll=True)

    def again(n, c):
        forth(back(n), n)
        return c

    def step(q, c):
        shrink(q)
        lax.fori_loop(0, 64 // C, again, 0, unroll=True)
        return c

    def last(n, c):
        put(n, back(n))
        return c

    lax.fori_loop(0, 64 // C, first, 0, unroll=True)
    lax.fori_loop(0, count - 1, step, 0)
    shrink(count - 1)
    lax.fori_loop(0, 64 // C, last, 0, unroll=True)


Q = 32000.0
LN = float(np.log(2.0) / 128.0)
i32 = jnp.int32
i16 = jnp.int16


def parity():
    return lax.rem(lax.axis_index("xl"), 2)


def even_place(axis, step=1):
    return 1 - lax.rem(lax.axis_index(axis) // step, 2)


def roll(x, s):
    if isinstance(s, int):
        s %= 128
        if s == 0:
            return x
    return pltpu.roll(x, s, 1)


def at(b, n):
    return pl.ds(pl.multiple_of(b * n, n), n)


def encode(get, dst, n, flagged, un=8):
    def top(b, m):
        x = get(b)
        a = jnp.abs(x)
        if flagged:
            a = jnp.where(x > 1e29, 0.0, a)
        return jnp.maximum(m, a)

    m = lax.fori_loop(0, n, top, jnp.full((16, 128), 1e-30, f32), unroll=un)
    code = jnp.ceil(jnp.log(m) * (1.0 / LN))
    scale = Q * jnp.exp(code * -LN)

    def put(b, c):
        x = get(b)
        q = jnp.round(x * scale)
        if flagged:
            q = jnp.where(x > 1e29, 0.0, jnp.where(q >= 0, q + 1.0, q))
        dst[at(b, 16), :] = q.astype(i32).astype(i16)
        return c

    lax.fori_loop(0, n, put, 0, unroll=un)
    dst[pl.ds(n * 16, 16), :] = code.astype(i32).astype(i16)


def blocks(ref, first=0):
    return lambda b: ref[at(b + first, 16), :]


def scale_of(ref, n):
    return jnp.exp(ref[pl.ds(n * 16, 16), :].astype(i32).astype(f32) * LN) * (1.0 / Q)


def decode(ref, b, scale, flagged=False):
    q = ref[at(b, 16), :].astype(i32).astype(f32)
    if flagged:
        return jnp.where(q == 0, DEAD, (q - jnp.where(q > 0, 1.0, 0.0)) * scale)
    return q * scale


def pair_rows(ref, r, scale):
    return jnp.concatenate([decode(ref, 2 * r + h, scale) for h in (0, 1)], 0)


def spread(parts, q):
    out = parts[3]
    for n in (2, 1, 0):
        out = jnp.where(q == n, parts[n], out)
    return out


def lane_quarter():
    return lax.broadcasted_iota(i32, (32, 128), 1) // 32


def load_kernel(x_hbm, live_hbm, tw_hbm, tt_hbm, own, tw, tt, x, live, sem):
    pairs = ((live_hbm, live), (x_hbm, x), (tw_hbm, tw), (tt_hbm, tt))
    copies = [pltpu.make_async_copy(a, b, sem.at[n]) for n, (a, b) in enumerate(pairs)]
    for copy in copies:
        copy.start()
    copies[0].wait()
    copies[1].wait()
    lt = live[...].astype(f32).T
    for i in range(32):
        own[i] = jnp.where(jnp.broadcast_to(lt[:, i : i + 1], (32, 128)) > 0.5, x[i], DEAD)
    copies[2].wait()
    copies[3].wait()


def pack_kernel(own, x_other, live_other, flagged, out, s):
    odd = parity()
    q = lane_quarter()
    lt = live_other[...].astype(f32).T
    for mine in (True, False):
        column = odd if mine else 1 - odd
        for r in range(8):
            x = []
            for i in (r, r + 8, r + 16, r + 24):
                if mine:
                    v = own[i]
                else:
                    alive = jnp.broadcast_to(lt[:, i : i + 1], (32, 128)) > 0.5
                    v = jnp.where(alive, x_other[i], DEAD)
                flagged[32 * column + i] = v
                x.append(jnp.where(v > 1e29, 0.0, v))
            s[pl.ds(pl.multiple_of(256 * column + 32 * r, 32), 32), :] = spread(
                [roll(v, (32 * n + 32 * odd) % 128) for n, v in enumerate(x)], q
            )
    encode(blocks(s), out, 32, False)


def widen_kernel(flagged, f, tw, tile, lo, hi):
    odd = parity()
    halo = lane_quarter() == 3 * odd
    k = scale_of(f, 32)
    for column in (0, 1):
        for r in range(8):
            h = pair_rows(f, 8 * column + r, k)
            for n in range(4):
                i = r + 8 * n
                v = flagged[32 * column + i]
                h_n = jnp.where(v > 1e29, DEAD, roll(h, (128 - 32 * n + 96 * odd) % 128))
                rows = pl.ds(i * 64 + 32 * column, 32)
                tile[rows, :] = jnp.where(halo, h_n, roll(v, 32 + 64 * odd))
    for n in range(4):
        v = tile[n * 512 : n * 512 + 512, :]
        t = tmul(jnp.where(v > 1e29, 0.0, v), tw[0])
        tile[n * 512 : n * 512 + 512, :] = jnp.where(v > 1e29, DEAD, t)
    even = even_place("il")
    encode(blocks(tile, 64 * even), lo, 64, True)
    encode(blocks(tile, 64 - 64 * even), hi, 64, True)


def edge_kernel(tile, fa, fb, ma, mb, s):
    even = even_place("il")
    for f, base in ((fa, 48 * even), (fb, 48 - 48 * even)):
        k = scale_of(f, 64)

        def take(i, c, f=f, k=k, base=base):
            s[at(base + i, 16), :] = decode(f, 4 * i, k, True)
            s[at(64 + base + i, 16), :] = decode(f, 4 * i + 3, k, True)
            return c

        lax.fori_loop(0, 16, take, 0, unroll=8)

    def copy(i, c):
        s[at(16 + i, 16), :] = tile[at(4 * i, 16), :]
        s[at(80 + i, 16), :] = tile[at(4 * i + 3, 16), :]
        return c

    lax.fori_loop(0, 32, copy, 0, unroll=8)
    even = even_place("xl", 2)
    encode(blocks(s, 64 * even), ma, 64, True)
    encode(blocks(s, 64 - 64 * even), mb, 64, True)


def main_kernel(cnt, levels, tile, f0, f3, fa, fb, tj, ti, sw, lo, hi, core, R, acc, Z, Y):
    even = even_place("xl", 2)
    for f, column in ((fa, 80 * even), (fb, 80 - 80 * even)):
        rim = pl.ds(pl.multiple_of(column, 16), 16)
        k = scale_of(f, 64)

        def side(i, c, f=f, k=k, rim=rim):
            R[i, rim, :] = decode(f, i, k, True)
            return c

        lax.fori_loop(0, 64, side, 0, unroll=8)
    il_even = even_place("il")
    for f, base in ((f0, 48 * il_even), (f3, 48 - 48 * il_even)):
        k = scale_of(f, 64)

        def take(i, c, f=f, k=k, base=base):
            for x in range(4):
                R[base + i, 16 + 16 * x : 32 + 16 * x, :] = decode(f, 4 * i + x, k, True)
            return c

        lax.fori_loop(0, 16, take, 0, unroll=4)

    def copy(i, c):
        R[16 + i, 16:80, :] = tile[at(i, 64), :]
        return c

    lax.fori_loop(0, 32, copy, 0, unroll=8)
    position = lax.axis_index("xl")
    odd = lax.rem(position, 2)
    zeros = jnp.zeros((32, 128), f32)

    def window(s, c):
        off = pl.multiple_of(s * 32, 32)

        def put(n, v):
            for q in range(C):
                i = n * C + q
                t = v[:, q * 128 : q * 128 + 128] * (tj[...] * ti[pl.ds(i, 1), :])
                acc[i, pl.ds(off, 32), :] = jnp.where(s > 0, acc[i, pl.ds(off, 32), :], zeros) + t[:32]
                acc[i, pl.ds(off + 32, 32), :] = t[32:]

        count = cnt[0, odd, position - odd + s]
        windows(count, off, R, Z, Y, put, lambda q: levels[q].astype(f32) * 0.001, sw)
        return c

    lax.fori_loop(0, 2, window, 0)
    for dst, column in ((lo, 80 * even), (hi, 80 - 80 * even)):
        rim = pl.ds(pl.multiple_of(column, 16), 16)
        encode(lambda i, rim=rim: acc[i, rim, :], dst, 64, False)

    def give(i, c):
        core[at(i, 64), :] = acc[i, 16:80, :]
        return c

    lax.fori_loop(0, 64, give, 0, unroll=8)


def fold_kernel(core, fa, fb, inner, ma, mb, s):
    even = even_place("xl", 2) > 0
    ka, kb = scale_of(fa, 64), scale_of(fb, 64)
    for first, n, dst, base in ((0, 16, s, 0), (16, 32, inner, 0), (48, 16, s, 16)):

        def add(i, c, first=first, dst=dst, base=base):
            p = first + i
            v = core[at(p, 64), :]
            a, b = decode(fa, p, ka), decode(fb, p, kb)
            r = base + i
            dst[at(4 * r, 16), :] = v[:16] + jnp.where(even, b, a)
            dst[pl.ds(pl.multiple_of(r * 64 + 16, 16), 32), :] = v[16:48]
            dst[at(4 * r + 3, 16), :] = v[48:] + jnp.where(even, a, b)
            return c

        lax.fori_loop(0, n, add, 0, unroll=8)
    il_even = even_place("il")
    encode(blocks(s, 64 * il_even), ma, 64, False)
    encode(blocks(s, 64 - 64 * il_even), mb, 64, False)


def narrow_kernel(inner, fa, fb, tt, tw, own, other, out, s, sv):
    odd = parity()
    q = lane_quarter()
    even = even_place("il")
    for f, base in ((fa, 64 * even), (fb, 64 - 64 * even)):
        k = scale_of(f, 64)
        for b in range(64):
            sv[at(base + b, 16), :] = inner[at(base + b, 16), :] + decode(f, b, k)
    for n in range(4):
        sv[n * 512 : n * 512 + 512, :] = tmul(sv[n * 512 : n * 512 + 512, :], tw[1]) * tt[0:1, :]
    for column in (0, 1):
        for r in range(8):
            parts = []
            for n in range(4):
                v = sv[pl.ds((r + 8 * n) * 64 + 32 * column, 32), :]
                parts.append(roll(v, (32 * n + 32 * odd) % 128))
            s[pl.ds(256 * column + 32 * r, 32), :] = spread(parts, q)
    for i in range(32):
        own[i] = sv[pl.ds(pl.multiple_of(i * 64 + 32 * odd, 32), 32), :]
        other[i] = sv[pl.ds(pl.multiple_of(i * 64 + 32 - 32 * odd, 32), 32), :]
    encode(blocks(s), out, 32, False)


def last_kernel(own, other, fa, fb, out):
    odd = parity()
    q = lane_quarter()
    low, high = 3 - 3 * odd, 3 * odd
    ka, kb = scale_of(fa, 32), scale_of(fb, 32)
    for r in range(8):
        a, b = pair_rows(fa, 8 * odd + r, ka), pair_rows(fb, 8 * odd + r, kb)
        for n in range(4):
            i = r + 8 * n
            v = jnp.where(q == low, roll(a, (224 - 32 * n + 32 * odd) % 128), roll(own[i], (96 + 64 * odd) % 128))
            w = jnp.where(q == high, roll(b, (256 - 32 * n + 96 * odd) % 128), roll(other[i], (32 + 64 * odd) % 128))
            out[i] = v + w


V = pl.BlockSpec(memory_space=pltpu.VMEM)
S = pl.BlockSpec(memory_space=pltpu.SMEM)
H = pl.BlockSpec(memory_space=pltpu.HBM)
SEM = pltpu.SemaphoreType.DMA


def call(kernel, name, mib, outs, scratch, specs, *args, cost=None):
    shapes = [jax.ShapeDtypeStruct(s, t) for s, t in outs]
    args = [pltpu.with_memory_space_constraint(a, pltpu.HBM) if p is H else a for a, p in zip(args, specs)]
    return pl.pallas_call(
        kernel,
        out_shape=shapes,
        in_specs=specs,
        out_specs=[V] * len(outs),
        scratch_shapes=[pltpu.VMEM(s, f32) if isinstance(s, tuple) else s for s in scratch],
        compiler_params=pltpu.CompilerParams(vmem_limit_bytes=mib * 1024 * 1024),
        name=name,
        cost_estimate=cost,
    )(*args)


def exchange(first, second, axis, step):
    count = lax.axis_size(axis)
    rounds = []
    for start in (0, step):
        up = [(i, i + step) for i in range(count - step) if i // step % 2 == start // step]
        rounds.append(up + [(b, a) for a, b in up])
    return lax.ppermute(first, axis, rounds[0]), lax.ppermute(second, axis, rounds[1])


def swap_pair(x):
    return lax.ppermute(x, "xl", [(i, i ^ 1) for i in range(lax.axis_size("xl"))])


def exchange_time(x):
    nx, nt = lax.axis_size("xl"), lax.axis_size("ta")
    pairs = []
    for x_at in range(nx):
        for t in range(nt):
            other = t + (-1 if x_at % 2 == 0 else 1)
            if 0 <= other < nt:
                pairs.append((x_at * nt + t, (x_at ^ 1) * nt + other))
    return lax.ppermute(x, ("xl", "ta"), pairs)


def codes(n):
    return ((n * 16 + 16, 128), i16)


def taper(order):
    return np.sin(np.pi * (np.arange(order) + 0.5) / order) ** 2


TILE = ((32, 32, 128), f32)


def shards(traces, live, counts, levels):
    tw, sw = tables()
    tj = jnp.asarray(np.broadcast_to(taper(64)[:, None], (64, 128)).astype(np.float32))
    tt = jnp.asarray(np.broadcast_to(taper(128)[None, :], (8, 128)).astype(np.float32))
    tw, sw = jnp.asarray(tw), jnp.asarray(sw)
    traces_other, live_other = swap_pair(traces), swap_pair(live)
    own, tw, tt = call(
        load_kernel,
        "load",
        4,
        [TILE, ((2, 256, 256), bf16), ((8, 128), f32)],
        [(32, 32, 128), pltpu.VMEM((32, 32), i32), SEM((4,))],
        [H] * 4,
        traces,
        live,
        tw,
        tt,
        cost=pl.CostEstimate(flops=1000000, bytes_accessed=6000000, transcendentals=0),
    )
    flagged, msg = call(
        pack_kernel,
        "pack",
        6,
        [((64, 32, 128), f32), codes(32)],
        [(512, 128)],
        [V] * 3,
        own,
        traces_other,
        live_other,
    )
    msg = exchange_time(msg)
    tile, lo, hi = call(
        widen_kernel,
        "widen",
        6,
        [((2048, 128), f32), codes(64), codes(64)],
        [],
        [V] * 3,
        flagged,
        msg,
        tw,
    )
    f0, f3 = exchange(lo, hi, "il", 1)
    lo, hi = call(edge_kernel, "edge", 6, [codes(64)] * 2, [(2048, 128)], [V] * 3, tile, f0, f3)
    fa, fb = exchange(lo, hi, "xl", 2)
    lo, hi, core = call(
        main_kernel,
        "windows",
        32,
        [codes(64), codes(64), ((4096, 128), f32)],
        [(64, 96, 128), (64, 96, 128), (64, 64, 128), (64, 64, 128)],
        [S, S] + [V] * 8,
        counts.transpose(0, 2, 1),
        levels,
        tile,
        f0,
        f3,
        fa,
        fb,
        tj,
        tj,
        sw,
    )
    fa, fb = exchange(lo, hi, "xl", 2)
    inner, lo, hi = call(
        fold_kernel, "fold", 8, [((2048, 128), f32), codes(64), codes(64)], [(2048, 128)], [V] * 3, core, fa, fb
    )
    fa, fb = exchange(lo, hi, "il", 1)
    own, other, msg = call(
        narrow_kernel,
        "narrow",
        8,
        [TILE, TILE, codes(32)],
        [(512, 128), (2048, 128)],
        [V] * 5,
        inner,
        fa,
        fb,
        tt,
        tw,
    )
    msg = exchange_time(msg)
    other, msg_other = swap_pair(other), swap_pair(msg)
    return call(last_kernel, "last", 4, [TILE], [], [V] * 4, own, other, msg_other, msg)[0]


def solution(mesh):
    placed = (P("il", "xl", "ta"), P("il", "xl"), P("il", None, "ta"), P())
    return jax.shard_map(
        shards, mesh=mesh, in_specs=placed, out_specs=P("il", "xl", "ta"), check_vma=False
    )
```

```python
import jax
import jax.numpy as jnp
import numpy as np
from jax import lax
from jax.experimental import pallas as pl
from jax.experimental.pallas import tpu as pltpu
from jax.sharding import PartitionSpec as P

f32=jnp.float32; bf16=jnp.bfloat16
DEAD=1e30
def dct(n):
    k=np.arange(n)[:,None]; j=np.arange(n)[None,:]
    c=np.sqrt(2.0/n)*np.cos(np.pi*(2*j+1)*k/(2*n)); c[0]*=np.sqrt(0.5); return c
def two(c):
    hi=np.asarray(c,np.float32).astype(jnp.bfloat16); lo=(c-hi.astype(np.float64)).astype(np.float32).astype(jnp.bfloat16)
    return hi,lo
def time_w(c):
    hi,lo=two(c)
    return np.concatenate([np.concatenate([hi,hi],0),np.concatenate([lo,np.zeros_like(lo)],0)],1)
def space_w(c):
    hi,lo=two(c)
    return np.concatenate([np.concatenate([hi,hi],1),np.concatenate([lo,np.zeros_like(lo)],1)],0)
def tables():
    ct=dct(128); cs=dct(64)
    tw=np.stack([time_w(ct.T),time_w(ct)])
    sw=np.stack([space_w(cs),space_w(cs.T)])
    return tw,sw
def split(x):
    hi=x.astype(bf16); return hi,(x-hi.astype(f32)).astype(bf16)
def tmul(x,w):
    hi,lo=split(x)
    y=jnp.dot(jnp.concatenate([hi,lo],1),w,preferred_element_type=f32)
    return y[:,:128]+y[:,128:]
def smul(x,w):
    hi,lo=split(x)
    y=jnp.dot(w,jnp.concatenate([hi,lo],0),preferred_element_type=f32)
    return y[:64]+y[64:]
def swap(x,n):
    y=jnp.stack([x[:,128*q:128*q+128] for q in range(n)],0)
    return jnp.swapaxes(y,0,1)


C = 32


def load_chunk(ref, n):
    return jnp.concatenate([ref[n * C + q] for q in range(C)], 1)


def windows(count, off, R, Z, Y, put, threshold, sw):
    def own(n):
        return jnp.concatenate([R[n * C + q, pl.ds(off, 64), :] for q in range(C)], 1)

    def forth(x, n):
        Z[:, pl.ds(pl.multiple_of(n * C, C), C), :] = swap(smul(x, sw[0]), C)

    def back(n):
        w = own(n)
        return jnp.where(w > 1e29, smul(load_chunk(Y, n), sw[1]), w)

    def first(n, c):
        w = own(n)
        forth(jnp.where(w > 1e29, 0.0, w), n)
        return c

    def shrink(q):
        t = threshold(q)

        def f(n, c):
            u = smul(load_chunk(Z, n), sw[0])
            u = u - jnp.clip(u, -t, t)
            Y[:, pl.ds(pl.multiple_of(n * C, C), C), :] = swap(smul(u, sw[1]), C)
            return c

        lax.fori_loop(0, 64 // C, f, 0, unroll=True)

    def again(n, c):
        forth(back(n), n)
        return c

    def step(q, c):
        shrink(q)
        lax.fori_loop(0, 64 // C, again, 0, unroll=True)
        return c

    def last(n, c):
        put(n, back(n))
        return c

    lax.fori_loop(0, 64 // C, first, 0, unroll=True)
    lax.fori_loop(0, count - 1, step, 0)
    shrink(count - 1)
    lax.fori_loop(0, 64 // C, last, 0, unroll=True)


Q = 32000.0
LN = float(np.log(2.0) / 128.0)
i32 = jnp.int32
i16 = jnp.int16


def parity():
    return lax.rem(lax.axis_index("xl"), 2)


def even_place(axis, step=1):
    return 1 - lax.rem(lax.axis_index(axis) // step, 2)


def roll(x, s):
    if isinstance(s, int):
        s %= 128
        if s == 0:
            return x
    return pltpu.roll(x, s, 1)


def at(b, n):
    return pl.ds(pl.multiple_of(b * n, n), n)


def encode(get, dst, n, flagged, un=8):
    def top(b, m):
        x = get(b)
        a = jnp.abs(x)
        if flagged:
            a = jnp.where(x > 1e29, 0.0, a)
        return jnp.maximum(m, a)

    m = lax.fori_loop(0, n, top, jnp.full((16, 128), 1e-30, f32), unroll=un)
    code = jnp.ceil(jnp.log(m) * (1.0 / LN))
    scale = Q * jnp.exp(code * -LN)

    def put(b, c):
        x = get(b)
        q = jnp.round(x * scale)
        if flagged:
            q = jnp.where(x > 1e29, 0.0, jnp.where(q >= 0, q + 1.0, q))
        dst[at(b, 16), :] = q.astype(i32).astype(i16)
        return c

    lax.fori_loop(0, n, put, 0, unroll=un)
    dst[pl.ds(n * 16, 16), :] = code.astype(i32).astype(i16)


def blocks(ref, first=0):
    return lambda b: ref[at(b + first, 16), :]


def scale_of(ref, n):
    return jnp.exp(ref[pl.ds(n * 16, 16), :].astype(i32).astype(f32) * LN) * (1.0 / Q)


def decode(ref, b, scale, flagged=False):
    q = ref[at(b, 16), :].astype(i32).astype(f32)
    if flagged:
        return jnp.where(q == 0, DEAD, (q - jnp.where(q > 0, 1.0, 0.0)) * scale)
    return q * scale


def pair_rows(ref, r, scale):
    return jnp.concatenate([decode(ref, 2 * r + h, scale) for h in (0, 1)], 0)


def spread(parts, q):
    out = parts[3]
    for n in (2, 1, 0):
        out = jnp.where(q == n, parts[n], out)
    return out


def lane_quarter():
    return lax.broadcasted_iota(i32, (32, 128), 1) // 32


def load_kernel(x_hbm, live_hbm, tw_hbm, tt_hbm, own, tw, tt, x, live, sem):
    pairs = ((live_hbm, live), (x_hbm, x), (tw_hbm, tw), (tt_hbm, tt))
    copies = [pltpu.make_async_copy(a, b, sem.at[n]) for n, (a, b) in enumerate(pairs)]
    for copy in copies:
        copy.start()
    copies[0].wait()
    copies[1].wait()
    lt = live[...].astype(f32).T
    for i in range(32):
        own[i] = jnp.where(jnp.broadcast_to(lt[:, i : i + 1], (32, 128)) > 0.5, x[i], DEAD)
    copies[2].wait()
    copies[3].wait()


def pack_kernel(own, x_other, live_other, flagged, out, s):
    odd = parity()
    q = lane_quarter()
    lt = live_other[...].astype(f32).T
    for mine in (True, False):
        column = odd if mine else 1 - odd
        for r in range(8):
            x = []
            for i in (r, r + 8, r + 16, r + 24):
                if mine:
                    v = own[i]
                else:
                    alive = jnp.broadcast_to(lt[:, i : i + 1], (32, 128)) > 0.5
                    v = jnp.where(alive, x_other[i], DEAD)
                flagged[32 * column + i] = v
                x.append(jnp.where(v > 1e29, 0.0, v))
            s[pl.ds(pl.multiple_of(256 * column + 32 * r, 32), 32), :] = spread(
                [roll(v, (32 * n + 32 * odd) % 128) for n, v in enumerate(x)], q
            )
    encode(blocks(s), out, 32, False)


def widen_kernel(flagged, f, tw, tile, lo, hi):
    odd = parity()
    halo = lane_quarter() == 3 * odd
    k = scale_of(f, 32)
    for column in (0, 1):
        for r in range(8):
            h = pair_rows(f, 8 * column + r, k)
            for n in range(4):
                i = r + 8 * n
                v = flagged[32 * column + i]
                h_n = jnp.where(v > 1e29, DEAD, roll(h, (128 - 32 * n + 96 * odd) % 128))
                rows = pl.ds(i * 64 + 32 * column, 32)
                tile[rows, :] = jnp.where(halo, h_n, roll(v, 32 + 64 * odd))
    for n in range(4):
        v = tile[n * 512 : n * 512 + 512, :]
        t = tmul(jnp.where(v > 1e29, 0.0, v), tw[0])
        tile[n * 512 : n * 512 + 512, :] = jnp.where(v > 1e29, DEAD, t)
    even = even_place("il")
    encode(blocks(tile, 64 * even), lo, 64, True)
    encode(blocks(tile, 64 - 64 * even), hi, 64, True)


def edge_kernel(tile, fa, fb, ma, mb, s):
    even = even_place("il")
    for f, base in ((fa, 48 * even), (fb, 48 - 48 * even)):
        k = scale_of(f, 64)

        def take(i, c, f=f, k=k, base=base):
            s[at(base + i, 16), :] = decode(f, 4 * i, k, True)
            s[at(64 + base + i, 16), :] = decode(f, 4 * i + 3, k, True)
            return c

        lax.fori_loop(0, 16, take, 0, unroll=8)

    def copy(i, c):
        s[at(16 + i, 16), :] = tile[at(4 * i, 16), :]
        s[at(80 + i, 16), :] = tile[at(4 * i + 3, 16), :]
        return c

    lax.fori_loop(0, 32, copy, 0, unroll=8)
    even = even_place("xl", 2)
    encode(blocks(s, 64 * even), ma, 64, True)
    encode(blocks(s, 64 - 64 * even), mb, 64, True)


def main_kernel(cnt, levels, tile, f0, f3, fa, fb, tj, ti, sw, lo, hi, acc, R, Z, Y):
    even = even_place("xl", 2)
    for f, column in ((fa, 80 * even), (fb, 80 - 80 * even)):
        rim = pl.ds(pl.multiple_of(column, 16), 16)
        k = scale_of(f, 64)

        def side(i, c, f=f, k=k, rim=rim):
            R[i, rim, :] = decode(f, i, k, True)
            return c

        lax.fori_loop(0, 64, side, 0, unroll=8)
    il_even = even_place("il")
    for f, base in ((f0, 48 * il_even), (f3, 48 - 48 * il_even)):
        k = scale_of(f, 64)

        def take(i, c, f=f, k=k, base=base):
            for x in range(4):
                R[base + i, 16 + 16 * x : 32 + 16 * x, :] = decode(f, 4 * i + x, k, True)
            return c

        lax.fori_loop(0, 16, take, 0, unroll=4)

    def copy(i, c):
        R[16 + i, 16:80, :] = tile[at(i, 64), :]
        return c

    lax.fori_loop(0, 32, copy, 0, unroll=8)
    position = lax.axis_index("xl")
    odd = lax.rem(position, 2)
    zeros = jnp.zeros((32, 128), f32)

    def window(s, c):
        off = pl.multiple_of(s * 32, 32)

        def put(n, v):
            for q in range(C):
                i = n * C + q
                t = v[:, q * 128 : q * 128 + 128] * (tj[...] * ti[pl.ds(i, 1), :])
                acc[i, pl.ds(off, 32), :] = jnp.where(s > 0, acc[i, pl.ds(off, 32), :], zeros) + t[:32]
                acc[i, pl.ds(off + 32, 32), :] = t[32:]

        count = cnt[0, odd, position - odd + s]
        windows(count, off, R, Z, Y, put, lambda q: levels[q].astype(f32) * 0.001, sw)
        return c

    lax.fori_loop(0, 2, window, 0)
    for dst, column in ((lo, 80 * even), (hi, 80 - 80 * even)):
        rim = pl.ds(pl.multiple_of(column, 16), 16)
        encode(lambda i, rim=rim: acc[i, rim, :], dst, 64, False)


def fold_row(acc, p, fa, fb, ka, kb, even, dst, r):
    a, b = decode(fa, p, ka), decode(fb, p, kb)
    dst[at(4 * r, 16), :] = acc[p, 16:32, :] + jnp.where(even, b, a)
    dst[pl.ds(pl.multiple_of(r * 64 + 16, 16), 32), :] = acc[p, 32:64, :]
    dst[at(4 * r + 3, 16), :] = acc[p, 64:80, :] + jnp.where(even, a, b)


def fold_kernel(acc, fa, fb, ma, mb, s):
    even = even_place("xl", 2) > 0
    ka, kb = scale_of(fa, 64), scale_of(fb, 64)
    for first, base in ((0, 0), (48, 16)):

        def add(i, c, first=first, base=base):
            fold_row(acc, first + i, fa, fb, ka, kb, even, s, base + i)
            return c

        lax.fori_loop(0, 16, add, 0, unroll=8)
    il_even = even_place("il")
    encode(blocks(s, 64 * il_even), ma, 64, False)
    encode(blocks(s, 64 - 64 * il_even), mb, 64, False)


def inner_kernel(acc, fa, fb, inner):
    even = even_place("xl", 2) > 0
    ka, kb = scale_of(fa, 64), scale_of(fb, 64)

    def add(i, c):
        fold_row(acc, 16 + i, fa, fb, ka, kb, even, inner, i)
        return c

    lax.fori_loop(0, 32, add, 0, unroll=8)


def narrow_kernel(inner, fa, fb, tt, tw, own, other, out, s, sv):
    odd = parity()
    q = lane_quarter()
    even = even_place("il")
    for f, base in ((fa, 64 * even), (fb, 64 - 64 * even)):
        k = scale_of(f, 64)
        for b in range(64):
            sv[at(base + b, 16), :] = inner[at(base + b, 16), :] + decode(f, b, k)
    for n in range(4):
        sv[n * 512 : n * 512 + 512, :] = tmul(sv[n * 512 : n * 512 + 512, :], tw[1]) * tt[0:1, :]
    for column in (0, 1):
        for r in range(8):
            parts = []
            for n in range(4):
                v = sv[pl.ds((r + 8 * n) * 64 + 32 * column, 32), :]
                parts.append(roll(v, (32 * n + 32 * odd) % 128))
            s[pl.ds(256 * column + 32 * r, 32), :] = spread(parts, q)
    for i in range(32):
        own[i] = sv[pl.ds(pl.multiple_of(i * 64 + 32 * odd, 32), 32), :]
        other[i] = sv[pl.ds(pl.multiple_of(i * 64 + 32 - 32 * odd, 32), 32), :]
    encode(blocks(s), out, 32, False)


def last_kernel(own, other, fa, fb, out, rows, sem):
    odd = parity()
    q = lane_quarter()
    low, high = 3 - 3 * odd, 3 * odd
    ka, kb = scale_of(fa, 32), scale_of(fb, 32)
    copies = []
    for n in range(4):
        for r in range(8):
            a, b = pair_rows(fa, 8 * odd + r, ka), pair_rows(fb, 8 * odd + r, kb)
            i = r + 8 * n
            v = jnp.where(q == low, roll(a, (224 - 32 * n + 32 * odd) % 128), roll(own[i], (96 + 64 * odd) % 128))
            w = jnp.where(q == high, roll(b, (256 - 32 * n + 96 * odd) % 128), roll(other[i], (32 + 64 * odd) % 128))
            rows[i] = v + w
        copies.append(pltpu.make_async_copy(rows.at[pl.ds(8 * n, 8)], out.at[pl.ds(8 * n, 8)], sem.at[n]))
        copies[-1].start()
    for copy in copies:
        copy.wait()


V = pl.BlockSpec(memory_space=pltpu.VMEM)
S = pl.BlockSpec(memory_space=pltpu.SMEM)
H = pl.BlockSpec(memory_space=pltpu.HBM)
SEM = pltpu.SemaphoreType.DMA


def call(kernel, name, mib, outs, scratch, specs, *args, cost=None, out_spec=V):
    shapes = [jax.ShapeDtypeStruct(s, t) for s, t in outs]
    args = [pltpu.with_memory_space_constraint(a, pltpu.HBM) if p is H else a for a, p in zip(args, specs)]
    return pl.pallas_call(
        kernel,
        out_shape=shapes,
        in_specs=specs,
        out_specs=[out_spec] * len(outs),
        scratch_shapes=[pltpu.VMEM(s, f32) if isinstance(s, tuple) else s for s in scratch],
        compiler_params=pltpu.CompilerParams(vmem_limit_bytes=mib * 1024 * 1024),
        name=name,
        cost_estimate=cost,
    )(*args)


def exchange(first, second, axis, step):
    count = lax.axis_size(axis)
    rounds = []
    for start in (0, step):
        up = [(i, i + step) for i in range(count - step) if i // step % 2 == start // step]
        rounds.append(up + [(b, a) for a, b in up])
    return lax.ppermute(first, axis, rounds[0]), lax.ppermute(second, axis, rounds[1])


def swap_pair(x):
    return lax.ppermute(x, "xl", [(i, i ^ 1) for i in range(lax.axis_size("xl"))])


def exchange_time(x):
    nx, nt = lax.axis_size("xl"), lax.axis_size("ta")
    pairs = []
    for x_at in range(nx):
        for t in range(nt):
            other = t + (-1 if x_at % 2 == 0 else 1)
            if 0 <= other < nt:
                pairs.append((x_at * nt + t, (x_at ^ 1) * nt + other))
    return lax.ppermute(x, ("xl", "ta"), pairs)


def codes(n):
    return ((n * 16 + 16, 128), i16)


def taper(order):
    return np.sin(np.pi * (np.arange(order) + 0.5) / order) ** 2


TILE = ((32, 32, 128), f32)


def shards(traces, live, counts, levels):
    tw, sw = tables()
    tj = jnp.asarray(np.broadcast_to(taper(64)[:, None], (64, 128)).astype(np.float32))
    tt = jnp.asarray(np.broadcast_to(taper(128)[None, :], (8, 128)).astype(np.float32))
    tw, sw = jnp.asarray(tw), jnp.asarray(sw)
    traces_other, live_other = swap_pair(traces), swap_pair(live)
    own, tw, tt = call(
        load_kernel,
        "load",
        4,
        [TILE, ((2, 256, 256), bf16), ((8, 128), f32)],
        [(32, 32, 128), pltpu.VMEM((32, 32), i32), SEM((4,))],
        [H] * 4,
        traces,
        live,
        tw,
        tt,
        cost=pl.CostEstimate(flops=1000000, bytes_accessed=6000000, transcendentals=0),
    )
    flagged, msg = call(
        pack_kernel,
        "pack",
        6,
        [((64, 32, 128), f32), codes(32)],
        [(512, 128)],
        [V] * 3,
        own,
        traces_other,
        live_other,
    )
    msg = exchange_time(msg)
    tile, lo, hi = call(
        widen_kernel,
        "widen",
        6,
        [((2048, 128), f32), codes(64), codes(64)],
        [],
        [V] * 3,
        flagged,
        msg,
        tw,
    )
    f0, f3 = exchange(lo, hi, "il", 1)
    lo, hi = call(edge_kernel, "edge", 6, [codes(64)] * 2, [(2048, 128)], [V] * 3, tile, f0, f3)
    fa, fb = exchange(lo, hi, "xl", 2)
    lo, hi, acc = call(
        main_kernel,
        "windows",
        32,
        [codes(64), codes(64), ((64, 96, 128), f32)],
        [(64, 96, 128), (64, 64, 128), (64, 64, 128)],
        [S, S] + [V] * 8,
        counts.transpose(0, 2, 1),
        levels,
        tile,
        f0,
        f3,
        fa,
        fb,
        tj,
        tj,
        sw,
    )
    fa, fb = exchange(lo, hi, "xl", 2)
    lo, hi = call(fold_kernel, "fold", 8, [codes(64)] * 2, [(2048, 128)], [V] * 3, acc, fa, fb)
    cost = pl.CostEstimate(flops=1000000, bytes_accessed=4000000, transcendentals=0)
    inner = call(inner_kernel, "inner", 4, [((2048, 128), f32)], [], [V] * 3, acc, fa, fb, cost=cost)[0]
    fa, fb = exchange(lo, hi, "il", 1)
    own, other, msg = call(
        narrow_kernel,
        "narrow",
        8,
        [TILE, TILE, codes(32)],
        [(512, 128), (2048, 128)],
        [V] * 5,
        inner,
        fa,
        fb,
        tt,
        tw,
    )
    msg = exchange_time(msg)
    other, msg_other = swap_pair(other), swap_pair(msg)
    return call(
        last_kernel, "last", 4, [TILE], [(32, 32, 128), SEM((4,))], [V] * 4, own, other, msg_other, msg, out_spec=H
    )[0]


def solution(mesh):
    placed = (P("il", "xl", "ta"), P("il", "xl"), P("il", None, "ta"), P())
    return jax.shard_map(
        shards, mesh=mesh, in_specs=placed, out_specs=P("il", "xl", "ta"), check_vma=False
    )
```

```python
import jax
import jax.numpy as jnp
import numpy as np
from jax import lax
from jax.experimental import pallas as pl
from jax.experimental.pallas import tpu as pltpu
from jax.sharding import PartitionSpec as P

f32=jnp.float32; bf16=jnp.bfloat16
DEAD=1e30
def dct(n):
    k=np.arange(n)[:,None]; j=np.arange(n)[None,:]
    c=np.sqrt(2.0/n)*np.cos(np.pi*(2*j+1)*k/(2*n)); c[0]*=np.sqrt(0.5); return c
def two(c):
    hi=np.asarray(c,np.float32).astype(jnp.bfloat16); lo=(c-hi.astype(np.float64)).astype(np.float32).astype(jnp.bfloat16)
    return hi,lo
def time_w(c):
    hi,lo=two(c)
    return np.concatenate([np.concatenate([hi,hi],0),np.concatenate([lo,np.zeros_like(lo)],0)],1)
def space_w(c):
    hi,lo=two(c)
    return np.concatenate([np.concatenate([hi,hi],1),np.concatenate([lo,np.zeros_like(lo)],1)],0)
def tables():
    ct=dct(128); cs=dct(64)
    tw=np.stack([time_w(ct.T),time_w(ct)])
    sw=np.stack([space_w(cs),space_w(cs.T)])
    return tw,sw
def split(x):
    hi=x.astype(bf16); return hi,(x-hi.astype(f32)).astype(bf16)
def tmul(x,w):
    hi,lo=split(x)
    y=jnp.dot(jnp.concatenate([hi,lo],1),w,preferred_element_type=f32)
    return y[:,:128]+y[:,128:]
def smul(x,w):
    hi,lo=split(x)
    y=jnp.dot(w,jnp.concatenate([hi,lo],0),preferred_element_type=f32)
    return y[:64]+y[64:]
def swap(x,n):
    y=jnp.stack([x[:,128*q:128*q+128] for q in range(n)],0)
    return jnp.swapaxes(y,0,1)


C = 32


def load_chunk(ref, n):
    return jnp.concatenate([ref[n * C + q] for q in range(C)], 1)


def windows(count, R, Z, Y, put, threshold, sw):
    def own(n):
        return jnp.concatenate([R[n * C + q] for q in range(C)], 1)

    def forth(x, n):
        Z[:, pl.ds(pl.multiple_of(n * C, C), C), :] = swap(smul(x, sw[0]), C)

    def back(n):
        w = own(n)
        return jnp.where(w > 1e29, smul(load_chunk(Y, n), sw[1]), w)

    def first(n, c):
        w = own(n)
        forth(jnp.where(w > 1e29, 0.0, w), n)
        return c

    def shrink(q):
        t = threshold(q)

        def f(n, c):
            u = smul(load_chunk(Z, n), sw[0])
            u = u - jnp.clip(u, -t, t)
            Y[:, pl.ds(pl.multiple_of(n * C, C), C), :] = swap(smul(u, sw[1]), C)
            return c

        lax.fori_loop(0, 64 // C, f, 0, unroll=True)

    def again(n, c):
        forth(back(n), n)
        return c

    def step(q, c):
        shrink(q)
        lax.fori_loop(0, 64 // C, again, 0, unroll=True)
        return c

    def last(n, c):
        put(n, back(n))
        return c

    lax.fori_loop(0, 64 // C, first, 0, unroll=True)
    lax.fori_loop(0, count - 1, step, 0)
    shrink(count - 1)
    lax.fori_loop(0, 64 // C, last, 0, unroll=True)


Q = 32000.0
LN = float(np.log(2.0) / 128.0)
i32 = jnp.int32
i16 = jnp.int16


def parity():
    return lax.rem(lax.axis_index("xl"), 2)


def even_place(axis, step=1):
    return 1 - lax.rem(lax.axis_index(axis) // step, 2)


def roll(x, s):
    if isinstance(s, int):
        s %= 128
        if s == 0:
            return x
    return pltpu.roll(x, s, 1)


def at(b, n):
    return pl.ds(pl.multiple_of(b * n, n), n)


def encode(get, dst, n, flagged, un=8):
    def top(b, m):
        x = get(b)
        a = jnp.abs(x)
        if flagged:
            a = jnp.where(x > 1e29, 0.0, a)
        return jnp.maximum(m, a)

    m = lax.fori_loop(0, n, top, jnp.full((16, 128), 1e-30, f32), unroll=un)
    code = jnp.ceil(jnp.log(m) * (1.0 / LN))
    scale = Q * jnp.exp(code * -LN)

    def put(b, c):
        x = get(b)
        q = jnp.round(x * scale)
        if flagged:
            q = jnp.where(x > 1e29, 0.0, jnp.where(q >= 0, q + 1.0, q))
        dst[at(b, 16), :] = q.astype(i32).astype(i16)
        return c

    lax.fori_loop(0, n, put, 0, unroll=un)
    dst[pl.ds(n * 16, 16), :] = code.astype(i32).astype(i16)


def blocks(ref, first=0):
    return lambda b: ref[at(b + first, 16), :]


def scale_of(ref, n):
    return jnp.exp(ref[pl.ds(n * 16, 16), :].astype(i32).astype(f32) * LN) * (1.0 / Q)


def decode(ref, b, scale, flagged=False):
    q = ref[at(b, 16), :].astype(i32).astype(f32)
    if flagged:
        return jnp.where(q == 0, DEAD, (q - jnp.where(q > 0, 1.0, 0.0)) * scale)
    return q * scale


def pair_rows(ref, r, scale):
    return jnp.concatenate([decode(ref, 2 * r + h, scale) for h in (0, 1)], 0)


def spread(parts, q):
    out = parts[3]
    for n in (2, 1, 0):
        out = jnp.where(q == n, parts[n], out)
    return out


def lane_quarter():
    return lax.broadcasted_iota(i32, (32, 128), 1) // 32


def load_kernel(x_hbm, live_hbm, tw_hbm, tt_hbm, own, tw, tt, x, live, sem):
    pairs = ((live_hbm, live), (x_hbm, x), (tw_hbm, tw), (tt_hbm, tt))
    copies = [pltpu.make_async_copy(a, b, sem.at[n]) for n, (a, b) in enumerate(pairs)]
    for copy in copies:
        copy.start()
    copies[0].wait()
    copies[1].wait()
    lt = live[...].astype(f32).T
    for i in range(32):
        own[i] = jnp.where(jnp.broadcast_to(lt[:, i : i + 1], (32, 128)) > 0.5, x[i], DEAD)
    copies[2].wait()
    copies[3].wait()


def pack_kernel(own, x_other, live_other, flagged, out, s):
    odd = parity()
    q = lane_quarter()
    lt = live_other[...].astype(f32).T
    for mine in (True, False):
        column = odd if mine else 1 - odd
        for r in range(8):
            x = []
            for i in (r, r + 8, r + 16, r + 24):
                if mine:
                    v = own[i]
                else:
                    alive = jnp.broadcast_to(lt[:, i : i + 1], (32, 128)) > 0.5
                    v = jnp.where(alive, x_other[i], DEAD)
                flagged[32 * column + i] = v
                x.append(jnp.where(v > 1e29, 0.0, v))
            s[pl.ds(pl.multiple_of(256 * column + 32 * r, 32), 32), :] = spread(
                [roll(v, (32 * n + 32 * odd) % 128) for n, v in enumerate(x)], q
            )
    encode(blocks(s), out, 32, False)


def widen_kernel(flagged, f, tw, tile, lo, hi):
    odd = parity()
    halo = lane_quarter() == 3 * odd
    k = scale_of(f, 32)
    for column in (0, 1):
        for r in range(8):
            h = pair_rows(f, 8 * column + r, k)
            for n in range(4):
                i = r + 8 * n
                v = flagged[32 * column + i]
                h_n = jnp.where(v > 1e29, DEAD, roll(h, (128 - 32 * n + 96 * odd) % 128))
                rows = pl.ds(i * 64 + 32 * column, 32)
                tile[rows, :] = jnp.where(halo, h_n, roll(v, 32 + 64 * odd))
    for n in range(4):
        v = tile[n * 512 : n * 512 + 512, :]
        t = tmul(jnp.where(v > 1e29, 0.0, v), tw[0])
        tile[n * 512 : n * 512 + 512, :] = jnp.where(v > 1e29, DEAD, t)
    even = even_place("il")
    encode(blocks(tile, 64 * even), lo, 64, True)
    encode(blocks(tile, 64 - 64 * even), hi, 64, True)


def edge_kernel(tile, fa, fb, ma, mb, s):
    even = even_place("il")
    for f, base in ((fa, 48 * even), (fb, 48 - 48 * even)):
        k = scale_of(f, 64)

        def take(i, c, f=f, k=k, base=base):
            s[at(base + i, 16), :] = decode(f, 4 * i, k, True)
            s[at(64 + base + i, 16), :] = decode(f, 4 * i + 3, k, True)
            return c

        lax.fori_loop(0, 16, take, 0, unroll=8)

    def copy(i, c):
        s[at(16 + i, 16), :] = tile[at(4 * i, 16), :]
        s[at(80 + i, 16), :] = tile[at(4 * i + 3, 16), :]
        return c

    lax.fori_loop(0, 32, copy, 0, unroll=8)
    even = even_place("xl", 2)
    encode(blocks(s, 64 * even), ma, 64, True)
    encode(blocks(s, 64 - 64 * even), mb, 64, True)


def one_window(s, cnt, levels, tile, f0, f3, rim, tj, sw, put, R, Z, Y):
    k = scale_of(rim, 64)
    start = pl.multiple_of(16 - 16 * s, 16)
    edge = pl.ds(pl.multiple_of(48 * s, 16), 16)

    def side(i, c):
        R[i, edge, :] = decode(rim, i, k, True)
        return c

    lax.fori_loop(0, 64, side, 0, unroll=8)
    il_even = even_place("il")
    for f, base in ((f0, 48 * il_even), (f3, 48 - 48 * il_even)):
        k = scale_of(f, 64)

        def take(i, c, f=f, k=k, base=base):
            for x in range(3):
                columns = pl.ds(pl.multiple_of(start + 16 * x, 16), 16)
                R[base + i, columns, :] = decode(f, 4 * i + s + x, k, True)
            return c

        lax.fori_loop(0, 16, take, 0, unroll=4)

    def copy(i, c):
        R[16 + i, pl.ds(start, 48), :] = tile[pl.ds(pl.multiple_of(i * 64 + 16 * s, 16), 48), :]
        return c

    lax.fori_loop(0, 32, copy, 0, unroll=8)
    position = lax.axis_index("xl")
    odd = lax.rem(position, 2)

    def put_rows(n, v):
        for q in range(C):
            i = n * C + q
            put(i, v[:, q * 128 : q * 128 + 128] * (tj[...] * tj[pl.ds(i, 1), :]))

    count = cnt[0, odd, position - odd + s]
    windows(count, R, Z, Y, put_rows, lambda q: levels[q].astype(f32) * 0.001, sw)


def first_kernel(cnt, levels, tile, f0, f3, rim, tj, sw, out, R, Z, Y):
    def put(i, t):
        out[i] = t

    one_window(even_place("xl", 2), cnt, levels, tile, f0, f3, rim, tj, sw, put, R, Z, Y)


def second_kernel(cnt, levels, tile, f0, f3, rim, tj, sw, before, lo, hi, acc, R, Z, Y):
    even = even_place("xl", 2)
    s = 1 - even

    def put(i, t):
        acc[i, pl.ds(pl.multiple_of(32 * s, 32), 64), :] = t
        rest = pl.ds(pl.multiple_of(64 - 64 * s, 32), 32)
        acc[i, rest, :] = before[i, pl.ds(pl.multiple_of(32 - 32 * s, 32), 32), :]
        acc[i, 32:64, :] = acc[i, 32:64, :] + before[i, pl.ds(pl.multiple_of(32 * s, 32), 32), :]

    one_window(s, cnt, levels, tile, f0, f3, rim, tj, sw, put, R, Z, Y)
    for dst, column in ((lo, 80 * even), (hi, 80 - 80 * even)):
        rim_at = pl.ds(pl.multiple_of(column, 16), 16)
        encode(lambda i, rim_at=rim_at: acc[i, rim_at, :], dst, 64, False)


def fold_row(acc, p, fa, fb, ka, kb, even, dst, r):
    a, b = decode(fa, p, ka), decode(fb, p, kb)
    dst[at(4 * r, 16), :] = acc[p, 16:32, :] + jnp.where(even, b, a)
    dst[pl.ds(pl.multiple_of(r * 64 + 16, 16), 32), :] = acc[p, 32:64, :]
    dst[at(4 * r + 3, 16), :] = acc[p, 64:80, :] + jnp.where(even, a, b)


def fold_kernel(acc, fa, fb, ma, mb, s):
    even = even_place("xl", 2) > 0
    ka, kb = scale_of(fa, 64), scale_of(fb, 64)
    for first, base in ((0, 0), (48, 16)):

        def add(i, c, first=first, base=base):
            fold_row(acc, first + i, fa, fb, ka, kb, even, s, base + i)
            return c

        lax.fori_loop(0, 16, add, 0, unroll=8)
    il_even = even_place("il")
    encode(blocks(s, 64 * il_even), ma, 64, False)
    encode(blocks(s, 64 - 64 * il_even), mb, 64, False)


def inner_kernel(acc, fa, fb, inner):
    even = even_place("xl", 2) > 0
    ka, kb = scale_of(fa, 64), scale_of(fb, 64)

    def add(i, c):
        fold_row(acc, 16 + i, fa, fb, ka, kb, even, inner, i)
        return c

    lax.fori_loop(0, 32, add, 0, unroll=8)


def narrow_kernel(inner, fa, fb, tt, tw, own, other, out, s, sv):
    odd = parity()
    q = lane_quarter()
    even = even_place("il")
    for f, base in ((fa, 64 * even), (fb, 64 - 64 * even)):
        k = scale_of(f, 64)
        for b in range(64):
            sv[at(base + b, 16), :] = inner[at(base + b, 16), :] + decode(f, b, k)
    for n in range(4):
        sv[n * 512 : n * 512 + 512, :] = tmul(sv[n * 512 : n * 512 + 512, :], tw[1]) * tt[0:1, :]
    for column in (0, 1):
        for r in range(8):
            parts = []
            for n in range(4):
                v = sv[pl.ds((r + 8 * n) * 64 + 32 * column, 32), :]
                parts.append(roll(v, (32 * n + 32 * odd) % 128))
            s[pl.ds(256 * column + 32 * r, 32), :] = spread(parts, q)
    for i in range(32):
        own[i] = sv[pl.ds(pl.multiple_of(i * 64 + 32 * odd, 32), 32), :]
        other[i] = sv[pl.ds(pl.multiple_of(i * 64 + 32 - 32 * odd, 32), 32), :]
    encode(blocks(s), out, 32, False)


def last_kernel(own, other, fa, fb, out, rows, sem):
    odd = parity()
    q = lane_quarter()
    low, high = 3 - 3 * odd, 3 * odd
    ka, kb = scale_of(fa, 32), scale_of(fb, 32)
    copies = []
    for n in range(4):
        for r in range(8):
            a, b = pair_rows(fa, 8 * odd + r, ka), pair_rows(fb, 8 * odd + r, kb)
            i = r + 8 * n
            v = jnp.where(q == low, roll(a, (224 - 32 * n + 32 * odd) % 128), roll(own[i], (96 + 64 * odd) % 128))
            w = jnp.where(q == high, roll(b, (256 - 32 * n + 96 * odd) % 128), roll(other[i], (32 + 64 * odd) % 128))
            rows[i] = v + w
        copies.append(pltpu.make_async_copy(rows.at[pl.ds(8 * n, 8)], out.at[pl.ds(8 * n, 8)], sem.at[n]))
        copies[-1].start()
    for copy in copies:
        copy.wait()


V = pl.BlockSpec(memory_space=pltpu.VMEM)
S = pl.BlockSpec(memory_space=pltpu.SMEM)
H = pl.BlockSpec(memory_space=pltpu.HBM)
SEM = pltpu.SemaphoreType.DMA


def call(kernel, name, mib, outs, scratch, specs, *args, cost=None, out_spec=V):
    shapes = [jax.ShapeDtypeStruct(s, t) for s, t in outs]
    args = [pltpu.with_memory_space_constraint(a, pltpu.HBM) if p is H else a for a, p in zip(args, specs)]
    return pl.pallas_call(
        kernel,
        out_shape=shapes,
        in_specs=specs,
        out_specs=[out_spec] * len(outs),
        scratch_shapes=[pltpu.VMEM(s, f32) if isinstance(s, tuple) else s for s in scratch],
        compiler_params=pltpu.CompilerParams(vmem_limit_bytes=mib * 1024 * 1024),
        name=name,
        cost_estimate=cost,
    )(*args)


def exchange(first, second, axis, step):
    count = lax.axis_size(axis)
    rounds = []
    for start in (0, step):
        up = [(i, i + step) for i in range(count - step) if i // step % 2 == start // step]
        rounds.append(up + [(b, a) for a, b in up])
    return lax.ppermute(first, axis, rounds[0]), lax.ppermute(second, axis, rounds[1])


def swap_pair(x):
    return lax.ppermute(x, "xl", [(i, i ^ 1) for i in range(lax.axis_size("xl"))])


def exchange_time(x):
    nx, nt = lax.axis_size("xl"), lax.axis_size("ta")
    pairs = []
    for x_at in range(nx):
        for t in range(nt):
            other = t + (-1 if x_at % 2 == 0 else 1)
            if 0 <= other < nt:
                pairs.append((x_at * nt + t, (x_at ^ 1) * nt + other))
    return lax.ppermute(x, ("xl", "ta"), pairs)


def codes(n):
    return ((n * 16 + 16, 128), i16)


def taper(order):
    return np.sin(np.pi * (np.arange(order) + 0.5) / order) ** 2


TILE = ((32, 32, 128), f32)


def shards(traces, live, counts, levels):
    tw, sw = tables()
    tj = jnp.asarray(np.broadcast_to(taper(64)[:, None], (64, 128)).astype(np.float32))
    tt = jnp.asarray(np.broadcast_to(taper(128)[None, :], (8, 128)).astype(np.float32))
    tw, sw = jnp.asarray(tw), jnp.asarray(sw)
    traces_other, live_other = swap_pair(traces), swap_pair(live)
    own, tw, tt = call(
        load_kernel,
        "load",
        4,
        [TILE, ((2, 256, 256), bf16), ((8, 128), f32)],
        [(32, 32, 128), pltpu.VMEM((32, 32), i32), SEM((4,))],
        [H] * 4,
        traces,
        live,
        tw,
        tt,
        cost=pl.CostEstimate(flops=1000000, bytes_accessed=6000000, transcendentals=0),
    )
    flagged, msg = call(
        pack_kernel,
        "pack",
        6,
        [((64, 32, 128), f32), codes(32)],
        [(512, 128)],
        [V] * 3,
        own,
        traces_other,
        live_other,
    )
    msg = exchange_time(msg)
    tile, lo, hi = call(
        widen_kernel,
        "widen",
        6,
        [((2048, 128), f32), codes(64), codes(64)],
        [],
        [V] * 3,
        flagged,
        msg,
        tw,
    )
    f0, f3 = exchange(lo, hi, "il", 1)
    lo, hi = call(edge_kernel, "edge", 6, [codes(64)] * 2, [(2048, 128)], [V] * 3, tile, f0, f3)
    fa, fb = exchange(lo, hi, "xl", 2)
    cost = pl.CostEstimate(flops=8000000000, bytes_accessed=30000000, transcendentals=0)
    shared = (counts.transpose(0, 2, 1), levels, tile, f0, f3)
    scratch = [(64, 64, 128)] * 3
    specs = [S, S] + [V] * 6
    before = call(
        first_kernel, "first", 16, [((64, 64, 128), f32)], scratch, specs, *shared, fa, tj, sw, cost=cost
    )[0]
    lo, hi, acc = call(
        second_kernel,
        "second",
        16,
        [codes(64), codes(64), ((64, 96, 128), f32)],
        scratch,
        specs + [V],
        *shared,
        fb,
        tj,
        sw,
        before,
        cost=cost,
    )
    fa, fb = exchange(lo, hi, "xl", 2)
    lo, hi = call(fold_kernel, "fold", 8, [codes(64)] * 2, [(2048, 128)], [V] * 3, acc, fa, fb)
    cost = pl.CostEstimate(flops=1000000, bytes_accessed=4000000, transcendentals=0)
    inner = call(inner_kernel, "inner", 4, [((2048, 128), f32)], [], [V] * 3, acc, fa, fb, cost=cost)[0]
    fa, fb = exchange(lo, hi, "il", 1)
    own, other, msg = call(
        narrow_kernel,
        "narrow",
        8,
        [TILE, TILE, codes(32)],
        [(512, 128), (2048, 128)],
        [V] * 5,
        inner,
        fa,
        fb,
        tt,
        tw,
    )
    msg = exchange_time(msg)
    other, msg_other = swap_pair(other), swap_pair(msg)
    return call(
        last_kernel, "last", 4, [TILE], [(32, 32, 128), SEM((4,))], [V] * 4, own, other, msg_other, msg, out_spec=H
    )[0]


def solution(mesh):
    placed = (P("il", "xl", "ta"), P("il", "xl"), P("il", None, "ta"), P())
    return jax.shard_map(
        shards, mesh=mesh, in_specs=placed, out_specs=P("il", "xl", "ta"), check_vma=False
    )
```

```python
import functools

import jax
import jax.numpy as jnp
import numpy as np
from jax import lax
from jax.experimental import pallas as pl
from jax.experimental.pallas import tpu as pltpu
from jax.sharding import PartitionSpec as P

f32=jnp.float32; bf16=jnp.bfloat16
DEAD=1e30
def dct(n):
    k=np.arange(n)[:,None]; j=np.arange(n)[None,:]
    c=np.sqrt(2.0/n)*np.cos(np.pi*(2*j+1)*k/(2*n)); c[0]*=np.sqrt(0.5); return c
def two(c):
    hi=np.asarray(c,np.float32).astype(jnp.bfloat16); lo=(c-hi.astype(np.float64)).astype(np.float32).astype(jnp.bfloat16)
    return hi,lo
def time_w(c):
    hi,lo=two(c)
    return np.concatenate([np.concatenate([hi,hi],0),np.concatenate([lo,np.zeros_like(lo)],0)],1)
def space_w(c):
    hi,lo=two(c)
    return np.concatenate([np.concatenate([hi,hi],1),np.concatenate([lo,np.zeros_like(lo)],1)],0)
def tables():
    ct=dct(128); cs=dct(64)
    tw=np.stack([time_w(ct.T),time_w(ct)])
    sw=np.stack([space_w(cs),space_w(cs.T)])
    return tw,sw
def split(x):
    hi=x.astype(bf16); return hi,(x-hi.astype(f32)).astype(bf16)
def tmul(x,w):
    hi,lo=split(x)
    y=jnp.dot(jnp.concatenate([hi,lo],1),w,preferred_element_type=f32)
    return y[:,:128]+y[:,128:]
def smul(x,w):
    hi,lo=split(x)
    y=jnp.dot(w,jnp.concatenate([hi,lo],0),preferred_element_type=f32)
    return y[:64]+y[64:]
def swap(x,n):
    y=jnp.stack([x[:,128*q:128*q+128] for q in range(n)],0)
    return jnp.swapaxes(y,0,1)


C = 32


def load_chunk(ref, n):
    return jnp.concatenate([ref[n * C + q] for q in range(C)], 1)


def windows(count, R, Z, Y, put, threshold, sw):
    def own(n):
        return jnp.concatenate([R[n * C + q] for q in range(C)], 1)

    def forth(x, n):
        Z[:, pl.ds(pl.multiple_of(n * C, C), C), :] = swap(smul(x, sw[0]), C)

    def back(n):
        w = own(n)
        return jnp.where(w > 1e29, smul(load_chunk(Y, n), sw[1]), w)

    def first(n, c):
        w = own(n)
        forth(jnp.where(w > 1e29, 0.0, w), n)
        return c

    def shrink(q):
        t = threshold(q)

        def f(n, c):
            u = smul(load_chunk(Z, n), sw[0])
            u = u - jnp.clip(u, -t, t)
            Y[:, pl.ds(pl.multiple_of(n * C, C), C), :] = swap(smul(u, sw[1]), C)
            return c

        lax.fori_loop(0, 64 // C, f, 0, unroll=True)

    def again(n, c):
        forth(back(n), n)
        return c

    def step(q, c):
        shrink(q)
        lax.fori_loop(0, 64 // C, again, 0, unroll=True)
        return c

    def last(n, c):
        put(n, back(n))
        return c

    lax.fori_loop(0, 64 // C, first, 0, unroll=True)
    lax.fori_loop(0, count - 1, step, 0)
    shrink(count - 1)
    lax.fori_loop(0, 64 // C, last, 0, unroll=True)


Q = 32000.0
LN = float(np.log(2.0) / 128.0)
i32 = jnp.int32
i16 = jnp.int16


def parity():
    return lax.rem(lax.axis_index("xl"), 2)


def even_place(axis, step=1):
    return 1 - lax.rem(lax.axis_index(axis) // step, 2)


def roll(x, s):
    if isinstance(s, int):
        s %= 128
        if s == 0:
            return x
    return pltpu.roll(x, s, 1)


def at(b, n):
    return pl.ds(pl.multiple_of(b * n, n), n)


def encode(get, dst, n, flagged, un=8):
    def top(b, m):
        x = get(b)
        a = jnp.abs(x)
        if flagged:
            a = jnp.where(x > 1e29, 0.0, a)
        return jnp.maximum(m, a)

    m = lax.fori_loop(0, n, top, jnp.full((16, 128), 1e-30, f32), unroll=un)
    code = jnp.ceil(jnp.log(m) * (1.0 / LN))
    scale = Q * jnp.exp(code * -LN)

    def put(b, c):
        x = get(b)
        q = jnp.round(x * scale)
        if flagged:
            q = jnp.where(x > 1e29, 0.0, jnp.where(q >= 0, q + 1.0, q))
        dst[at(b, 16), :] = q.astype(i32).astype(i16)
        return c

    lax.fori_loop(0, n, put, 0, unroll=un)
    dst[pl.ds(n * 16, 16), :] = code.astype(i32).astype(i16)


def blocks(ref, first=0):
    return lambda b: ref[at(b + first, 16), :]


def scale_of(ref, n):
    return jnp.exp(ref[pl.ds(n * 16, 16), :].astype(i32).astype(f32) * LN) * (1.0 / Q)


def decode(ref, b, scale, flagged=False):
    q = ref[at(b, 16), :].astype(i32).astype(f32)
    if flagged:
        return jnp.where(q == 0, DEAD, (q - jnp.where(q > 0, 1.0, 0.0)) * scale)
    return q * scale


def pair_rows(ref, r, scale):
    return jnp.concatenate([decode(ref, 2 * r + h, scale) for h in (0, 1)], 0)


def spread(parts, q):
    out = parts[3]
    for n in (2, 1, 0):
        out = jnp.where(q == n, parts[n], out)
    return out


def lane_quarter():
    return lax.broadcasted_iota(i32, (32, 128), 1) // 32


def load_kernel(x_hbm, live_hbm, tw_hbm, tt_hbm, own, tw, tt, x, live, sem):
    pairs = ((live_hbm, live), (x_hbm, x), (tw_hbm, tw), (tt_hbm, tt))
    copies = [pltpu.make_async_copy(a, b, sem.at[n]) for n, (a, b) in enumerate(pairs)]
    for copy in copies:
        copy.start()
    copies[0].wait()
    copies[1].wait()
    lt = live[...].astype(f32).T
    for i in range(32):
        own[i] = jnp.where(jnp.broadcast_to(lt[:, i : i + 1], (32, 128)) > 0.5, x[i], DEAD)
    copies[2].wait()
    copies[3].wait()


def pack_kernel(own, x_other, live_other, flagged, out, s):
    odd = parity()
    q = lane_quarter()
    lt = live_other[...].astype(f32).T
    for mine in (True, False):
        column = odd if mine else 1 - odd
        for r in range(8):
            x = []
            for i in (r, r + 8, r + 16, r + 24):
                if mine:
                    v = own[i]
                else:
                    alive = jnp.broadcast_to(lt[:, i : i + 1], (32, 128)) > 0.5
                    v = jnp.where(alive, x_other[i], DEAD)
                flagged[32 * column + i] = v
                x.append(jnp.where(v > 1e29, 0.0, v))
            s[pl.ds(pl.multiple_of(256 * column + 32 * r, 32), 32), :] = spread(
                [roll(v, (32 * n + 32 * odd) % 128) for n, v in enumerate(x)], q
            )
    encode(blocks(s), out, 32, False)


def widen_kernel(flagged, f, tw, tile, lo, hi):
    odd = parity()
    halo = lane_quarter() == 3 * odd
    k = scale_of(f, 32)
    for column in (0, 1):
        for r in range(8):
            h = pair_rows(f, 8 * column + r, k)
            for n in range(4):
                i = r + 8 * n
                v = flagged[32 * column + i]
                h_n = jnp.where(v > 1e29, DEAD, roll(h, (128 - 32 * n + 96 * odd) % 128))
                rows = pl.ds(i * 64 + 32 * column, 32)
                tile[rows, :] = jnp.where(halo, h_n, roll(v, 32 + 64 * odd))
    for n in range(4):
        v = tile[n * 512 : n * 512 + 512, :]
        t = tmul(jnp.where(v > 1e29, 0.0, v), tw[0])
        tile[n * 512 : n * 512 + 512, :] = jnp.where(v > 1e29, DEAD, t)
    even = even_place("il")
    encode(blocks(tile, 64 * even), lo, 64, True)
    encode(blocks(tile, 64 - 64 * even), hi, 64, True)


def edge_kernel(tile, fa, fb, ma, mb, s):
    even = even_place("il")
    for f, base in ((fa, 48 * even), (fb, 48 - 48 * even)):
        k = scale_of(f, 64)

        def take(i, c, f=f, k=k, base=base):
            s[at(base + i, 16), :] = decode(f, 4 * i, k, True)
            s[at(64 + base + i, 16), :] = decode(f, 4 * i + 3, k, True)
            return c

        lax.fori_loop(0, 16, take, 0, unroll=8)

    def copy(i, c):
        s[at(16 + i, 16), :] = tile[at(4 * i, 16), :]
        s[at(80 + i, 16), :] = tile[at(4 * i + 3, 16), :]
        return c

    lax.fori_loop(0, 32, copy, 0, unroll=8)
    even = even_place("xl", 2)
    encode(blocks(s, 64 * even), ma, 64, True)
    encode(blocks(s, 64 - 64 * even), mb, 64, True)


def one_window(s, cnt, levels, tile, f0, f3, rim, tj, sw, put, R, Z, Y):
    k = scale_of(rim, 64)
    start = pl.multiple_of(16 - 16 * s, 16)
    edge = pl.ds(pl.multiple_of(48 * s, 16), 16)

    def side(i, c):
        R[i, edge, :] = decode(rim, i, k, True)
        return c

    lax.fori_loop(0, 64, side, 0, unroll=8)
    il_even = even_place("il")
    for f, base in ((f0, 48 * il_even), (f3, 48 - 48 * il_even)):
        k = scale_of(f, 64)

        def take(i, c, f=f, k=k, base=base):
            for x in range(3):
                columns = pl.ds(pl.multiple_of(start + 16 * x, 16), 16)
                R[base + i, columns, :] = decode(f, 4 * i + s + x, k, True)
            return c

        lax.fori_loop(0, 16, take, 0, unroll=4)

    def copy(i, c):
        R[16 + i, pl.ds(start, 48), :] = tile[pl.ds(pl.multiple_of(i * 64 + 16 * s, 16), 48), :]
        return c

    lax.fori_loop(0, 32, copy, 0, unroll=8)
    position = lax.axis_index("xl")
    odd = lax.rem(position, 2)

    def put_rows(n, v):
        for q in range(C):
            i = n * C + q
            put(i, v[:, q * 128 : q * 128 + 128] * (tj[...] * tj[pl.ds(i, 1), :]))

    count = cnt[0, odd, position - odd + s]
    windows(count, R, Z, Y, put_rows, lambda q: levels[q].astype(f32) * 0.001, sw)


def window_kernel(second, cnt, levels, tile, f0, f3, rim, tj, sw, code, out, R, Z, Y):
    even = even_place("xl", 2)
    s = 1 - even if second else even

    def put(i, t):
        out[i] = t

    one_window(s, cnt, levels, tile, f0, f3, rim, tj, sw, put, R, Z, Y)
    edge = pl.ds(pl.multiple_of(48 * s, 16), 16)
    encode(lambda i: out[i, edge, :], code, 64, False)


def fold_row(first, second, p, fa, fb, ka, kb, even, dst, r):
    a, b = decode(fa, p, ka), decode(fb, p, kb)
    low = jnp.where(even > 0, second[p, 16:32, :] + b, first[p, 16:32, :] + a)
    high = jnp.where(even > 0, first[p, 32:48, :] + a, second[p, 32:48, :] + b)
    dst[at(4 * r, 16), :] = low
    dst[pl.ds(pl.multiple_of(r * 64 + 16, 16), 32), :] = (
        first[p, pl.ds(pl.multiple_of(32 - 32 * even, 32), 32), :]
        + second[p, pl.ds(pl.multiple_of(32 * even, 32), 32), :]
    )
    dst[at(4 * r + 3, 16), :] = high


def fold_kernel(w1, w2, fa, fb, ma, mb, s):
    even = even_place("xl", 2)
    ka, kb = scale_of(fa, 64), scale_of(fb, 64)
    for first, base in ((0, 0), (48, 16)):

        def add(i, c, first=first, base=base):
            fold_row(w1, w2, first + i, fa, fb, ka, kb, even, s, base + i)
            return c

        lax.fori_loop(0, 16, add, 0, unroll=8)
    il_even = even_place("il")
    encode(blocks(s, 64 * il_even), ma, 64, False)
    encode(blocks(s, 64 - 64 * il_even), mb, 64, False)


def inner_kernel(w1, w2, fa, fb, inner):
    even = even_place("xl", 2)
    ka, kb = scale_of(fa, 64), scale_of(fb, 64)

    def add(i, c):
        fold_row(w1, w2, 16 + i, fa, fb, ka, kb, even, inner, i)
        return c

    lax.fori_loop(0, 32, add, 0, unroll=8)


def narrow_kernel(inner, fa, fb, tt, tw, own, other, out, s, sv):
    odd = parity()
    q = lane_quarter()
    even = even_place("il")
    for f, base in ((fa, 64 * even), (fb, 64 - 64 * even)):
        k = scale_of(f, 64)
        for b in range(64):
            sv[at(base + b, 16), :] = inner[at(base + b, 16), :] + decode(f, b, k)
    for n in range(4):
        sv[n * 512 : n * 512 + 512, :] = tmul(sv[n * 512 : n * 512 + 512, :], tw[1]) * tt[0:1, :]
    for column in (0, 1):
        for r in range(8):
            parts = []
            for n in range(4):
                v = sv[pl.ds((r + 8 * n) * 64 + 32 * column, 32), :]
                parts.append(roll(v, (32 * n + 32 * odd) % 128))
            s[pl.ds(256 * column + 32 * r, 32), :] = spread(parts, q)
    for i in range(32):
        own[i] = sv[pl.ds(pl.multiple_of(i * 64 + 32 * odd, 32), 32), :]
        other[i] = sv[pl.ds(pl.multiple_of(i * 64 + 32 - 32 * odd, 32), 32), :]
    encode(blocks(s), out, 32, False)


def last_kernel(own, other, fa, fb, out, rows, sem):
    odd = parity()
    q = lane_quarter()
    low, high = 3 - 3 * odd, 3 * odd
    ka, kb = scale_of(fa, 32), scale_of(fb, 32)
    copies = []
    for n in range(4):
        for r in range(8):
            a, b = pair_rows(fa, 8 * odd + r, ka), pair_rows(fb, 8 * odd + r, kb)
            i = r + 8 * n
            v = jnp.where(q == low, roll(a, (224 - 32 * n + 32 * odd) % 128), roll(own[i], (96 + 64 * odd) % 128))
            w = jnp.where(q == high, roll(b, (256 - 32 * n + 96 * odd) % 128), roll(other[i], (32 + 64 * odd) % 128))
            rows[i] = v + w
        copies.append(pltpu.make_async_copy(rows.at[pl.ds(8 * n, 8)], out.at[pl.ds(8 * n, 8)], sem.at[n]))
        copies[-1].start()
    for copy in copies:
        copy.wait()


V = pl.BlockSpec(memory_space=pltpu.VMEM)
S = pl.BlockSpec(memory_space=pltpu.SMEM)
H = pl.BlockSpec(memory_space=pltpu.HBM)
SEM = pltpu.SemaphoreType.DMA


def call(kernel, name, mib, outs, scratch, specs, *args, cost=None, out_spec=V):
    shapes = [jax.ShapeDtypeStruct(s, t) for s, t in outs]
    args = [pltpu.with_memory_space_constraint(a, pltpu.HBM) if p is H else a for a, p in zip(args, specs)]
    return pl.pallas_call(
        kernel,
        out_shape=shapes,
        in_specs=specs,
        out_specs=[out_spec] * len(outs),
        scratch_shapes=[pltpu.VMEM(s, f32) if isinstance(s, tuple) else s for s in scratch],
        compiler_params=pltpu.CompilerParams(vmem_limit_bytes=mib * 1024 * 1024),
        name=name,
        cost_estimate=cost,
    )(*args)


def exchange(first, second, axis, step):
    count = lax.axis_size(axis)
    rounds = []
    for start in (0, step):
        up = [(i, i + step) for i in range(count - step) if i // step % 2 == start // step]
        rounds.append(up + [(b, a) for a, b in up])
    return lax.ppermute(first, axis, rounds[0]), lax.ppermute(second, axis, rounds[1])


def swap_pair(x):
    return lax.ppermute(x, "xl", [(i, i ^ 1) for i in range(lax.axis_size("xl"))])


def exchange_time(x):
    nx, nt = lax.axis_size("xl"), lax.axis_size("ta")
    pairs = []
    for x_at in range(nx):
        for t in range(nt):
            other = t + (-1 if x_at % 2 == 0 else 1)
            if 0 <= other < nt:
                pairs.append((x_at * nt + t, (x_at ^ 1) * nt + other))
    return lax.ppermute(x, ("xl", "ta"), pairs)


def codes(n):
    return ((n * 16 + 16, 128), i16)


def taper(order):
    return np.sin(np.pi * (np.arange(order) + 0.5) / order) ** 2


TILE = ((32, 32, 128), f32)


def shards(traces, live, counts, levels):
    tw, sw = tables()
    tj = jnp.asarray(np.broadcast_to(taper(64)[:, None], (64, 128)).astype(np.float32))
    tt = jnp.asarray(np.broadcast_to(taper(128)[None, :], (8, 128)).astype(np.float32))
    tw, sw = jnp.asarray(tw), jnp.asarray(sw)
    traces_other, live_other = swap_pair(traces), swap_pair(live)
    own, tw, tt = call(
        load_kernel,
        "load",
        4,
        [TILE, ((2, 256, 256), bf16), ((8, 128), f32)],
        [(32, 32, 128), pltpu.VMEM((32, 32), i32), SEM((4,))],
        [H] * 4,
        traces,
        live,
        tw,
        tt,
        cost=pl.CostEstimate(flops=1000000, bytes_accessed=6000000, transcendentals=0),
    )
    flagged, msg = call(
        pack_kernel,
        "pack",
        6,
        [((64, 32, 128), f32), codes(32)],
        [(512, 128)],
        [V] * 3,
        own,
        traces_other,
        live_other,
    )
    msg = exchange_time(msg)
    tile, lo, hi = call(
        widen_kernel,
        "widen",
        6,
        [((2048, 128), f32), codes(64), codes(64)],
        [],
        [V] * 3,
        flagged,
        msg,
        tw,
    )
    f0, f3 = exchange(lo, hi, "il", 1)
    lo, hi = call(edge_kernel, "edge", 6, [codes(64)] * 2, [(2048, 128)], [V] * 3, tile, f0, f3)
    fa, fb = exchange(lo, hi, "xl", 2)
    cost = pl.CostEstimate(flops=8000000000, bytes_accessed=30000000, transcendentals=0)
    shared = (counts.transpose(0, 2, 1), levels, tile, f0, f3)
    scratch = [(64, 64, 128)] * 3
    specs = [S, S] + [V] * 6
    outs = [codes(64), ((64, 64, 128), f32)]
    kernels = [functools.partial(window_kernel, n) for n in (False, True)]
    lo, w1 = call(kernels[0], "first", 16, outs, scratch, specs, *shared, fa, tj, sw, cost=cost)
    hi, w2 = call(kernels[1], "second", 16, outs, scratch, specs, *shared, fb, tj, sw, cost=cost)
    lo, hi = lax.optimization_barrier((lo, hi))
    fa, fb = exchange(lo, hi, "xl", 2)
    lo, hi = call(fold_kernel, "fold", 8, [codes(64)] * 2, [(2048, 128)], [V] * 4, w1, w2, fa, fb)
    cost = pl.CostEstimate(flops=1000000, bytes_accessed=4000000, transcendentals=0)
    inner = call(inner_kernel, "inner", 4, [((2048, 128), f32)], [], [V] * 4, w1, w2, fa, fb, cost=cost)[0]
    fa, fb = exchange(lo, hi, "il", 1)
    own, other, msg = call(
        narrow_kernel,
        "narrow",
        8,
        [TILE, TILE, codes(32)],
        [(512, 128), (2048, 128)],
        [V] * 5,
        inner,
        fa,
        fb,
        tt,
        tw,
    )
    msg = exchange_time(msg)
    other, msg_other = swap_pair(other), swap_pair(msg)
    return call(
        last_kernel, "last", 4, [TILE], [(32, 32, 128), SEM((4,))], [V] * 4, own, other, msg_other, msg, out_spec=H
    )[0]


def solution(mesh):
    placed = (P("il", "xl", "ta"), P("il", "xl"), P("il", None, "ta"), P())
    return jax.shard_map(
        shards, mesh=mesh, in_specs=placed, out_specs=P("il", "xl", "ta"), check_vma=False
    )
```

```python
import functools

import jax
import jax.numpy as jnp
import numpy as np
from jax import lax
from jax.experimental import pallas as pl
from jax.experimental.pallas import tpu as pltpu
from jax.sharding import PartitionSpec as P

f32=jnp.float32; bf16=jnp.bfloat16
DEAD=1e30
def dct(n):
    k=np.arange(n)[:,None]; j=np.arange(n)[None,:]
    c=np.sqrt(2.0/n)*np.cos(np.pi*(2*j+1)*k/(2*n)); c[0]*=np.sqrt(0.5); return c
def two(c):
    hi=np.asarray(c,np.float32).astype(jnp.bfloat16); lo=(c-hi.astype(np.float64)).astype(np.float32).astype(jnp.bfloat16)
    return hi,lo
def time_w(c):
    hi,lo=two(c)
    return np.concatenate([np.concatenate([hi,hi],0),np.concatenate([lo,np.zeros_like(lo)],0)],1)
def space_w(c):
    hi,lo=two(c)
    return np.concatenate([np.concatenate([hi,hi],1),np.concatenate([lo,np.zeros_like(lo)],1)],0)
def tables():
    ct=dct(128); cs=dct(64)
    tw=np.stack([time_w(ct.T),time_w(ct)])
    sw=np.stack([space_w(cs),space_w(cs.T)])
    return tw,sw
def split(x):
    hi=x.astype(bf16); return hi,(x-hi.astype(f32)).astype(bf16)
def tmul(x,w):
    hi,lo=split(x)
    y=jnp.dot(jnp.concatenate([hi,lo],1),w,preferred_element_type=f32)
    return y[:,:128]+y[:,128:]
def smul(x,w):
    hi,lo=split(x)
    y=jnp.dot(w,jnp.concatenate([hi,lo],0),preferred_element_type=f32)
    return y[:64]+y[64:]
def swap(x,n):
    y=jnp.stack([x[:,128*q:128*q+128] for q in range(n)],0)
    return jnp.swapaxes(y,0,1)


C = 32


def load_chunk(ref, n):
    return jnp.concatenate([ref[n * C + q] for q in range(C)], 1)


def windows(count, R, Z, Y, put, threshold, sw):
    def own(n):
        return jnp.concatenate([R[n * C + q] for q in range(C)], 1)

    def forth(x, n):
        Z[:, pl.ds(pl.multiple_of(n * C, C), C), :] = swap(smul(x, sw[0]), C)

    def back(n):
        w = own(n)
        return jnp.where(w > 1e29, smul(load_chunk(Y, n), sw[1]), w)

    def first(n, c):
        w = own(n)
        forth(jnp.where(w > 1e29, 0.0, w), n)
        return c

    def shrink(q):
        t = threshold(q)

        def f(n, c):
            u = smul(load_chunk(Z, n), sw[0])
            u = u - jnp.clip(u, -t, t)
            Y[:, pl.ds(pl.multiple_of(n * C, C), C), :] = swap(smul(u, sw[1]), C)
            return c

        lax.fori_loop(0, 64 // C, f, 0, unroll=True)

    def again(n, c):
        forth(back(n), n)
        return c

    def step(q, c):
        shrink(q)
        lax.fori_loop(0, 64 // C, again, 0, unroll=True)
        return c

    def last(n, c):
        put(n, back(n))
        return c

    lax.fori_loop(0, 64 // C, first, 0, unroll=True)
    lax.fori_loop(0, count - 1, step, 0)
    shrink(count - 1)
    lax.fori_loop(0, 64 // C, last, 0, unroll=True)


Q = 32000.0
LN = float(np.log(2.0) / 128.0)
i32 = jnp.int32
i16 = jnp.int16


def parity():
    return lax.rem(lax.axis_index("xl"), 2)


def even_place(axis, step=1):
    return 1 - lax.rem(lax.axis_index(axis) // step, 2)


def roll(x, s):
    if isinstance(s, int):
        s %= 128
        if s == 0:
            return x
    return pltpu.roll(x, s, 1)


def at(b, n):
    return pl.ds(pl.multiple_of(b * n, n), n)


def encode(get, dst, n, flagged, un=8):
    def top(b, m):
        x = get(b)
        a = jnp.abs(x)
        if flagged:
            a = jnp.where(x > 1e29, 0.0, a)
        return jnp.maximum(m, a)

    m = lax.fori_loop(0, n, top, jnp.full((16, 128), 1e-30, f32), unroll=un)
    code = jnp.ceil(jnp.log(m) * (1.0 / LN))
    scale = Q * jnp.exp(code * -LN)

    def put(b, c):
        x = get(b)
        q = jnp.round(x * scale)
        if flagged:
            q = jnp.where(x > 1e29, 0.0, jnp.where(q >= 0, q + 1.0, q))
        dst[at(b, 16), :] = q.astype(i32).astype(i16)
        return c

    lax.fori_loop(0, n, put, 0, unroll=un)
    dst[pl.ds(n * 16, 16), :] = code.astype(i32).astype(i16)


def blocks(ref, first=0):
    return lambda b: ref[at(b + first, 16), :]


def scale_of(ref, n):
    return jnp.exp(ref[pl.ds(n * 16, 16), :].astype(i32).astype(f32) * LN) * (1.0 / Q)


def decode(ref, b, scale, flagged=False):
    q = ref[at(b, 16), :].astype(i32).astype(f32)
    if flagged:
        return jnp.where(q == 0, DEAD, (q - jnp.where(q > 0, 1.0, 0.0)) * scale)
    return q * scale


def pair_rows(ref, r, scale):
    return jnp.concatenate([decode(ref, 2 * r + h, scale) for h in (0, 1)], 0)


def spread(parts, q):
    out = parts[3]
    for n in (2, 1, 0):
        out = jnp.where(q == n, parts[n], out)
    return out


def lane_quarter():
    return lax.broadcasted_iota(i32, (32, 128), 1) // 32


def load_kernel(x_hbm, live_hbm, tw_hbm, tt_hbm, own, tw, tt, x, live, sem):
    pairs = ((live_hbm, live), (x_hbm, x), (tw_hbm, tw), (tt_hbm, tt))
    copies = [pltpu.make_async_copy(a, b, sem.at[n]) for n, (a, b) in enumerate(pairs)]
    for copy in copies:
        copy.start()
    copies[0].wait()
    copies[1].wait()
    lt = live[...].astype(f32).T
    for i in range(32):
        own[i] = jnp.where(jnp.broadcast_to(lt[:, i : i + 1], (32, 128)) > 0.5, x[i], DEAD)
    copies[2].wait()
    copies[3].wait()


def pack_kernel(own, x_other, live_other, flagged, out, s):
    odd = parity()
    q = lane_quarter()
    lt = live_other[...].astype(f32).T
    for mine in (True, False):
        column = odd if mine else 1 - odd
        for r in range(8):
            x = []
            for i in (r, r + 8, r + 16, r + 24):
                if mine:
                    v = own[i]
                else:
                    alive = jnp.broadcast_to(lt[:, i : i + 1], (32, 128)) > 0.5
                    v = jnp.where(alive, x_other[i], DEAD)
                flagged[32 * column + i] = v
                x.append(jnp.where(v > 1e29, 0.0, v))
            s[pl.ds(pl.multiple_of(256 * column + 32 * r, 32), 32), :] = spread(
                [roll(v, (32 * n + 32 * odd) % 128) for n, v in enumerate(x)], q
            )
    encode(blocks(s), out, 32, False)


def widen_kernel(flagged, f, tw, tile, lo, hi):
    odd = parity()
    halo = lane_quarter() == 3 * odd
    k = scale_of(f, 32)
    for column in (0, 1):
        for r in range(8):
            h = pair_rows(f, 8 * column + r, k)
            for n in range(4):
                i = r + 8 * n
                v = flagged[32 * column + i]
                h_n = jnp.where(v > 1e29, DEAD, roll(h, (128 - 32 * n + 96 * odd) % 128))
                rows = pl.ds(i * 64 + 32 * column, 32)
                tile[rows, :] = jnp.where(halo, h_n, roll(v, 32 + 64 * odd))
    for n in range(4):
        v = tile[n * 512 : n * 512 + 512, :]
        t = tmul(jnp.where(v > 1e29, 0.0, v), tw[0])
        tile[n * 512 : n * 512 + 512, :] = jnp.where(v > 1e29, DEAD, t)
    even = even_place("il")
    encode(blocks(tile, 64 * even), lo, 64, True)
    encode(blocks(tile, 64 - 64 * even), hi, 64, True)


def edge_kernel(tile, fa, fb, ma, mb, s):
    even = even_place("il")
    for f, base in ((fa, 48 * even), (fb, 48 - 48 * even)):
        k = scale_of(f, 64)

        def take(i, c, f=f, k=k, base=base):
            s[at(base + i, 16), :] = decode(f, 4 * i, k, True)
            s[at(64 + base + i, 16), :] = decode(f, 4 * i + 3, k, True)
            return c

        lax.fori_loop(0, 16, take, 0, unroll=8)

    def copy(i, c):
        s[at(16 + i, 16), :] = tile[at(4 * i, 16), :]
        s[at(80 + i, 16), :] = tile[at(4 * i + 3, 16), :]
        return c

    lax.fori_loop(0, 32, copy, 0, unroll=8)
    even = even_place("xl", 2)
    encode(blocks(s, 64 * even), ma, 64, True)
    encode(blocks(s, 64 - 64 * even), mb, 64, True)


def one_window(s, cnt, levels, tile, f0, f3, rim, tj, sw, put, R, Z, Y):
    k = scale_of(rim, 64)
    start = pl.multiple_of(16 - 16 * s, 16)
    edge = pl.ds(pl.multiple_of(48 * s, 16), 16)

    def side(i, c):
        R[i, edge, :] = decode(rim, i, k, True)
        return c

    lax.fori_loop(0, 64, side, 0, unroll=8)
    il_even = even_place("il")
    for f, base in ((f0, 48 * il_even), (f3, 48 - 48 * il_even)):
        k = scale_of(f, 64)

        def take(i, c, f=f, k=k, base=base):
            for x in range(3):
                columns = pl.ds(pl.multiple_of(start + 16 * x, 16), 16)
                R[base + i, columns, :] = decode(f, 4 * i + s + x, k, True)
            return c

        lax.fori_loop(0, 16, take, 0, unroll=4)

    def copy(i, c):
        R[16 + i, pl.ds(start, 48), :] = tile[pl.ds(pl.multiple_of(i * 64 + 16 * s, 16), 48), :]
        return c

    lax.fori_loop(0, 32, copy, 0, unroll=8)
    position = lax.axis_index("xl")
    odd = lax.rem(position, 2)

    def put_rows(n, v):
        for q in range(C):
            i = n * C + q
            put(i, v[:, q * 128 : q * 128 + 128] * (tj[...] * tj[pl.ds(i, 1), :]))

    count = cnt[0, odd, position - odd + s]
    windows(count, R, Z, Y, put_rows, lambda q: levels[q].astype(f32) * 0.001, sw)


def window_kernel(second, cnt, levels, tile, f0, f3, rim, tj, sw, code, out, R, Z, Y):
    even = even_place("xl", 2)
    s = 1 - even if second else even

    def put(i, t):
        out[i] = t

    one_window(s, cnt, levels, tile, f0, f3, rim, tj, sw, put, R, Z, Y)
    edge = pl.ds(pl.multiple_of(48 * s, 16), 16)
    encode(lambda i: out[i, edge, :], code, 64, False)


def fold_row(first, second, p, fa, fb, ka, kb, even, dst, r):
    a, b = decode(fa, p, ka), decode(fb, p, kb)
    low = jnp.where(even > 0, second[p, 16:32, :] + b, first[p, 16:32, :] + a)
    high = jnp.where(even > 0, first[p, 32:48, :] + a, second[p, 32:48, :] + b)
    dst[at(4 * r, 16), :] = low
    dst[pl.ds(pl.multiple_of(r * 64 + 16, 16), 32), :] = (
        first[p, pl.ds(pl.multiple_of(32 - 32 * even, 32), 32), :]
        + second[p, pl.ds(pl.multiple_of(32 * even, 32), 32), :]
    )
    dst[at(4 * r + 3, 16), :] = high


def fold_kernel(w1, w2, fa, fb, ma, mb, s):
    even = even_place("xl", 2)
    ka, kb = scale_of(fa, 64), scale_of(fb, 64)
    for first, base in ((0, 0), (48, 16)):

        def add(i, c, first=first, base=base):
            fold_row(w1, w2, first + i, fa, fb, ka, kb, even, s, base + i)
            return c

        lax.fori_loop(0, 16, add, 0, unroll=8)
    il_even = even_place("il")
    encode(blocks(s, 64 * il_even), ma, 64, False)
    encode(blocks(s, 64 - 64 * il_even), mb, 64, False)


def inner_kernel(w1, w2, fa, fb, inner):
    even = even_place("xl", 2)
    ka, kb = scale_of(fa, 64), scale_of(fb, 64)

    def add(i, c):
        fold_row(w1, w2, 16 + i, fa, fb, ka, kb, even, inner, i)
        return c

    lax.fori_loop(0, 32, add, 0, unroll=8)


def narrow_kernel(inner, fa, fb, tt, tw, own, other, out, s, sv):
    odd = parity()
    q = lane_quarter()
    even = even_place("il")
    for f, base in ((fa, 64 * even), (fb, 64 - 64 * even)):
        k = scale_of(f, 64)
        for b in range(64):
            sv[at(base + b, 16), :] = inner[at(base + b, 16), :] + decode(f, b, k)
    for n in range(4):
        sv[n * 512 : n * 512 + 512, :] = tmul(sv[n * 512 : n * 512 + 512, :], tw[1]) * tt[0:1, :]
    for column in (0, 1):
        for r in range(8):
            parts = []
            for n in range(4):
                v = sv[pl.ds((r + 8 * n) * 64 + 32 * column, 32), :]
                parts.append(roll(v, (32 * n + 32 * odd) % 128))
            s[pl.ds(256 * column + 32 * r, 32), :] = spread(parts, q)
    for i in range(32):
        own[i] = sv[pl.ds(pl.multiple_of(i * 64 + 32 * odd, 32), 32), :]
        other[i] = sv[pl.ds(pl.multiple_of(i * 64 + 32 - 32 * odd, 32), 32), :]
    encode(blocks(s), out, 32, False)


def last_kernel(own, other, fa, fb, out, rows, sem):
    odd = parity()
    q = lane_quarter()
    low, high = 3 - 3 * odd, 3 * odd
    ka, kb = scale_of(fa, 32), scale_of(fb, 32)
    copies = []
    for n in range(4):
        for r in range(8):
            a, b = pair_rows(fa, 8 * odd + r, ka), pair_rows(fb, 8 * odd + r, kb)
            i = r + 8 * n
            v = jnp.where(q == low, roll(a, (224 - 32 * n + 32 * odd) % 128), roll(own[i], (96 + 64 * odd) % 128))
            w = jnp.where(q == high, roll(b, (256 - 32 * n + 96 * odd) % 128), roll(other[i], (32 + 64 * odd) % 128))
            rows[i] = v + w
        copies.append(pltpu.make_async_copy(rows.at[pl.ds(8 * n, 8)], out.at[pl.ds(8 * n, 8)], sem.at[n]))
        copies[-1].start()
    for copy in copies:
        copy.wait()


V = pl.BlockSpec(memory_space=pltpu.VMEM)
S = pl.BlockSpec(memory_space=pltpu.SMEM)
H = pl.BlockSpec(memory_space=pltpu.HBM)
SEM = pltpu.SemaphoreType.DMA


def call(kernel, name, mib, outs, scratch, specs, *args, cost=None, out_spec=V):
    shapes = [jax.ShapeDtypeStruct(s, t) for s, t in outs]
    args = [pltpu.with_memory_space_constraint(a, pltpu.HBM) if p is H else a for a, p in zip(args, specs)]
    return pl.pallas_call(
        kernel,
        out_shape=shapes,
        in_specs=specs,
        out_specs=[out_spec] * len(outs),
        scratch_shapes=[pltpu.VMEM(s, f32) if isinstance(s, tuple) else s for s in scratch],
        compiler_params=pltpu.CompilerParams(vmem_limit_bytes=mib * 1024 * 1024),
        name=name,
        cost_estimate=cost,
    )(*args)


def exchange(first, second, axis, step):
    count = lax.axis_size(axis)
    rounds = []
    for start in (0, step):
        up = [(i, i + step) for i in range(count - step) if i // step % 2 == start // step]
        rounds.append(up + [(b, a) for a, b in up])
    return lax.ppermute(first, axis, rounds[0]), lax.ppermute(second, axis, rounds[1])


def swap_pair(x):
    return lax.ppermute(x, "xl", [(i, i ^ 1) for i in range(lax.axis_size("xl"))])


def exchange_time(x):
    nx, nt = lax.axis_size("xl"), lax.axis_size("ta")
    pairs = []
    for x_at in range(nx):
        for t in range(nt):
            other = t + (-1 if x_at % 2 == 0 else 1)
            if 0 <= other < nt:
                pairs.append((x_at * nt + t, (x_at ^ 1) * nt + other))
    return lax.ppermute(x, ("xl", "ta"), pairs)


def codes(n):
    return ((n * 16 + 16, 128), i16)


def taper(order):
    return np.sin(np.pi * (np.arange(order) + 0.5) / order) ** 2


TILE = ((32, 32, 128), f32)


def shards(traces, live, counts, levels):
    tw, sw = tables()
    tj = jnp.asarray(np.broadcast_to(taper(64)[:, None], (64, 128)).astype(np.float32))
    tt = jnp.asarray(np.broadcast_to(taper(128)[None, :], (8, 128)).astype(np.float32))
    tw, sw = jnp.asarray(tw), jnp.asarray(sw)
    traces_other, live_other = swap_pair(traces), swap_pair(live)
    own, tw, tt = call(
        load_kernel,
        "load",
        4,
        [TILE, ((2, 256, 256), bf16), ((8, 128), f32)],
        [(32, 32, 128), pltpu.VMEM((32, 32), i32), SEM((4,))],
        [H] * 4,
        traces,
        live,
        tw,
        tt,
        cost=pl.CostEstimate(flops=1000000, bytes_accessed=6000000, transcendentals=0),
    )
    flagged, msg = call(
        pack_kernel,
        "pack",
        6,
        [((64, 32, 128), f32), codes(32)],
        [(512, 128)],
        [V] * 3,
        own,
        traces_other,
        live_other,
    )
    msg = exchange_time(msg)
    tile, lo, hi = call(
        widen_kernel,
        "widen",
        6,
        [((2048, 128), f32), codes(64), codes(64)],
        [],
        [V] * 3,
        flagged,
        msg,
        tw,
    )
    f0, f3 = exchange(lo, hi, "il", 1)
    lo, hi = call(edge_kernel, "edge", 6, [codes(64)] * 2, [(2048, 128)], [V] * 3, tile, f0, f3)
    fa, fb = exchange(lo, hi, "xl", 2)
    cost = pl.CostEstimate(flops=8000000000, bytes_accessed=30000000, transcendentals=0)
    shared = (counts.transpose(0, 2, 1), levels, tile, f0, f3)
    scratch = [(64, 64, 128)] * 3
    specs = [S, S] + [V] * 6
    outs = [codes(64), ((64, 64, 128), f32)]
    kernels = [functools.partial(window_kernel, n) for n in (False, True)]
    lo, w1 = call(kernels[0], "first", 16, outs, scratch, specs, *shared, fa, tj, sw, cost=cost)
    tj_after, lo = lax.optimization_barrier((tj, lo))
    hi, w2 = call(kernels[1], "second", 16, outs, scratch, specs, *shared, fb, tj_after, sw, cost=cost)
    lo, hi = lax.optimization_barrier((lo, hi))
    fa, fb = exchange(lo, hi, "xl", 2)
    lo, hi = call(fold_kernel, "fold", 8, [codes(64)] * 2, [(2048, 128)], [V] * 4, w1, w2, fa, fb)
    cost = pl.CostEstimate(flops=1000000, bytes_accessed=4000000, transcendentals=0)
    inner = call(inner_kernel, "inner", 4, [((2048, 128), f32)], [], [V] * 4, w1, w2, fa, fb, cost=cost)[0]
    fa, fb = exchange(lo, hi, "il", 1)
    own, other, msg = call(
        narrow_kernel,
        "narrow",
        8,
        [TILE, TILE, codes(32)],
        [(512, 128), (2048, 128)],
        [V] * 5,
        inner,
        fa,
        fb,
        tt,
        tw,
    )
    msg = exchange_time(msg)
    other, msg_other = swap_pair(other), swap_pair(msg)
    return call(
        last_kernel, "last", 4, [TILE], [(32, 32, 128), SEM((4,))], [V] * 4, own, other, msg_other, msg, out_spec=H
    )[0]


def solution(mesh):
    placed = (P("il", "xl", "ta"), P("il", "xl"), P("il", None, "ta"), P())
    return jax.shard_map(
        shards, mesh=mesh, in_specs=placed, out_specs=P("il", "xl", "ta"), check_vma=False
    )
```

```python
import functools

import jax
import jax.numpy as jnp
import numpy as np
from jax import lax
from jax.experimental import pallas as pl
from jax.experimental.pallas import tpu as pltpu
from jax.sharding import PartitionSpec as P

f32=jnp.float32; bf16=jnp.bfloat16
DEAD=1e30
def dct(n):
    k=np.arange(n)[:,None]; j=np.arange(n)[None,:]
    c=np.sqrt(2.0/n)*np.cos(np.pi*(2*j+1)*k/(2*n)); c[0]*=np.sqrt(0.5); return c
def two(c):
    hi=np.asarray(c,np.float32).astype(jnp.bfloat16); lo=(c-hi.astype(np.float64)).astype(np.float32).astype(jnp.bfloat16)
    return hi,lo
def time_w(c):
    hi,lo=two(c)
    return np.concatenate([np.concatenate([hi,hi],0),np.concatenate([lo,np.zeros_like(lo)],0)],1)
def space_w(c):
    hi,lo=two(c)
    return np.concatenate([np.concatenate([hi,hi],1),np.concatenate([lo,np.zeros_like(lo)],1)],0)
def tables():
    ct=dct(128); cs=dct(64)
    tw=np.stack([time_w(ct.T),time_w(ct)])
    sw=np.stack([space_w(cs),space_w(cs.T)])
    return tw,sw
def split(x):
    hi=x.astype(bf16); return hi,(x-hi.astype(f32)).astype(bf16)
def tmul(x,w):
    hi,lo=split(x)
    y=jnp.dot(jnp.concatenate([hi,lo],1),w,preferred_element_type=f32)
    return y[:,:128]+y[:,128:]
def smul(x,w):
    hi,lo=split(x)
    y=jnp.dot(w,jnp.concatenate([hi,lo],0),preferred_element_type=f32)
    return y[:64]+y[64:]
def swap(x,n):
    y=jnp.stack([x[:,128*q:128*q+128] for q in range(n)],0)
    return jnp.swapaxes(y,0,1)


C = 32


def load_chunk(ref, n):
    return jnp.concatenate([ref[n * C + q] for q in range(C)], 1)


def windows(count, R, Z, Y, put, threshold, sw):
    def own(n):
        return jnp.concatenate([R[n * C + q] for q in range(C)], 1)

    def forth(x, n):
        Z[:, pl.ds(pl.multiple_of(n * C, C), C), :] = swap(smul(x, sw[0]), C)

    def back(n):
        w = own(n)
        return jnp.where(w > 1e29, smul(load_chunk(Y, n), sw[1]), w)

    def first(n, c):
        w = own(n)
        forth(jnp.where(w > 1e29, 0.0, w), n)
        return c

    def shrink(q):
        t = threshold(q)

        def f(n, c):
            u = smul(load_chunk(Z, n), sw[0])
            u = u - jnp.clip(u, -t, t)
            Y[:, pl.ds(pl.multiple_of(n * C, C), C), :] = swap(smul(u, sw[1]), C)
            return c

        lax.fori_loop(0, 64 // C, f, 0, unroll=True)

    def again(n, c):
        forth(back(n), n)
        return c

    def step(q, c):
        shrink(q)
        lax.fori_loop(0, 64 // C, again, 0, unroll=True)
        return c

    def last(n, c):
        put(n, back(n))
        return c

    lax.fori_loop(0, 64 // C, first, 0, unroll=True)
    lax.fori_loop(0, count - 1, step, 0)
    shrink(count - 1)
    lax.fori_loop(0, 64 // C, last, 0, unroll=True)


Q = 32000.0
LN = float(np.log(2.0) / 128.0)
i32 = jnp.int32
i16 = jnp.int16


def parity():
    return lax.rem(lax.axis_index("xl"), 2)


def even_place(axis, step=1):
    return 1 - lax.rem(lax.axis_index(axis) // step, 2)


def roll(x, s):
    if isinstance(s, int):
        s %= 128
        if s == 0:
            return x
    return pltpu.roll(x, s, 1)


def at(b, n):
    return pl.ds(pl.multiple_of(b * n, n), n)


def encode(get, dst, n, flagged, un=16):
    def top(b, m):
        x = get(b)
        a = jnp.abs(x)
        if flagged:
            a = jnp.where(x > 1e29, 0.0, a)
        return jnp.maximum(m, a)

    m = lax.fori_loop(0, n, top, jnp.full((16, 128), 1e-30, f32), unroll=un)
    code = jnp.ceil(jnp.log(m) * (1.0 / LN))
    scale = Q * jnp.exp(code * -LN)

    def put(b, c):
        x = get(b)
        q = jnp.round(x * scale)
        if flagged:
            q = jnp.where(x > 1e29, 0.0, jnp.where(q >= 0, q + 1.0, q))
        dst[at(b, 16), :] = q.astype(i32).astype(i16)
        return c

    lax.fori_loop(0, n, put, 0, unroll=un)
    dst[pl.ds(n * 16, 16), :] = code.astype(i32).astype(i16)


def blocks(ref, first=0):
    return lambda b: ref[at(b + first, 16), :]


def scale_of(ref, n):
    return jnp.exp(ref[pl.ds(n * 16, 16), :].astype(i32).astype(f32) * LN) * (1.0 / Q)


def decode(ref, b, scale, flagged=False):
    q = ref[at(b, 16), :].astype(i32).astype(f32)
    if flagged:
        return jnp.where(q == 0, DEAD, (q - jnp.where(q > 0, 1.0, 0.0)) * scale)
    return q * scale


def pair_rows(ref, r, scale):
    return jnp.concatenate([decode(ref, 2 * r + h, scale) for h in (0, 1)], 0)


def spread(parts, q):
    out = parts[3]
    for n in (2, 1, 0):
        out = jnp.where(q == n, parts[n], out)
    return out


def lane_quarter():
    return lax.broadcasted_iota(i32, (32, 128), 1) // 32


def load_kernel(x_hbm, live_hbm, tw_hbm, tt_hbm, own, tw, tt, x, live, sem):
    pairs = ((live_hbm, live), (x_hbm, x), (tw_hbm, tw), (tt_hbm, tt))
    copies = [pltpu.make_async_copy(a, b, sem.at[n]) for n, (a, b) in enumerate(pairs)]
    for copy in copies:
        copy.start()
    copies[0].wait()
    copies[1].wait()
    lt = live[...].astype(f32).T
    for i in range(32):
        own[i] = jnp.where(jnp.broadcast_to(lt[:, i : i + 1], (32, 128)) > 0.5, x[i], DEAD)
    copies[2].wait()
    copies[3].wait()


def pack_kernel(own, x_other, live_other, flagged, out, s):
    odd = parity()
    q = lane_quarter()
    lt = live_other[...].astype(f32).T
    for mine in (True, False):
        column = odd if mine else 1 - odd
        for r in range(8):
            x = []
            for i in (r, r + 8, r + 16, r + 24):
                if mine:
                    v = own[i]
                else:
                    alive = jnp.broadcast_to(lt[:, i : i + 1], (32, 128)) > 0.5
                    v = jnp.where(alive, x_other[i], DEAD)
                flagged[32 * column + i] = v
                x.append(jnp.where(v > 1e29, 0.0, v))
            s[pl.ds(pl.multiple_of(256 * column + 32 * r, 32), 32), :] = spread(
                [roll(v, (32 * n + 32 * odd) % 128) for n, v in enumerate(x)], q
            )
    encode(blocks(s), out, 32, False)


def widen_kernel(flagged, f, tw, tile, lo, hi):
    odd = parity()
    halo = lane_quarter() == 3 * odd
    k = scale_of(f, 32)
    for column in (0, 1):
        for r in range(8):
            h = pair_rows(f, 8 * column + r, k)
            for n in range(4):
                i = r + 8 * n
                v = flagged[32 * column + i]
                h_n = jnp.where(v > 1e29, DEAD, roll(h, (128 - 32 * n + 96 * odd) % 128))
                rows = pl.ds(i * 64 + 32 * column, 32)
                tile[rows, :] = jnp.where(halo, h_n, roll(v, 32 + 64 * odd))
    for n in range(4):
        v = tile[n * 512 : n * 512 + 512, :]
        t = tmul(jnp.where(v > 1e29, 0.0, v), tw[0])
        tile[n * 512 : n * 512 + 512, :] = jnp.where(v > 1e29, DEAD, t)
    even = even_place("il")
    encode(blocks(tile, 64 * even), lo, 64, True)
    encode(blocks(tile, 64 - 64 * even), hi, 64, True)


def edge_kernel(tile, fa, fb, ma, mb, s):
    even = even_place("il")
    for f, base in ((fa, 48 * even), (fb, 48 - 48 * even)):
        k = scale_of(f, 64)

        def take(i, c, f=f, k=k, base=base):
            s[at(base + i, 16), :] = decode(f, 4 * i, k, True)
            s[at(64 + base + i, 16), :] = decode(f, 4 * i + 3, k, True)
            return c

        lax.fori_loop(0, 16, take, 0, unroll=8)

    def copy(i, c):
        s[at(16 + i, 16), :] = tile[at(4 * i, 16), :]
        s[at(80 + i, 16), :] = tile[at(4 * i + 3, 16), :]
        return c

    lax.fori_loop(0, 32, copy, 0, unroll=8)
    even = even_place("xl", 2)
    encode(blocks(s, 64 * even), ma, 64, True)
    encode(blocks(s, 64 - 64 * even), mb, 64, True)


def one_window(s, cnt, levels, tile, f0, f3, rim, tj, sw, put, R, Z, Y):
    k = scale_of(rim, 64)
    start = pl.multiple_of(16 - 16 * s, 16)
    edge = pl.ds(pl.multiple_of(48 * s, 16), 16)

    def side(i, c):
        R[i, edge, :] = decode(rim, i, k, True)
        return c

    lax.fori_loop(0, 64, side, 0, unroll=8)
    il_even = even_place("il")
    for f, base in ((f0, 48 * il_even), (f3, 48 - 48 * il_even)):
        k = scale_of(f, 64)

        def take(i, c, f=f, k=k, base=base):
            for x in range(3):
                columns = pl.ds(pl.multiple_of(start + 16 * x, 16), 16)
                R[base + i, columns, :] = decode(f, 4 * i + s + x, k, True)
            return c

        lax.fori_loop(0, 16, take, 0, unroll=4)

    def copy(i, c):
        R[16 + i, pl.ds(start, 48), :] = tile[pl.ds(pl.multiple_of(i * 64 + 16 * s, 16), 48), :]
        return c

    lax.fori_loop(0, 32, copy, 0, unroll=8)
    position = lax.axis_index("xl")
    odd = lax.rem(position, 2)

    def put_rows(n, v):
        for q in range(C):
            i = n * C + q
            put(i, v[:, q * 128 : q * 128 + 128] * (tj[...] * tj[pl.ds(i, 1), :]))

    count = cnt[0, odd, position - odd + s]
    windows(count, R, Z, Y, put_rows, lambda q: levels[q].astype(f32) * 0.001, sw)


def window_kernel(second, cnt, levels, tile, f0, f3, rim, tj, sw, code, out, R, Z, Y):
    even = even_place("xl", 2)
    s = 1 - even if second else even

    def put(i, t):
        out[i] = t

    one_window(s, cnt, levels, tile, f0, f3, rim, tj, sw, put, R, Z, Y)
    edge = pl.ds(pl.multiple_of(48 * s, 16), 16)
    encode(lambda i: out[i, edge, :], code, 64, False)


def fold_row(first, second, p, fa, fb, ka, kb, even, dst, r):
    a, b = decode(fa, p, ka), decode(fb, p, kb)
    low = jnp.where(even > 0, second[p, 16:32, :] + b, first[p, 16:32, :] + a)
    high = jnp.where(even > 0, first[p, 32:48, :] + a, second[p, 32:48, :] + b)
    dst[at(4 * r, 16), :] = low
    dst[pl.ds(pl.multiple_of(r * 64 + 16, 16), 32), :] = (
        first[p, pl.ds(pl.multiple_of(32 - 32 * even, 32), 32), :]
        + second[p, pl.ds(pl.multiple_of(32 * even, 32), 32), :]
    )
    dst[at(4 * r + 3, 16), :] = high


def fold_kernel(w1, w2, fa, fb, ma, mb, s):
    even = even_place("xl", 2)
    ka, kb = scale_of(fa, 64), scale_of(fb, 64)
    for first, base in ((0, 0), (48, 16)):

        def add(i, c, first=first, base=base):
            fold_row(w1, w2, first + i, fa, fb, ka, kb, even, s, base + i)
            return c

        lax.fori_loop(0, 16, add, 0, unroll=8)
    il_even = even_place("il")
    encode(blocks(s, 64 * il_even), ma, 64, False)
    encode(blocks(s, 64 - 64 * il_even), mb, 64, False)


def inner_kernel(w1, w2, fa, fb, inner):
    even = even_place("xl", 2)
    ka, kb = scale_of(fa, 64), scale_of(fb, 64)

    def add(i, c):
        fold_row(w1, w2, 16 + i, fa, fb, ka, kb, even, inner, i)
        return c

    lax.fori_loop(0, 32, add, 0, unroll=8)


def narrow_kernel(inner, fa, fb, tt, tw, own, other, out, s, sv):
    odd = parity()
    q = lane_quarter()
    even = even_place("il")
    for f, base in ((fa, 64 * even), (fb, 64 - 64 * even)):
        k = scale_of(f, 64)
        for b in range(64):
            sv[at(base + b, 16), :] = inner[at(base + b, 16), :] + decode(f, b, k)
    for n in range(4):
        sv[n * 512 : n * 512 + 512, :] = tmul(sv[n * 512 : n * 512 + 512, :], tw[1]) * tt[0:1, :]
    for column in (0, 1):
        for r in range(8):
            parts = []
            for n in range(4):
                v = sv[pl.ds((r + 8 * n) * 64 + 32 * column, 32), :]
                parts.append(roll(v, (32 * n + 32 * odd) % 128))
            s[pl.ds(256 * column + 32 * r, 32), :] = spread(parts, q)
    for i in range(32):
        own[i] = sv[pl.ds(pl.multiple_of(i * 64 + 32 * odd, 32), 32), :]
        other[i] = sv[pl.ds(pl.multiple_of(i * 64 + 32 - 32 * odd, 32), 32), :]
    encode(blocks(s), out, 32, False)


def last_kernel(own, other, fa, fb, out, rows, sem):
    odd = parity()
    q = lane_quarter()
    low, high = 3 - 3 * odd, 3 * odd
    ka, kb = scale_of(fa, 32), scale_of(fb, 32)
    copies = []
    for n in range(4):
        for r in range(8):
            a, b = pair_rows(fa, 8 * odd + r, ka), pair_rows(fb, 8 * odd + r, kb)
            i = r + 8 * n
            v = jnp.where(q == low, roll(a, (224 - 32 * n + 32 * odd) % 128), roll(own[i], (96 + 64 * odd) % 128))
            w = jnp.where(q == high, roll(b, (256 - 32 * n + 96 * odd) % 128), roll(other[i], (32 + 64 * odd) % 128))
            rows[i] = v + w
        copies.append(pltpu.make_async_copy(rows.at[pl.ds(8 * n, 8)], out.at[pl.ds(8 * n, 8)], sem.at[n]))
        copies[-1].start()
    for copy in copies:
        copy.wait()


V = pl.BlockSpec(memory_space=pltpu.VMEM)
S = pl.BlockSpec(memory_space=pltpu.SMEM)
H = pl.BlockSpec(memory_space=pltpu.HBM)
SEM = pltpu.SemaphoreType.DMA


def call(kernel, name, mib, outs, scratch, specs, *args, cost=None, out_spec=V):
    shapes = [jax.ShapeDtypeStruct(s, t) for s, t in outs]
    args = [pltpu.with_memory_space_constraint(a, pltpu.HBM) if p is H else a for a, p in zip(args, specs)]
    return pl.pallas_call(
        kernel,
        out_shape=shapes,
        in_specs=specs,
        out_specs=[out_spec] * len(outs),
        scratch_shapes=[pltpu.VMEM(s, f32) if isinstance(s, tuple) else s for s in scratch],
        compiler_params=pltpu.CompilerParams(vmem_limit_bytes=mib * 1024 * 1024),
        name=name,
        cost_estimate=cost,
    )(*args)


def exchange(first, second, axis, step):
    count = lax.axis_size(axis)
    rounds = []
    for start in (0, step):
        up = [(i, i + step) for i in range(count - step) if i // step % 2 == start // step]
        rounds.append(up + [(b, a) for a, b in up])
    return lax.ppermute(first, axis, rounds[0]), lax.ppermute(second, axis, rounds[1])


def swap_pair(x):
    return lax.ppermute(x, "xl", [(i, i ^ 1) for i in range(lax.axis_size("xl"))])


def exchange_time(x):
    nx, nt = lax.axis_size("xl"), lax.axis_size("ta")
    pairs = []
    for x_at in range(nx):
        for t in range(nt):
            other = t + (-1 if x_at % 2 == 0 else 1)
            if 0 <= other < nt:
                pairs.append((x_at * nt + t, (x_at ^ 1) * nt + other))
    return lax.ppermute(x, ("xl", "ta"), pairs)


def codes(n):
    return ((n * 16 + 16, 128), i16)


def taper(order):
    return np.sin(np.pi * (np.arange(order) + 0.5) / order) ** 2


TILE = ((32, 32, 128), f32)


def shards(traces, live, counts, levels):
    tw, sw = tables()
    tj = jnp.asarray(np.broadcast_to(taper(64)[:, None], (64, 128)).astype(np.float32))
    tt = jnp.asarray(np.broadcast_to(taper(128)[None, :], (8, 128)).astype(np.float32))
    tw, sw = jnp.asarray(tw), jnp.asarray(sw)
    traces_other, live_other = swap_pair(traces), swap_pair(live)
    own, tw, tt = call(
        load_kernel,
        "load",
        4,
        [TILE, ((2, 256, 256), bf16), ((8, 128), f32)],
        [(32, 32, 128), pltpu.VMEM((32, 32), i32), SEM((4,))],
        [H] * 4,
        traces,
        live,
        tw,
        tt,
        cost=pl.CostEstimate(flops=1000000, bytes_accessed=6000000, transcendentals=0),
    )
    flagged, msg = call(
        pack_kernel,
        "pack",
        6,
        [((64, 32, 128), f32), codes(32)],
        [(512, 128)],
        [V] * 3,
        own,
        traces_other,
        live_other,
    )
    msg = exchange_time(msg)
    tile, lo, hi = call(
        widen_kernel,
        "widen",
        6,
        [((2048, 128), f32), codes(64), codes(64)],
        [],
        [V] * 3,
        flagged,
        msg,
        tw,
    )
    f0, f3 = exchange(lo, hi, "il", 1)
    lo, hi = call(edge_kernel, "edge", 6, [codes(64)] * 2, [(2048, 128)], [V] * 3, tile, f0, f3)
    fa, fb = exchange(lo, hi, "xl", 2)
    cost = pl.CostEstimate(flops=8000000000, bytes_accessed=30000000, transcendentals=0)
    shared = (counts.transpose(0, 2, 1), levels, tile, f0, f3)
    scratch = [(64, 64, 128)] * 3
    specs = [S, S] + [V] * 6
    outs = [codes(64), ((64, 64, 128), f32)]
    kernels = [functools.partial(window_kernel, n) for n in (False, True)]
    lo, w1 = call(kernels[0], "first", 16, outs, scratch, specs, *shared, fa, tj, sw, cost=cost)
    tj_after, lo = lax.optimization_barrier((tj, lo))
    hi, w2 = call(kernels[1], "second", 16, outs, scratch, specs, *shared, fb, tj_after, sw, cost=cost)
    lo, hi = lax.optimization_barrier((lo, hi))
    fa, fb = exchange(lo, hi, "xl", 2)
    lo, hi = call(fold_kernel, "fold", 8, [codes(64)] * 2, [(2048, 128)], [V] * 4, w1, w2, fa, fb)
    cost = pl.CostEstimate(flops=1000000, bytes_accessed=4000000, transcendentals=0)
    inner = call(inner_kernel, "inner", 4, [((2048, 128), f32)], [], [V] * 4, w1, w2, fa, fb, cost=cost)[0]
    fa, fb = exchange(lo, hi, "il", 1)
    own, other, msg = call(
        narrow_kernel,
        "narrow",
        8,
        [TILE, TILE, codes(32)],
        [(512, 128), (2048, 128)],
        [V] * 5,
        inner,
        fa,
        fb,
        tt,
        tw,
    )
    msg = exchange_time(msg)
    other, msg_other = swap_pair(other), swap_pair(msg)
    return call(
        last_kernel, "last", 4, [TILE], [(32, 32, 128), SEM((4,))], [V] * 4, own, other, msg_other, msg, out_spec=H
    )[0]


def solution(mesh):
    placed = (P("il", "xl", "ta"), P("il", "xl"), P("il", None, "ta"), P())
    return jax.shard_map(
        shards, mesh=mesh, in_specs=placed, out_specs=P("il", "xl", "ta"), check_vma=False
    )
```
